128 devices in a mesh: dp: 16 (over x, z_hi, core), tm: 8 (over z_lo, y).
Axes of the slice: x: 4, y: 4, z: 4 (z_hi: 2, z_lo: 2; z = z_hi * 2 + z_lo), core: 2. Of those that a mesh axis runs over, the one named last changes fastest.
Arguments:
- loaded: bfloat16 [16, 64, 16, 16, 256], P('dp', 'tm')
- lengths: int32 [16, 8], P('dp'), may hold values from 1 to 8, as said below
- resolution: int32 [16, 2], P('dp'), may hold values from 8 to 16, as said below
- weight: bfloat16 [27, 256, 256], replicated, may hold values from -0.078125 to 0.078125
- norm_gain: float32 [256], replicated, may hold values from 0.1 to 1.9
- norm_bias: float32 [256], replicated, may hold values from -3 to 3
- cotangent: bfloat16 [16, 64, 16, 16, 256], P('dp', 'tm'), may hold values from -6 to 6
Outputs:
- encoded: bfloat16 [16, 64, 16, 16, 256], P('dp', 'tm')
- input_grad: bfloat16 [16, 64, 16, 16, 256], P('dp', 'tm')
- weight_grad: float32 [27, 256, 256], replicated
- gain_grad: float32 [256], replicated
- bias_grad: float32 [256], replicated
The draws below stay inside these ranges and needn't reach their ends.
Inputs may be any that keep to these rules, and one draw needn't show every extreme that they name: `lengths`: row c lists how many consecutive frames of clip c each index of tm loaded, in frame order; the row sums to the clip's frame count, which is 64 - k for some 0 <= k <= 8, so that every loaded frame belongs to the loader's own temporal slab or to the one before it; in every draw one clip has all 64 frames, 8 on every index. `resolution`: valid rows (column 0) and columns (column 1) of clip c; frames are padded at the bottom and right; at least 8 rows and 8 columns, and in every draw one clip has the full 16 by 16.
All inputs are finite; a program needn't handle non-finite values.
Results may differ from the reference program's by a relative error of at most 0.0046.
The reference program's roundings to bfloat16 on the way count: a program that leaves them out, or rounds other values in their place, can miss the bound.
Values may be sent and summed in bfloat16 or wider, within the bound.
A program may use at most 128 MiB of HBM per device.

```python
import math
from functools import partial
import jax
import jax.numpy as jnp
from jax import lax

C = 256
GROUPS = 32
F_DEV = 8
HH = 16
WW = 16
CLIPS = 16
FRAMES = 64


def draw_lengths(key, part):
    loaders = FRAMES // F_DEV
    first_key, second_key = jax.random.split(jax.random.fold_in(key, 11), 2)
    full_clip = jax.random.randint(first_key, (), 0, CLIPS)
    deficit = jax.random.randint(second_key, (CLIPS,), F_DEV // 2, F_DEV + 1)
    deficit = jnp.where(jnp.arange(CLIPS) == full_clip, 0, deficit)
    before = jnp.arange(loaders, dtype=jnp.int32)[None, :] * (F_DEV - 1)
    removed = jnp.clip(deficit[:, None] - before, 0, F_DEV - 1)
    return (F_DEV - removed).astype(jnp.int32)


def draw_resolution(key, part):
    first_key, second_key, third_key = jax.random.split(jax.random.fold_in(key, 23), 3)
    full_clip = jax.random.randint(first_key, (), 0, CLIPS)
    row_count = jax.random.randint(second_key, (CLIPS,), HH // 2, HH + 1)
    col_count = jax.random.randint(third_key, (CLIPS,), WW // 2, WW + 1)
    is_full = jnp.arange(CLIPS) == full_clip
    row_count = jnp.where(is_full, HH, row_count)
    col_count = jnp.where(is_full, WW, col_count)
    return jnp.stack([row_count, col_count], axis=1).astype(jnp.int32)


def draw_loaded(key, part):
    draw_keys = jax.random.split(jax.random.fold_in(key, 31), 3)
    full_shape = (CLIPS, FRAMES, HH, WW, C)
    noise_field = jax.random.normal(draw_keys[0], full_shape)
    rising = 3.0 ** (jnp.arange(FRAMES, dtype=jnp.float32) / FRAMES)
    frame_scale = rising[None, :] * jnp.exp(jax.random.uniform(draw_keys[1], (CLIPS, FRAMES), minval=-0.9, maxval=0.9))
    channel_scale = jnp.exp(jax.random.uniform(draw_keys[2], (C,), minval=-0.7, maxval=0.7))
    values = noise_field * frame_scale[:, :, None, None, None] * channel_scale
    return values.astype(jnp.bfloat16)


def block_scale(own_key, dims, shards, least, largest):
    factor_of, own = 1.0, jax.random.fold_in(own_key, 6)
    for dim, blocks in shards:
        draws = jnp.exp(jax.random.uniform(jax.random.fold_in(own, dim), (blocks,), jnp.float32, least / len(shards), largest / len(shards)))
        factor_of = factor_of * jnp.repeat(draws, dims[dim] // blocks).reshape([-1 if axis == dim else 1 for axis in range(len(dims))])
    return factor_of


def scatter_about(own_key, shape, spread, most, cuts=(), kind=jnp.bfloat16):
    values = spread * jax.random.normal(own_key, shape, jnp.float32)
    if cuts:
        values = values * block_scale(own_key, shape, cuts, -0.22, 0.18)
    return jnp.clip(values, -most, most).astype(kind)


def setup_inputs(seed: int = 0) -> dict:
    splits = jax.random.split(jax.random.key(seed), 8)
    loaded = draw_loaded(jax.random.fold_in(splits[7], 71), 0)
    lengths = draw_lengths(jax.random.fold_in(splits[7], 71), 0)
    resolution = draw_resolution(jax.random.fold_in(splits[7], 71), 0)
    weight = scatter_about(splits[3], (27, C, C), (27 * C) ** -0.5, 0.078125)
    norm_gain = jnp.clip(1.0 + 0.18 * jax.random.normal(splits[4], (C,), jnp.float32), 0.1, 1.9)
    norm_bias = scatter_about(splits[5], (C,), 0.5, 3.0, (), jnp.float32)
    cotangent = scatter_about(splits[6], (CLIPS, FRAMES, HH, WW, C), 1.0, 6.0, ((0, 16), (1, 8)))
    return dict(loaded=loaded, lengths=lengths, resolution=resolution, weight=weight, norm_gain=norm_gain, norm_bias=norm_bias, cotangent=cotangent)


EPSILON = 1e-05

def group_total(values):
    shaped = values.reshape(values.shape[:-1] + (GROUPS, values.shape[-1] // GROUPS))
    return lax.optimization_barrier(jnp.sum(shaped, axis=(0, 1, 2, 4)))

def spread_groups(per_group, channels):
    return jnp.repeat(per_group, channels // per_group.shape[0])

def tap_sweeps(past_pad, future_pad, weight, frames, frame_rows, frame_cols):
    channels = weight.shape[2]
    positions = frames * frame_rows * frame_cols
    forward = jnp.zeros((positions, channels), jnp.float32)
    backward = jnp.zeros((positions, channels), jnp.float32)
    grad_flat = future_pad[:frames, 1:frame_rows + 1, 1:frame_cols + 1].reshape(positions, channels)
    kernel_parts = []
    for time_tap in range(3):
        for row_tap in range(3):
            for col_tap in range(3):
                tap_index = time_tap * 9 + row_tap * 3 + col_tap
                past_slice = past_pad[time_tap:time_tap + frames, row_tap:row_tap + frame_rows, col_tap:col_tap + frame_cols].reshape(positions, channels)
                forward = forward + jnp.dot(past_slice, weight[tap_index], preferred_element_type=jnp.float32)
                kernel_parts.append(lax.dot_general(past_slice, grad_flat, (((0,), (0,)), ((), ())), preferred_element_type=jnp.float32))
                future_slice = future_pad[2 - time_tap:2 - time_tap + frames, 2 - row_tap:2 - row_tap + frame_rows, 2 - col_tap:2 - col_tap + frame_cols].reshape(positions, channels)
                backward = backward + lax.dot_general(future_slice, weight[tap_index], (((1,), (1,)), ((), ())), preferred_element_type=jnp.float32)
    return (forward, backward, jnp.stack(kernel_parts))

def clip_pass(weight, norm_gain, norm_bias, running, inputs):
    loaded_clip, length_row, resolution_row, cotangent_clip = inputs
    length_row = length_row.astype(jnp.int32)
    starts = (jnp.cumsum(length_row) - length_row).astype(jnp.int32)
    frame_total = jnp.sum(length_row).astype(jnp.int32)
    frame_ids = jnp.arange(FRAMES, dtype=jnp.int32)
    loader = (lax.optimization_barrier(jnp.sum((starts[None, :] <= frame_ids[:, None]).astype(jnp.int32), axis=1)) - 1).astype(jnp.int32)
    source = jnp.clip(loader * F_DEV + frame_ids - starts[loader], 0, FRAMES - 1).astype(jnp.int32)
    live_time = frame_ids < frame_total
    live_rows = jnp.arange(HH, dtype=jnp.int32) < resolution_row[0]
    live_cols = jnp.arange(WW, dtype=jnp.int32) < resolution_row[1]
    live_cells = (live_time[:, None, None] & live_rows[None, :, None] & live_cols[None, None, :]).astype(jnp.float32)[..., None]
    inputs_f = jnp.take(loaded_clip, source, axis=0).astype(jnp.float32) * live_cells
    cell_count = (frame_total * resolution_row[0] * resolution_row[1] * (C // GROUPS)).astype(jnp.float32)
    group_means = group_total(inputs_f) / cell_count
    centred = (inputs_f - spread_groups(group_means, C)) * live_cells
    variance = group_total(centred * centred) / cell_count
    inverse_root = spread_groups(lax.rsqrt(variance + EPSILON), C)
    normed = centred * inverse_root
    pre_activation = normed * norm_gain + norm_bias
    gate_value = jax.nn.sigmoid(pre_activation)
    activation = (pre_activation * gate_value * live_cells).astype(jnp.bfloat16)
    past_pad = jnp.pad(activation, ((2, 0), (1, 1), (1, 1), (0, 0)))
    masked_grad = cotangent_clip * live_cells.astype(jnp.bfloat16)
    future_pad = jnp.pad(masked_grad, ((0, 2), (1, 1), (1, 1), (0, 0)))
    forward, backward, kernel_part = tap_sweeps(past_pad, future_pad, weight, FRAMES, HH, WW)
    encoded = (forward.reshape(FRAMES, HH, WW, C) * live_cells).astype(jnp.bfloat16)
    activation_grad = backward.reshape(FRAMES, HH, WW, C) * live_cells
    pre_grad = activation_grad * gate_value * (1.0 + pre_activation * (1.0 - gate_value))
    gain_part = lax.optimization_barrier(jnp.sum(pre_grad * normed, axis=(0, 1, 2)))
    bias_part = lax.optimization_barrier(jnp.sum(pre_grad, axis=(0, 1, 2)))
    normed_grad = pre_grad * norm_gain
    grad_mean = spread_groups(group_total(normed_grad) / cell_count, C)
    grad_proj = spread_groups(group_total(normed_grad * normed) / cell_count, C)
    input_grad = (inverse_root * (normed_grad - grad_mean - normed * grad_proj) * live_cells).astype(jnp.bfloat16)
    running = (running[0] + kernel_part, running[1] + gain_part, running[2] + bias_part)
    return (running, (encoded, input_grad))

def reference(loaded, lengths, resolution, weight, norm_gain, norm_bias, cotangent):
    start_sums = (jnp.zeros((27, C, C), jnp.float32), jnp.zeros((C,), jnp.float32), jnp.zeros((C,), jnp.float32))
    per_clip = partial(clip_pass, weight, norm_gain, norm_bias)
    totals, outputs = lax.scan(per_clip, start_sums, (loaded, lengths, resolution, cotangent))
    grad_scale = 1.0 / math.sqrt(CLIPS * FRAMES * HH * WW)
    return (outputs[0], outputs[1], totals[0] * grad_scale, totals[1] * grad_scale, totals[2] * grad_scale)
```

```python
import functools
import math

import jax
import jax.numpy as jnp
from jax import lax
from jax.experimental import pallas as pl
from jax.experimental.pallas import tpu as pltpu
from jax.sharding import PartitionSpec as P

GROUPS = 32
EPSILON = 1e-05
MESH = pl.DeviceIdType.MESH
F32 = jnp.float32
BF16 = jnp.bfloat16

VMEM = pl.BlockSpec(memory_space=pltpu.VMEM)
SMEM = pl.BlockSpec(memory_space=pltpu.SMEM)


def params(limit, **others):
    return pltpu.CompilerParams(vmem_limit_bytes=limit << 20, **others)


def shifted(block, axis, distance):
    devices = range(lax.axis_size(axis))
    route = [(i - distance, i) for i in devices if i - distance in devices]
    return lax.ppermute(block, axis, route)


def start_of(len_ref, slabs, index):
    total = jnp.int32(0)
    for i in range(slabs):
        total = total + jnp.where(i < index, len_ref[0, i], 0)
    return total


def length_of(len_ref, slabs, index):
    total = jnp.int32(0)
    for i in range(slabs):
        total = total + jnp.where(i == index, len_ref[0, i], 0)
    return total


def group_sum(rows, width):
    lanes = rows.shape[1]
    lane = lax.broadcasted_iota(jnp.int32, rows.shape, 1)
    step = 1
    while step < width:
        up = pltpu.roll(rows, lanes - step, 1)
        down = pltpu.roll(rows, step, 1)
        rows = rows + jnp.where((lane & step) == 0, up, down)
        step *= 2
    return rows


def cells(res_ref, cols, shape):
    place = lax.broadcasted_iota(jnp.int32, shape, 0)
    return ((place // cols) < res_ref[0, 0]) & ((place % cols) < res_ref[0, 1])


def stats_kernel(slabs, cols, width, len_ref, res_ref, loaded_ref, stats_ref, tail_ref, mask_ref):
    frames, places, channels = loaded_ref.shape
    own = lax.axis_index("tm")
    length = length_of(len_ref, slabs, own)
    mask_ref[...] = cells(res_ref, cols, (places, channels)).astype(F32)
    count = (length * res_ref[0, 0] * res_ref[0, 1] * width).astype(F32)
    zero = jnp.zeros((8, channels), F32)

    def add_up(f, total):
        x = loaded_ref[f].astype(F32) * mask_ref[...]
        return total + jnp.sum(x.reshape(places // 8, 8, channels), axis=0)

    total = lax.fori_loop(0, length, add_up, zero)
    total = group_sum(jnp.broadcast_to(jnp.sum(total, axis=0, keepdims=True), (8, channels)), width)
    mean = total / count
    mean_row = mean[0:1]

    def spread(f, total):
        x = (loaded_ref[f].astype(F32) - mean_row) * mask_ref[...]
        return total + jnp.sum((x * x).reshape(places // 8, 8, channels), axis=0)

    squares = lax.fori_loop(0, length, spread, zero)
    squares = group_sum(
        jnp.broadcast_to(jnp.sum(squares, axis=0, keepdims=True), (8, channels)), width
    )
    row = lax.broadcasted_iota(jnp.int32, (8, channels), 0)
    stats_ref[...] = jnp.where(row == 0, mean, squares)
    first = own * frames + frames - 2 - start_of(len_ref, slabs, own)
    for k in range(2):
        offset = first + k
        usable = (offset >= 0) & (offset < length)
        picked = loaded_ref[jnp.clip(offset, 0, frames - 1)]
        tail_ref[k] = jnp.where(usable, picked, jnp.zeros_like(picked))


def share_kernel(size, mine_ref, all_ref, send_sem, recv_sem):
    own = lax.axis_index("tm")
    barrier = pltpu.get_barrier_semaphore()
    for off in range(1, size):
        peer = lax.rem(own + off, size)
        pl.semaphore_signal(barrier, inc=1, device_id={"tm": peer}, device_id_type=MESH)
    all_ref[own] = mine_ref[...]
    pl.semaphore_wait(barrier, size - 1)
    copies = []
    for off in range(1, size):
        peer = lax.rem(own + off, size)
        copy = pltpu.make_async_remote_copy(
            src_ref=mine_ref,
            dst_ref=all_ref.at[own],
            send_sem=send_sem.at[off],
            recv_sem=recv_sem.at[off],
            device_id={"tm": peer},
            device_id_type=MESH,
        )
        copy.start()
        copies.append(copy)
    for copy in copies:
        copy.wait()


def share(mine, size, collective_id):
    return pl.pallas_call(
        functools.partial(share_kernel, size),
        out_shape=jax.ShapeDtypeStruct((size,) + mine.shape, mine.dtype),
        in_specs=[VMEM],
        out_specs=VMEM,
        scratch_shapes=[pltpu.SemaphoreType.DMA((size,)), pltpu.SemaphoreType.DMA((size,))],
        compiler_params=pltpu.CompilerParams(collective_id=collective_id, has_side_effects=True),
    )(mine)


def lay_out(cat_ref, frame, value, rows, cols, first_col, last_col):
    places, channels = value.shape
    left = pltpu.roll(value, 1, 0) * first_col
    right = pltpu.roll(value, places - 1, 0) * last_col
    for k, part in enumerate((left, value, right)):
        cat_ref[frame, 1 : rows + 1, :, k * channels : (k + 1) * channels] = (
            part.astype(BF16).reshape(rows, cols, channels)
        )


def col_masks(cols, shape):
    place = lax.broadcasted_iota(jnp.int32, shape, 0) % cols
    return (place != 0).astype(F32), (place != cols - 1).astype(F32)


def back_kernel(
    slabs, rows, cols, len_ref, res_ref, cot_ref, next_ref, weight_ref, agrad_ref,
    cat_ref, turned_ref, mask_ref, first_ref, last_ref,
):
    frames, places, channels = cot_ref.shape
    own = lax.axis_index("tm")
    frame_total = start_of(len_ref, slabs, slabs)
    mask_ref[...] = cells(res_ref, cols, (places, channels)).astype(F32)
    first, last = col_masks(cols, (places, channels))
    first_ref[...] = first
    last_ref[...] = last

    def turn(block, _):
        for k in range(3):
            turned_ref[block, k * channels : (k + 1) * channels, :] = weight_ref[
                3 * block + 2 - k
            ].T
        return 0

    lax.fori_loop(0, 9, turn, 0)
    blank = jnp.zeros((cols, 3 * channels), BF16)

    def place(frame, value):
        alive = (own * frames + frame < frame_total).astype(F32)
        value = value.astype(F32) * (mask_ref[...] * alive)
        cat_ref[frame, 0] = blank
        cat_ref[frame, rows + 1] = blank
        lay_out(cat_ref, frame, value, rows, cols, first_ref[...], last_ref[...])

    def own_frame(f, _):
        place(f, cot_ref[f])
        return 0

    lax.fori_loop(0, frames, own_frame, 0)
    for k in range(2):
        place(frames + k, next_ref[k])

    def sweep(f, _):
        total = jnp.zeros((places, channels), F32)
        for d in range(3):
            for r in range(3):
                rows_in = cat_ref[f + 2 - d, 2 - r : 2 - r + rows].reshape(places, 3 * channels)
                total = total + jnp.dot(
                    rows_in, turned_ref[3 * d + r], preferred_element_type=F32
                )
        alive = (own * frames + f < frame_total).astype(F32)
        agrad_ref[f] = total * (mask_ref[...] * alive)
        return 0

    lax.fori_loop(0, frames, sweep, 0)


def main_kernel(
    slabs, rows, cols, width,
    len_ref, res_ref, loaded_ref, arrived_ref, tail_ref, cot_ref, agrad_ref, stats_ref,
    gain_ref, bias_ref, weight_ref,
    encoded_ref, kernel_ref, sums_ref, root_ref, ngrad_ref, normed_ref,
    cat_ref, grad_ref, mask_ref, first_ref, last_ref,
):
    frames, places, channels = cot_ref.shape
    own = lax.axis_index("tm")
    frame_total = start_of(len_ref, slabs, slabs)
    own_start, own_length = start_of(len_ref, slabs, own), length_of(len_ref, slabs, own)
    next_start, next_length = own_start + own_length, length_of(len_ref, slabs, own + 1)
    mask_ref[...] = cells(res_ref, cols, (places, channels)).astype(F32)
    first, last = col_masks(cols, (places, channels))
    first_ref[...] = first
    last_ref[...] = last

    area = res_ref[0, 0] * res_ref[0, 1] * width
    count = (frame_total * area).astype(F32)
    counts = [(len_ref[0, i] * area).astype(F32) for i in range(slabs)]
    mean = jnp.zeros((1, channels), F32)
    for i in range(slabs):
        mean = mean + counts[i] * stats_ref[i, 0:1]
    mean = mean / count
    squares = jnp.zeros((1, channels), F32)
    for i in range(slabs):
        apart = stats_ref[i, 0:1] - mean
        squares = squares + stats_ref[i, 1:2] + counts[i] * (apart * apart)
    root = lax.rsqrt(squares / count + EPSILON)
    root_ref[...] = jnp.broadcast_to(root, (8, channels))
    gain, bias = gain_ref[...], bias_ref[...]
    blank = jnp.zeros((cols, 3 * channels), BF16)

    def activate(slot, frame_id, value):
        alive = ((frame_id >= 0) & (frame_id < frame_total)).astype(F32)
        live = mask_ref[...] * alive
        normed = (value.astype(F32) * live - mean) * live * root
        pre = normed * gain + bias
        gate = 1.0 / (1.0 + jnp.exp(-pre))
        act = (pre * gate * live).astype(BF16).astype(F32)
        cat_ref[slot, 0] = blank
        cat_ref[slot, rows + 1] = blank
        lay_out(cat_ref, slot, act, rows, cols, first_ref[...], last_ref[...])
        return live, normed, pre, gate

    for k in range(2):
        frame_id = own * frames + k - 2
        offset = frame_id - own_start
        usable = (offset >= 0) & (offset < own_length)
        picked = jnp.where(usable, loaded_ref[jnp.clip(offset, 0, frames - 1)], tail_ref[k])
        activate(k, frame_id, picked)

    zero = jnp.zeros((8, channels), F32)

    def own_frame(f, sums):
        frame_id = own * frames + f
        offset = frame_id - own_start
        later = frame_id - next_start
        picked = jnp.where(
            offset < own_length,
            loaded_ref[jnp.clip(offset, 0, frames - 1)],
            arrived_ref[jnp.clip(later, 0, frames - 1)],
        )
        live, normed, pre, gate = activate(f + 2, frame_id, picked)
        grad_ref[pl.ds(pl.multiple_of(f * places, places), places)] = (
            cot_ref[f].astype(F32) * live
        ).astype(BF16)
        pre_grad = agrad_ref[f] * gate * (1.0 + pre * (1.0 - gate))
        normed_ref[f] = normed
        ngrad_ref[f] = pre_grad * gain
        return (
            sums[0] + jnp.sum((pre_grad * normed).reshape(places // 8, 8, channels), axis=0),
            sums[1] + jnp.sum(pre_grad.reshape(places // 8, 8, channels), axis=0),
        )

    gain_sum, bias_sum = lax.fori_loop(0, frames, own_frame, (zero, zero))
    row = lax.broadcasted_iota(jnp.int32, (8, channels), 0)
    sums_ref[...] = jnp.where(
        row == 0,
        jnp.sum(gain_sum, axis=0, keepdims=True),
        jnp.where(row == 1, jnp.sum(bias_sum, axis=0, keepdims=True), 0.0),
    )

    for d in range(3):
        for r in range(3):
            rows_in = cat_ref[d : d + frames, r : r + rows].reshape(frames * places, 3 * channels)
            kernel_ref[3 * d + r] = lax.dot_general(
                rows_in, grad_ref[...], (((0,), (0,)), ((), ())), preferred_element_type=F32
            ).astype(kernel_ref.dtype)

    def sweep(f, _):
        total = jnp.zeros((places, channels), F32)
        for d in range(3):
            for r in range(3):
                rows_in = cat_ref[f + d, r : r + rows].reshape(places, 3 * channels)
                total = total + jnp.dot(
                    rows_in, weight_ref[3 * d + r], preferred_element_type=F32
                )
        alive = (own * frames + f < frame_total).astype(F32)
        encoded_ref[f] = (total * (mask_ref[...] * alive)).astype(BF16)
        return 0

    lax.fori_loop(0, frames, sweep, 0)


def last_kernel(
    slabs, cols, width, frames,
    len_ref, res_ref, sums_ref, gain_ref, root_ref, ngrad_ref, normed_ref, out_ref,
):
    _, places, channels = ngrad_ref.shape
    own = lax.axis_index("tm")
    frame_total = start_of(len_ref, slabs, slabs)
    frame_id = own * frames + pl.program_id(0)
    count = (frame_total * res_ref[0, 0] * res_ref[0, 1] * width).astype(F32)
    total = sums_ref[0]
    for i in range(1, slabs):
        total = total + sums_ref[i]
    total = group_sum(total * gain_ref[...], width) / count
    live = (cells(res_ref, cols, (places, channels)) & (frame_id < frame_total)).astype(F32)
    inner = ngrad_ref[0] - total[1:2] - normed_ref[0] * total[0:1]
    out_ref[0] = (inner * root_ref[0:1] * live).astype(BF16)


def body(loaded, lengths, resolution, weight, norm_gain, norm_bias, cotangent):
    frames, rows, cols, channels = loaded.shape[1:]
    places, width = rows * cols, channels // GROUPS
    slabs = lax.axis_size("tm")
    shape = jax.ShapeDtypeStruct
    loaded = loaded.reshape(frames, places, channels)
    cotangent = cotangent.reshape(frames, places, channels)
    gain, bias = norm_gain.reshape(1, channels), norm_bias.reshape(1, channels)

    following = shifted(cotangent[:2], "tm", -1)
    arrived = shifted(loaded, "tm", -1)
    stats, tail = pl.pallas_call(
        functools.partial(stats_kernel, slabs, cols, width),
        out_shape=(shape((8, channels), F32), shape((2, places, channels), BF16)),
        in_specs=[SMEM, SMEM, VMEM],
        out_specs=(VMEM, VMEM),
        scratch_shapes=[pltpu.VMEM((places, channels), F32)],
        compiler_params=params(16),
        cost_estimate=pl.CostEstimate(flops=4 << 20, bytes_accessed=2 << 20, transcendentals=0),
    )(lengths, resolution, loaded)
    tail = shifted(tail, "tm", 1)
    all_stats = share(stats, slabs, 1)

    cat = pltpu.VMEM((frames + 2, rows + 2, cols, 3 * channels), BF16)
    plane = pltpu.VMEM((places, channels), F32)
    agrad = pl.pallas_call(
        functools.partial(back_kernel, slabs, rows, cols),
        out_shape=shape((frames, places, channels), F32),
        in_specs=[SMEM, SMEM, VMEM, VMEM, VMEM],
        out_specs=VMEM,
        scratch_shapes=[cat, pltpu.VMEM((9, 3 * channels, channels), BF16), plane, plane, plane],
        compiler_params=params(40),
        cost_estimate=pl.CostEstimate(
            flops=2 * 27 * frames * places * channels * channels,
            bytes_accessed=8 << 20,
            transcendentals=0,
        ),
    )(lengths, resolution, cotangent, following, weight)

    encoded, kernel_part, sums, root, ngrad, normed = pl.pallas_call(
        functools.partial(main_kernel, slabs, rows, cols, width),
        out_shape=(
            shape((frames, places, channels), BF16),
            shape((9, 3 * channels, channels), F32),
            shape((8, channels), F32),
            shape((8, channels), F32),
            shape((frames, places, channels), F32),
            shape((frames, places, channels), F32),
        ),
        in_specs=[SMEM, SMEM] + [VMEM] * 9,
        out_specs=(VMEM,) * 6,
        scratch_shapes=[cat, pltpu.VMEM((frames * places, channels), BF16), plane, plane, plane],
        compiler_params=params(56),
        cost_estimate=pl.CostEstimate(
            flops=4 * 27 * frames * places * channels * channels,
            bytes_accessed=20 << 20,
            transcendentals=frames * places * channels,
        ),
    )(
        lengths, resolution, loaded, arrived, tail, cotangent, agrad, all_stats,
        gain, bias, weight.reshape(9, 3 * channels, channels),
    )

    all_sums = share(sums, slabs, 2)
    block = pl.BlockSpec((1, places, channels), lambda f: (f, 0, 0))
    input_grad = pl.pallas_call(
        functools.partial(last_kernel, slabs, cols, width, frames),
        out_shape=shape((frames, places, channels), BF16),
        grid=(frames,),
        in_specs=[
            SMEM,
            SMEM,
            pl.BlockSpec((slabs, 8, channels), lambda f: (0, 0, 0)),
            pl.BlockSpec((1, channels), lambda f: (0, 0)),
            pl.BlockSpec((8, channels), lambda f: (0, 0)),
            block,
            block,
        ],
        out_specs=block,
        compiler_params=params(16),
    )(lengths, resolution, all_sums, gain, root, ngrad, normed)

    kernel_sum, pair_sum = lax.psum((kernel_part, sums[:2]), ("dp", "tm"))
    scale = 1.0 / math.sqrt(lax.axis_size("dp") * slabs * frames * places)
    whole = (1, frames, rows, cols, channels)
    return (
        encoded.reshape(whole),
        input_grad.reshape(whole),
        kernel_sum.reshape(27, channels, channels) * scale,
        pair_sum[0] * scale,
        pair_sum[1] * scale,
    )


def solution(mesh):
    slab = P("dp", "tm", None, None, None)
    return jax.shard_map(
        body,
        mesh=mesh,
        in_specs=(slab, P("dp", None), P("dp", None), P(), P(), P(), slab),
        out_specs=(slab, slab, P(), P(), P()),
        check_vma=False,
    )
```

```python
import functools
import math

import jax
import jax.numpy as jnp
from jax import lax
from jax.experimental import pallas as pl
from jax.experimental.pallas import tpu as pltpu
from jax.sharding import PartitionSpec as P

GROUPS = 32
EPSILON = 1e-05
MESH = pl.DeviceIdType.MESH
F32 = jnp.float32
BF16 = jnp.bfloat16

VMEM = pl.BlockSpec(memory_space=pltpu.VMEM)
SMEM = pl.BlockSpec(memory_space=pltpu.SMEM)


def params(limit, **others):
    return pltpu.CompilerParams(vmem_limit_bytes=limit << 20, **others)


def shifted(block, axis, distance):
    devices = range(lax.axis_size(axis))
    route = [(i - distance, i) for i in devices if i - distance in devices]
    return lax.ppermute(block, axis, route)


def start_of(len_ref, slabs, index):
    total = jnp.int32(0)
    for i in range(slabs):
        total = total + jnp.where(i < index, len_ref[0, i], 0)
    return total


def length_of(len_ref, slabs, index):
    total = jnp.int32(0)
    for i in range(slabs):
        total = total + jnp.where(i == index, len_ref[0, i], 0)
    return total


def group_sum(rows, width):
    lanes = rows.shape[1]
    lane = lax.broadcasted_iota(jnp.int32, rows.shape, 1)
    step = 1
    while step < width:
        up = pltpu.roll(rows, lanes - step, 1)
        down = pltpu.roll(rows, step, 1)
        rows = rows + jnp.where((lane & step) == 0, up, down)
        step *= 2
    return rows


def cells(res_ref, cols, shape):
    place = lax.broadcasted_iota(jnp.int32, shape, 0)
    return ((place // cols) < res_ref[0, 0]) & ((place % cols) < res_ref[0, 1])


def stats_kernel(slabs, cols, width, len_ref, res_ref, loaded_ref, stats_ref, tail_ref, mask_ref):
    frames, places, channels = loaded_ref.shape
    own = lax.axis_index("tm")
    length = length_of(len_ref, slabs, own)
    mask_ref[...] = cells(res_ref, cols, (places, channels)).astype(F32)
    count = (length * res_ref[0, 0] * res_ref[0, 1] * width).astype(F32)
    zero = jnp.zeros((8, channels), F32)

    def add_up(f, total):
        x = loaded_ref[f].astype(F32) * mask_ref[...]
        return total + jnp.sum(x.reshape(places // 8, 8, channels), axis=0)

    total = lax.fori_loop(0, length, add_up, zero)
    total = group_sum(jnp.broadcast_to(jnp.sum(total, axis=0, keepdims=True), (8, channels)), width)
    mean = total / count
    mean_row = mean[0:1]

    def spread(f, total):
        x = (loaded_ref[f].astype(F32) - mean_row) * mask_ref[...]
        return total + jnp.sum((x * x).reshape(places // 8, 8, channels), axis=0)

    squares = lax.fori_loop(0, length, spread, zero)
    squares = group_sum(
        jnp.broadcast_to(jnp.sum(squares, axis=0, keepdims=True), (8, channels)), width
    )
    row = lax.broadcasted_iota(jnp.int32, (8, channels), 0)
    stats_ref[...] = jnp.where(row == 0, mean, squares)
    first = own * frames + frames - 2 - start_of(len_ref, slabs, own)
    for k in range(2):
        offset = first + k
        usable = (offset >= 0) & (offset < length)
        picked = loaded_ref[jnp.clip(offset, 0, frames - 1)]
        tail_ref[k] = jnp.where(usable, picked, jnp.zeros_like(picked))


def share_kernel(size, mine_ref, all_ref, send_sem, recv_sem):
    own = lax.axis_index("tm")
    barrier = pltpu.get_barrier_semaphore()
    for off in range(1, size):
        peer = lax.rem(own + off, size)
        pl.semaphore_signal(barrier, inc=1, device_id={"tm": peer}, device_id_type=MESH)
    all_ref[own] = mine_ref[...]
    pl.semaphore_wait(barrier, size - 1)
    copies = []
    for off in range(1, size):
        peer = lax.rem(own + off, size)
        copy = pltpu.make_async_remote_copy(
            src_ref=mine_ref,
            dst_ref=all_ref.at[own],
            send_sem=send_sem.at[off],
            recv_sem=recv_sem.at[off],
            device_id={"tm": peer},
            device_id_type=MESH,
        )
        copy.start()
        copies.append(copy)
    for copy in copies:
        copy.wait()


def share(mine, size, collective_id):
    return pl.pallas_call(
        functools.partial(share_kernel, size),
        out_shape=jax.ShapeDtypeStruct((size,) + mine.shape, mine.dtype),
        in_specs=[VMEM],
        out_specs=VMEM,
        scratch_shapes=[pltpu.SemaphoreType.DMA((size,)), pltpu.SemaphoreType.DMA((size,))],
        compiler_params=pltpu.CompilerParams(collective_id=collective_id, has_side_effects=True),
    )(mine)


def lay_out(cat_ref, frame, value, rows, cols, first_col, last_col):
    places, channels = value.shape
    left = pltpu.roll(value, 1, 0) * first_col
    right = pltpu.roll(value, places - 1, 0) * last_col
    for k, part in enumerate((left, value, right)):
        cat_ref[frame, 1 : rows + 1, :, k * channels : (k + 1) * channels] = (
            part.astype(BF16).reshape(rows, cols, channels)
        )


def col_masks(cols, shape):
    place = lax.broadcasted_iota(jnp.int32, shape, 0) % cols
    return (place != 0).astype(F32), (place != cols - 1).astype(F32)


def back_kernel(
    slabs, rows, cols, len_ref, res_ref, cot_ref, next_ref, weight_ref, agrad_ref,
    cat_ref, turned_ref, mask_ref, first_ref, last_ref,
):
    frames, places, channels = cot_ref.shape
    own = lax.axis_index("tm")
    frame_total = start_of(len_ref, slabs, slabs)
    mask_ref[...] = cells(res_ref, cols, (places, channels)).astype(F32)
    first, last = col_masks(cols, (places, channels))
    first_ref[...] = first
    last_ref[...] = last

    def turn(block, _):
        for k in range(3):
            turned_ref[block, k * channels : (k + 1) * channels, :] = weight_ref[
                3 * block + 2 - k
            ].T
        return 0

    lax.fori_loop(0, 9, turn, 0)
    blank = jnp.zeros((cols, 3 * channels), BF16)

    def place(frame, value):
        alive = (own * frames + frame < frame_total).astype(F32)
        value = value.astype(F32) * (mask_ref[...] * alive)
        cat_ref[frame, 0] = blank
        cat_ref[frame, rows + 1] = blank
        lay_out(cat_ref, frame, value, rows, cols, first_ref[...], last_ref[...])

    def own_frame(f, _):
        place(f, cot_ref[f])
        return 0

    lax.fori_loop(0, frames, own_frame, 0)
    for k in range(2):
        place(frames + k, next_ref[k])

    def sweep(f, _):
        total = jnp.zeros((places, channels), F32)
        for d in range(3):
            for r in range(3):
                rows_in = cat_ref[f + 2 - d, 2 - r : 2 - r + rows].reshape(places, 3 * channels)
                total = total + jnp.dot(
                    rows_in, turned_ref[3 * d + r], preferred_element_type=F32
                )
        alive = (own * frames + f < frame_total).astype(F32)
        agrad_ref[f] = total * (mask_ref[...] * alive)
        return 0

    lax.fori_loop(0, frames, sweep, 0)


def main_kernel(
    slabs, rows, cols, width,
    len_ref, res_ref, loaded_ref, arrived_ref, tail_ref, cot_ref, agrad_ref, stats_ref,
    gain_ref, bias_ref, weight_ref,
    encoded_ref, kernel_ref, sums_ref, root_ref, ngrad_ref, normed_ref,
    cat_ref, grad_ref, mask_ref, first_ref, last_ref,
):
    frames, places, channels = cot_ref.shape
    own = lax.axis_index("tm")
    frame_total = start_of(len_ref, slabs, slabs)
    own_start, own_length = start_of(len_ref, slabs, own), length_of(len_ref, slabs, own)
    next_start, next_length = own_start + own_length, length_of(len_ref, slabs, own + 1)
    mask_ref[...] = cells(res_ref, cols, (places, channels)).astype(F32)
    first, last = col_masks(cols, (places, channels))
    first_ref[...] = first
    last_ref[...] = last

    area = res_ref[0, 0] * res_ref[0, 1] * width
    count = (frame_total * area).astype(F32)
    counts = [(len_ref[0, i] * area).astype(F32) for i in range(slabs)]
    mean = jnp.zeros((1, channels), F32)
    for i in range(slabs):
        mean = mean + counts[i] * stats_ref[i, 0:1]
    mean = mean / count
    squares = jnp.zeros((1, channels), F32)
    for i in range(slabs):
        apart = stats_ref[i, 0:1] - mean
        squares = squares + stats_ref[i, 1:2] + counts[i] * (apart * apart)
    root = lax.rsqrt(squares / count + EPSILON)
    root_ref[...] = jnp.broadcast_to(root, (8, channels))
    gain, bias = gain_ref[...], bias_ref[...]
    blank = jnp.zeros((cols, 3 * channels), BF16)

    def activate(slot, frame_id, value):
        alive = ((frame_id >= 0) & (frame_id < frame_total)).astype(F32)
        live = mask_ref[...] * alive
        normed = (value.astype(F32) * live - mean) * live * root
        pre = normed * gain + bias
        gate = 1.0 / (1.0 + jnp.exp(-pre))
        act = (pre * gate * live).astype(BF16).astype(F32)
        cat_ref[slot, 0] = blank
        cat_ref[slot, rows + 1] = blank
        lay_out(cat_ref, slot, act, rows, cols, first_ref[...], last_ref[...])
        return live, normed, pre, gate

    for k in range(2):
        frame_id = own * frames + k - 2
        offset = frame_id - own_start
        usable = (offset >= 0) & (offset < own_length)
        picked = jnp.where(usable, loaded_ref[jnp.clip(offset, 0, frames - 1)], tail_ref[k])
        activate(k, frame_id, picked)

    zero = jnp.zeros((8, channels), F32)

    def own_frame(f, sums):
        frame_id = own * frames + f
        offset = frame_id - own_start
        later = frame_id - next_start
        picked = jnp.where(
            offset < own_length,
            loaded_ref[jnp.clip(offset, 0, frames - 1)],
            arrived_ref[jnp.clip(later, 0, frames - 1)],
        )
        live, normed, pre, gate = activate(f + 2, frame_id, picked)
        grad_ref[pl.ds(pl.multiple_of(f * places, places), places)] = (
            cot_ref[f].astype(F32) * live
        ).astype(BF16)
        pre_grad = agrad_ref[f] * gate * (1.0 + pre * (1.0 - gate))
        normed_ref[f] = normed
        ngrad_ref[f] = pre_grad * gain
        return (
            sums[0] + jnp.sum((pre_grad * normed).reshape(places // 8, 8, channels), axis=0),
            sums[1] + jnp.sum(pre_grad.reshape(places // 8, 8, channels), axis=0),
        )

    gain_sum, bias_sum = lax.fori_loop(0, frames, own_frame, (zero, zero))
    row = lax.broadcasted_iota(jnp.int32, (8, channels), 0)
    sums_ref[...] = jnp.where(
        row == 0,
        jnp.sum(gain_sum, axis=0, keepdims=True),
        jnp.where(row == 1, jnp.sum(bias_sum, axis=0, keepdims=True), 0.0),
    )

    for d in range(3):
        for r in range(3):
            rows_in = cat_ref[d : d + frames, r : r + rows].reshape(frames * places, 3 * channels)
            kernel_ref[3 * d + r] = lax.dot_general(
                rows_in, grad_ref[...], (((0,), (0,)), ((), ())), preferred_element_type=F32
            ).astype(kernel_ref.dtype)

    def sweep(f, _):
        total = jnp.zeros((places, channels), F32)
        for d in range(3):
            for r in range(3):
                rows_in = cat_ref[f + d, r : r + rows].reshape(places, 3 * channels)
                total = total + jnp.dot(
                    rows_in, weight_ref[3 * d + r], preferred_element_type=F32
                )
        alive = (own * frames + f < frame_total).astype(F32)
        encoded_ref[f] = (total * (mask_ref[...] * alive)).astype(BF16)
        return 0

    lax.fori_loop(0, frames, sweep, 0)


def last_kernel(
    slabs, cols, width, frames,
    len_ref, res_ref, sums_ref, gain_ref, root_ref, ngrad_ref, normed_ref, out_ref,
):
    _, places, channels = ngrad_ref.shape
    own = lax.axis_index("tm")
    frame_total = start_of(len_ref, slabs, slabs)
    frame_id = own * frames + pl.program_id(0)
    count = (frame_total * res_ref[0, 0] * res_ref[0, 1] * width).astype(F32)
    total = sums_ref[0]
    for i in range(1, slabs):
        total = total + sums_ref[i]
    total = group_sum(total * gain_ref[...], width) / count
    live = (cells(res_ref, cols, (places, channels)) & (frame_id < frame_total)).astype(F32)
    inner = ngrad_ref[0] - total[1:2] - normed_ref[0] * total[0:1]
    out_ref[0] = (inner * root_ref[0:1] * live).astype(BF16)


def reduce_kernel(
    blocks, mine_ref, sums_ref, total_ref, slabs_ref, pair_ref,
    core_in, send1, in1, send2, in2, in3, tm_total, core_sum, x_sums, x_total, z_sum,
    send_sem, recv_sem, pair_send, pair_recv,
):
    dp, tm = lax.axis_index("dp"), lax.axis_index("tm")
    core, x, y = dp % 2, dp // 4, tm % 4
    z = (dp // 2) % 2 * 2 + tm // 4
    here = (x, y, z)
    part, piece = blocks // 4, blocks // 16

    def device(place, its_core):
        return ((place[0] * 2 + place[2] // 2) * 2 + its_core, (place[2] % 2) * 4 + place[1])

    def along(axis, off):
        place = list(here)
        place[axis] = (here[axis] + off) % 4
        return place[axis], device(place, core)

    other = device(here, 1 - core)
    across = device((x, y, (z + 2) % 4), core)
    tm_peers = [(dp, (tm + off) % 8) for off in range(1, 8)]
    axis_peers = [along(axis, off)[1] for axis in (0, 1, 2) for off in (1, 2, 3)]
    barrier = pltpu.get_barrier_semaphore()
    greeted = [other] + axis_peers + tm_peers
    for peer in greeted:
        pl.semaphore_signal(barrier, inc=1, device_id=peer, device_id_type=MESH)
    pl.semaphore_wait(barrier, len(greeted))

    def send(src, dst, sems, peer):
        copy = pltpu.make_async_remote_copy(
            src_ref=src, dst_ref=dst, send_sem=sems[0], recv_sem=sems[1],
            device_id=peer, device_id_type=MESH,
        )
        copy.start()
        return copy

    def sems(stage, stream, peer):
        return send_sem.at[stage, stream, peer], recv_sem.at[stage, stream, peer]

    def pair_sems(i):
        return pair_send.at[i], pair_recv.at[i]

    lanes = mine_ref.shape[-1] // 2
    own_lanes = pl.ds(pl.multiple_of(core * lanes, lanes), lanes)
    far_lanes = pl.ds(pl.multiple_of((1 - core) * lanes, lanes), lanes)
    order = [(k % 3, (k + 1) % 3, (k + 2) % 3) for k in range(3)]

    started = []
    halves = []
    for k in range(3):
        halves.append(
            send(mine_ref.at[k, :, :, far_lanes], core_in.at[k], sems(0, k, 0), other)
        )
    slabs_ref[tm] = sums_ref[...]
    shares = [
        send(sums_ref, slabs_ref.at[tm], pair_sems(i), peer) for i, peer in enumerate(tm_peers)
    ]

    firsts = []
    for k in range(3):
        halves[k].wait()

        def add_half(b, _, k=k):
            at = pl.ds(b * 4, 4)
            both = mine_ref[k, at]
            own = jnp.where(core == 0, both[..., :lanes], both[..., lanes:])
            send1[k, at] = (own.astype(F32) + core_in[k, at].astype(F32)).astype(BF16)
            return 0

        lax.fori_loop(0, blocks // 4, add_half, 0)
        axis = order[k][0]
        row = []
        for off in (1, 2, 3):
            there, peer = along(axis, off)
            row.append(
                send(
                    send1.at[k, pl.ds(there * part, part)],
                    in1.at[k, off - 1],
                    sems(1, k, off - 1),
                    peer,
                )
            )
        firsts.append(row)

    for copy in shares:
        copy.wait()
    total = slabs_ref[0]
    for i in range(1, 8):
        total = total + slabs_ref[i]
    tm_total[...] = total
    core_copy = send(tm_total, core_sum, pair_sems(7), other)
    core_copy.wait()
    x_sums[x] = tm_total[...] + core_sum[...]
    x_copies = []
    for off in (1, 2, 3):
        _, peer = along(0, off)
        x_copies.append(send(x_sums.at[x], x_sums.at[x], pair_sems(7 + off), peer))

    seconds = []
    for k in range(3):
        for copy in firsts[k]:
            copy.wait()
        base = here[order[k][0]] * part

        def add_first(b, _, k=k, base=base):
            at = pl.ds(b * 3, 3)
            own = send1[k, pl.ds(base + b * 3, 3)].astype(F32)
            for i in range(3):
                own = own + in1[k, i, at].astype(F32)
            send2[k, at] = own.astype(BF16)
            return 0

        lax.fori_loop(0, part // 3, add_first, 0)
        axis = order[k][1]
        row = []
        for off in (1, 2, 3):
            there, peer = along(axis, off)
            row.append(
                send(
                    send2.at[k, pl.ds(there * piece, piece)],
                    in2.at[k, off - 1],
                    sems(2, k, off - 1),
                    peer,
                )
            )
        seconds.append(row)

    for copy in x_copies:
        copy.wait()
    x_total[...] = x_sums[0] + x_sums[1] + x_sums[2] + x_sums[3]
    z_copy = send(x_total, z_sum, pair_sems(11), across)

    thirds = []
    for k in range(3):
        for copy in seconds[k]:
            copy.wait()
        base = here[order[k][1]] * piece
        spot = here[order[k][2]]

        def add_second(b, _, k=k, base=base, spot=spot):
            at = pl.ds(b * 3, 3)
            own = send2[k, pl.ds(base + b * 3, 3)].astype(F32)
            for i in range(3):
                own = own + in2[k, i, at].astype(F32)
            in3[k, spot, at] = own.astype(BF16)
            return 0

        lax.fori_loop(0, piece // 3, add_second, 0)
        axis = order[k][2]
        row = []
        for off in (1, 2, 3):
            _, peer = along(axis, off)
            row.append(send(in3.at[k, spot], in3.at[k, spot], sems(3, k, off - 1), peer))
        thirds.append(row)

    z_copy.wait()
    pair_ref[...] = x_total[...] + z_sum[...]

    fourths = []
    for k in range(3):
        for copy in thirds[k]:
            copy.wait()
        base = here[order[k][0]] * part + here[order[k][1]] * piece

        def add_third(b, _, k=k, base=base):
            at = pl.ds(b * 3, 3)
            own = in3[k, 0, at].astype(F32)
            for i in range(1, 4):
                own = own + in3[k, i, at].astype(F32)
            total_ref[k, pl.ds(base + b * 3, 3), :, own_lanes] = own.astype(BF16)
            return 0

        lax.fori_loop(0, piece // 3, add_third, 0)
        spot = total_ref.at[k, pl.ds(base, piece), :, own_lanes]
        row = []
        for off in (1, 2, 3):
            _, peer = along(order[k][1], off)
            row.append(send(spot, spot, sems(4, k, off - 1), peer))
        fourths.append(row)
    fifths = []
    for k in range(3):
        for copy in fourths[k]:
            copy.wait()
        spot = total_ref.at[k, pl.ds(here[order[k][0]] * part, part), :, own_lanes]
        row = []
        for off in (1, 2, 3):
            _, peer = along(order[k][0], off)
            row.append(send(spot, spot, sems(5, k, off - 1), peer))
        fifths.append(row)
    for k in range(3):
        for copy in fifths[k]:
            copy.wait()
        spot = total_ref.at[k, :, :, own_lanes]
        started.append(send(spot, spot, sems(6, k, 0), other))
    for copy in started:
        copy.wait()


def reduce_all(mine, sums, slabs, collective_id):
    streams, blocks, sub, channels = mine.shape
    part, piece, lanes = blocks // 4, blocks // 16, channels // 2
    small = pltpu.VMEM(sums.shape, F32)

    def slots(*lead):
        return pltpu.VMEM(lead + (sub, lanes), BF16)

    return pl.pallas_call(
        functools.partial(reduce_kernel, blocks),
        out_shape=(
            jax.ShapeDtypeStruct(mine.shape, BF16),
            jax.ShapeDtypeStruct((slabs,) + sums.shape, F32),
            jax.ShapeDtypeStruct(sums.shape, F32),
        ),
        in_specs=[VMEM, VMEM],
        out_specs=(VMEM,) * 3,
        scratch_shapes=[
            slots(streams, blocks),
            slots(streams, blocks),
            slots(streams, 3, part),
            slots(streams, part),
            slots(streams, 3, piece),
            slots(streams, 4, piece),
            small,
            small,
            pltpu.VMEM((4,) + sums.shape, F32),
            small,
            small,
            pltpu.SemaphoreType.DMA((7, streams, 3)),
            pltpu.SemaphoreType.DMA((7, streams, 3)),
            pltpu.SemaphoreType.DMA((12,)),
            pltpu.SemaphoreType.DMA((12,)),
        ],
        compiler_params=params(40, collective_id=collective_id, has_side_effects=True),
    )(mine, sums)


def body(loaded, lengths, resolution, weight, norm_gain, norm_bias, cotangent):
    frames, rows, cols, channels = loaded.shape[1:]
    places, width = rows * cols, channels // GROUPS
    slabs = lax.axis_size("tm")
    shape = jax.ShapeDtypeStruct
    loaded = loaded.reshape(frames, places, channels)
    cotangent = cotangent.reshape(frames, places, channels)
    gain, bias = norm_gain.reshape(1, channels), norm_bias.reshape(1, channels)

    following = shifted(cotangent[:2], "tm", -1)
    arrived = shifted(loaded, "tm", -1)
    stats, tail = pl.pallas_call(
        functools.partial(stats_kernel, slabs, cols, width),
        out_shape=(shape((8, channels), F32), shape((2, places, channels), BF16)),
        in_specs=[SMEM, SMEM, VMEM],
        out_specs=(VMEM, VMEM),
        scratch_shapes=[pltpu.VMEM((places, channels), F32)],
        compiler_params=params(16),
        cost_estimate=pl.CostEstimate(flops=4 << 20, bytes_accessed=2 << 20, transcendentals=0),
    )(lengths, resolution, loaded)
    tail = shifted(tail, "tm", 1)
    cat = pltpu.VMEM((frames + 2, rows + 2, cols, 3 * channels), BF16)
    plane = pltpu.VMEM((places, channels), F32)
    agrad = pl.pallas_call(
        functools.partial(back_kernel, slabs, rows, cols),
        out_shape=shape((frames, places, channels), F32),
        in_specs=[SMEM, SMEM, VMEM, VMEM, VMEM],
        out_specs=VMEM,
        scratch_shapes=[cat, pltpu.VMEM((9, 3 * channels, channels), BF16), plane, plane, plane],
        compiler_params=params(40),
        cost_estimate=pl.CostEstimate(
            flops=2 * 27 * frames * places * channels * channels,
            bytes_accessed=8 << 20,
            transcendentals=0,
        ),
    )(lengths, resolution, cotangent, following, weight)
    stats, agrad = lax.optimization_barrier((stats, agrad))
    all_stats = share(stats, slabs, 1)

    encoded, kernel_part, sums, root, ngrad, normed = pl.pallas_call(
        functools.partial(main_kernel, slabs, rows, cols, width),
        out_shape=(
            shape((frames, places, channels), BF16),
            shape((9, 3 * channels, channels), BF16),
            shape((8, channels), F32),
            shape((8, channels), F32),
            shape((frames, places, channels), F32),
            shape((frames, places, channels), F32),
        ),
        in_specs=[SMEM, SMEM] + [VMEM] * 9,
        out_specs=(VMEM,) * 6,
        scratch_shapes=[cat, pltpu.VMEM((frames * places, channels), BF16), plane, plane, plane],
        compiler_params=params(56),
        cost_estimate=pl.CostEstimate(
            flops=4 * 27 * frames * places * channels * channels,
            bytes_accessed=20 << 20,
            transcendentals=frames * places * channels,
        ),
    )(
        lengths, resolution, loaded, arrived, tail, cotangent, agrad, all_stats,
        gain, bias, weight.reshape(9, 3 * channels, channels),
    )

    total, all_sums, pair = reduce_all(
        kernel_part.reshape(3, 9 * channels // 16, 16, channels), sums, slabs, 2
    )
    block = pl.BlockSpec((1, places, channels), lambda f: (f, 0, 0))
    input_grad = pl.pallas_call(
        functools.partial(last_kernel, slabs, cols, width, frames),
        out_shape=shape((frames, places, channels), BF16),
        grid=(frames,),
        in_specs=[
            SMEM,
            SMEM,
            pl.BlockSpec((slabs, 8, channels), lambda f: (0, 0, 0)),
            pl.BlockSpec((1, channels), lambda f: (0, 0)),
            pl.BlockSpec((8, channels), lambda f: (0, 0)),
            block,
            block,
        ],
        out_specs=block,
        compiler_params=params(16),
    )(lengths, resolution, all_sums, gain, root, ngrad, normed)

    scale = 1.0 / math.sqrt(lax.axis_size("dp") * slabs * frames * places)
    whole = (1, frames, rows, cols, channels)
    return (
        encoded.reshape(whole),
        input_grad.reshape(whole),
        total.reshape(27, channels, channels).astype(F32) * scale,
        pair[0] * scale,
        pair[1] * scale,
    )


def solution(mesh):
    slab = P("dp", "tm", None, None, None)
    return jax.shard_map(
        body,
        mesh=mesh,
        in_specs=(slab, P("dp", None), P("dp", None), P(), P(), P(), slab),
        out_specs=(slab, slab, P(), P(), P()),
        check_vma=False,
    )
```

```python
import functools
import math

import jax
import jax.numpy as jnp
from jax import lax
from jax.experimental import pallas as pl
from jax.experimental.pallas import tpu as pltpu
from jax.sharding import PartitionSpec as P

GROUPS = 32
EPSILON = 1e-05
MESH = pl.DeviceIdType.MESH
F32 = jnp.float32
BF16 = jnp.bfloat16

VMEM = pl.BlockSpec(memory_space=pltpu.VMEM)
ANY = pl.BlockSpec(memory_space=pl.ANY)
SMEM = pl.BlockSpec(memory_space=pltpu.SMEM)


def params(limit, **others):
    return pltpu.CompilerParams(vmem_limit_bytes=limit << 20, **others)


def start_of(len_ref, slabs, index):
    total = jnp.int32(0)
    for i in range(slabs):
        total = total + jnp.where(i < index, len_ref[0, i], 0)
    return total


def length_of(len_ref, slabs, index):
    total = jnp.int32(0)
    for i in range(slabs):
        total = total + jnp.where(i == index, len_ref[0, i], 0)
    return total


def group_sum(rows, width):
    lanes = rows.shape[1]
    lane = lax.broadcasted_iota(jnp.int32, rows.shape, 1)
    step = 1
    while step < width:
        up = pltpu.roll(rows, lanes - step, 1)
        down = pltpu.roll(rows, step, 1)
        rows = rows + jnp.where((lane & step) == 0, up, down)
        step *= 2
    return rows


def cells(res_ref, cols, shape):
    place = lax.broadcasted_iota(jnp.int32, shape, 0)
    return ((place // cols) < res_ref[0, 0]) & ((place % cols) < res_ref[0, 1])


def lay_out(cat_ref, frame, value, rows, cols, first_col, last_col):
    places, channels = value.shape
    left = pltpu.roll(value, 1, 0) * first_col
    right = pltpu.roll(value, places - 1, 0) * last_col
    for k, part in enumerate((left, value, right)):
        cat_ref[frame, 1 : rows + 1, :, k * channels : (k + 1) * channels] = (
            part.astype(BF16).reshape(rows, cols, channels)
        )


def col_masks(cols, shape):
    place = lax.broadcasted_iota(jnp.int32, shape, 0) % cols
    return (place != 0).astype(F32), (place != cols - 1).astype(F32)


def section_kernel(
    rows, cols, width,
    len_ref, res_ref, loaded_hbm, cot_hbm, weight_hbm, gain_ref, bias_ref,
    encoded_hbm, igrad_hbm, total_ref, pair_ref,
    loaded_ref, arrived_ref, cot_ref, next_ref, tail_out, tail_ref, weight_ref, turned_ref,
    back_cat, cat_ref, grad_ref, agrad_ref, normed_ref, encoded_ref, igrad_ref,
    mask_ref, first_ref, last_ref, stats_out, stats_ref, sums_ref, slabs_ref,
    own_part, far_part, core_in, send1, in1, send2, in2, in3,
    tm_total, core_sum, x_sums, x_total, z_sum,
    local_sem, move_send, move_recv, stat_send, stat_recv,
    send_sem, recv_sem, pair_send, pair_recv,
):
    frames, places, channels = loaded_ref.shape
    blocks = own_part.shape[1]
    part, piece, lanes = blocks // 4, blocks // 16, channels // 2
    per_row = blocks // 3
    slabs = 8

    dp, tm = lax.axis_index("dp"), lax.axis_index("tm")
    core, x, y = dp % 2, dp // 4, tm % 4
    z = (dp // 2) % 2 * 2 + tm // 4
    here = (x, y, z)

    def device(place, its_core):
        return ((place[0] * 2 + place[2] // 2) * 2 + its_core, (place[2] % 2) * 4 + place[1])

    def along(axis, off):
        place = list(here)
        place[axis] = (here[axis] + off) % 4
        return place[axis], device(place, core)

    other = device(here, 1 - core)
    across = device((x, y, (z + 2) % 4), core)
    tm_peers = [(dp, (tm + off) % slabs) for off in range(1, slabs)]
    axis_peers = [along(axis, off)[1] for axis in (0, 1, 2) for off in (1, 2, 3)]
    before, after = (dp, (tm + slabs - 1) % slabs), (dp, (tm + 1) % slabs)
    has_before, has_after = tm > 0, tm < slabs - 1

    barrier = pltpu.get_barrier_semaphore()
    greeted = [other] + axis_peers + tm_peers
    for peer in greeted:
        pl.semaphore_signal(barrier, inc=1, device_id=peer, device_id_type=MESH)

    loads = [
        pltpu.make_async_copy(src, dst, local_sem.at[i])
        for i, (src, dst) in enumerate(
            ((loaded_hbm, loaded_ref), (cot_hbm, cot_ref), (weight_hbm, weight_ref))
        )
    ]
    for load in loads:
        load.start()
    pl.semaphore_wait(barrier, len(greeted))

    def remote(src, dst, send_at, recv_at, peer):
        return pltpu.make_async_remote_copy(
            src_ref=src, dst_ref=dst, send_sem=send_at, recv_sem=recv_at,
            device_id=peer, device_id_type=MESH,
        )

    def send(*arguments):
        copy = remote(*arguments)
        copy.start()
        return copy

    halo = remote(cot_hbm.at[pl.ds(0, 2)], next_ref, move_send.at[0], move_recv.at[0], before)
    bulk = remote(loaded_hbm, arrived_ref, move_send.at[1], move_recv.at[1], before)
    tails = remote(tail_out, tail_ref, move_send.at[2], move_recv.at[2], after)

    @pl.when(has_before)
    def _():
        halo.start()
        bulk.start()

    @pl.when(tm == slabs - 1)
    def _():
        next_ref[...] = jnp.zeros_like(next_ref)
        arrived_ref[...] = jnp.zeros_like(arrived_ref)

    @pl.when(tm == 0)
    def _():
        tail_ref[...] = jnp.zeros_like(tail_ref)

    own_start, own_length = start_of(len_ref, slabs, tm), length_of(len_ref, slabs, tm)
    next_start, next_length = own_start + own_length, length_of(len_ref, slabs, tm + 1)
    frame_total = start_of(len_ref, slabs, slabs)
    area = res_ref[0, 0] * res_ref[0, 1] * width
    count = (frame_total * area).astype(F32)
    mask_ref[...] = cells(res_ref, cols, (places, channels)).astype(F32)
    first, last = col_masks(cols, (places, channels))
    first_ref[...] = first
    last_ref[...] = last
    zero = jnp.zeros((8, channels), F32)
    row = lax.broadcasted_iota(jnp.int32, (8, channels), 0)

    loads[0].wait()

    def fold(value):
        return jnp.sum(value.reshape(places // 8, 8, channels), axis=0)

    def over_groups(total):
        line = jnp.sum(total, axis=0, keepdims=True)
        return group_sum(jnp.broadcast_to(line, (8, channels)), width)

    def add_up(f, total):
        held = (f < own_length).astype(F32)
        return total + fold(loaded_ref[f].astype(F32) * (mask_ref[...] * held))

    own_mean = over_groups(lax.fori_loop(0, frames, add_up, zero)) / (own_length * area).astype(F32)
    mean_row = own_mean[0:1]

    def spread(f, total):
        held = (f < own_length).astype(F32)
        apart = (loaded_ref[f].astype(F32) - mean_row) * (mask_ref[...] * held)
        return total + fold(apart * apart)

    squares = over_groups(lax.fori_loop(0, frames, spread, zero))
    stats_out[...] = jnp.where(row == 0, own_mean, squares)
    stats_ref[tm] = stats_out[...]
    stats_shares = [
        send(stats_out, stats_ref.at[tm], stat_send.at[i], stat_recv.at[i], peer)
        for i, peer in enumerate(tm_peers)
    ]
    for k in range(2):
        offset = tm * frames + frames - 2 + k - own_start
        usable = (offset >= 0) & (offset < own_length)
        picked = loaded_ref[jnp.clip(offset, 0, frames - 1)]
        tail_out[k] = jnp.where(usable, picked, jnp.zeros_like(picked))

    @pl.when(has_after)
    def _():
        tails.start()

    loads[2].wait()

    def turn(block, _):
        for k in range(3):
            turned_ref[block, k * channels : (k + 1) * channels, :] = weight_ref[
                block, (2 - k) * channels : (3 - k) * channels, :
            ].T
        return 0

    lax.fori_loop(0, 9, turn, 0)
    blank = jnp.zeros((cols, 3 * channels), BF16)

    def place(frame, value):
        alive = (tm * frames + frame < frame_total).astype(F32)
        value = value.astype(F32) * (mask_ref[...] * alive)
        back_cat[frame, 0] = blank
        back_cat[frame, rows + 1] = blank
        lay_out(back_cat, frame, value, rows, cols, first_ref[...], last_ref[...])
        return value

    loads[1].wait()

    def own_grad(f, _):
        value = place(f, cot_ref[f])
        grad_ref[pl.ds(pl.multiple_of(f * places, places), places)] = value.astype(BF16)
        return 0

    lax.fori_loop(0, frames, own_grad, 0)

    def convolve(source, factor, f, back):
        total = jnp.zeros((places, channels), F32)
        for d in range(3):
            for r in range(3):
                at = (f + 2 - d, 2 - r) if back else (f + d, r)
                lines = source[at[0], at[1] : at[1] + rows].reshape(places, 3 * channels)
                total = total + jnp.dot(lines, factor[3 * d + r], preferred_element_type=F32)
        return total * (mask_ref[...] * (tm * frames + f < frame_total).astype(F32))

    def back_sweep(f, _):
        agrad_ref[f] = convolve(back_cat, turned_ref, f, True)
        return 0

    lax.fori_loop(0, frames - 2, back_sweep, 0)

    @pl.when(has_after)
    def _():
        halo.wait_recv()

    for k in range(2):
        place(frames + k, next_ref[k])
    lax.fori_loop(frames - 2, frames, back_sweep, 0)

    for copy in stats_shares:
        copy.wait()
    counts = [(len_ref[0, i] * area).astype(F32) for i in range(slabs)]
    mean = jnp.zeros((1, channels), F32)
    for i in range(slabs):
        mean = mean + counts[i] * stats_ref[i, 0:1]
    mean = mean / count
    squares = jnp.zeros((1, channels), F32)
    for i in range(slabs):
        apart = stats_ref[i, 0:1] - mean
        squares = squares + stats_ref[i, 1:2] + counts[i] * (apart * apart)
    root = lax.rsqrt(squares / count + EPSILON)
    gain, bias = gain_ref[...], bias_ref[...]

    def activate(slot, frame_id, value):
        alive = ((frame_id >= 0) & (frame_id < frame_total)).astype(F32)
        live = mask_ref[...] * alive
        normed = (value.astype(F32) * live - mean) * live * root
        pre = normed * gain + bias
        gate = 1.0 / (1.0 + jnp.exp(-pre))
        act = (pre * gate * live).astype(BF16).astype(F32)
        cat_ref[slot, 0] = blank
        cat_ref[slot, rows + 1] = blank
        lay_out(cat_ref, slot, act, rows, cols, first_ref[...], last_ref[...])
        return normed, pre, gate

    @pl.when(has_before)
    def _():
        tails.wait_recv()

    for k in range(2):
        frame_id = tm * frames + k - 2
        offset = frame_id - own_start
        usable = (offset >= 0) & (offset < own_length)
        picked = jnp.where(usable, loaded_ref[jnp.clip(offset, 0, frames - 1)], tail_ref[k])
        activate(k, frame_id, picked)

    @pl.when(has_after)
    def _():
        bulk.wait_recv()

    def own_frame(f, sums):
        frame_id = tm * frames + f
        offset = frame_id - own_start
        later = frame_id - next_start
        picked = jnp.where(
            offset < own_length,
            loaded_ref[jnp.clip(offset, 0, frames - 1)],
            arrived_ref[jnp.clip(later, 0, frames - 1)],
        )
        normed, pre, gate = activate(f + 2, frame_id, picked)
        pre_grad = agrad_ref[f] * gate * (1.0 + pre * (1.0 - gate))
        normed_ref[f] = normed
        agrad_ref[f] = pre_grad * gain
        return sums[0] + fold(pre_grad * normed), sums[1] + fold(pre_grad)

    gain_sum, bias_sum = lax.fori_loop(0, frames, own_frame, (zero, zero))
    sums_ref[...] = jnp.where(
        row == 0,
        jnp.sum(gain_sum, axis=0, keepdims=True),
        jnp.where(row == 1, jnp.sum(bias_sum, axis=0, keepdims=True), 0.0),
    )
    slabs_ref[tm] = sums_ref[...]
    shares = [
        send(sums_ref, slabs_ref.at[tm], pair_send.at[i], pair_recv.at[i], peer)
        for i, peer in enumerate(tm_peers)
    ]

    order = [(k % 3, (k + 1) % 3, (k + 2) % 3) for k in range(3)]
    own_lanes = pl.ds(pl.multiple_of(core * lanes, lanes), lanes)

    def spread_out(stage, k, axis, source, target):
        row_of = []
        for off in (1, 2, 3):
            there, peer = along(axis, off)
            row_of.append(
                send(
                    source(there), target(off - 1),
                    send_sem.at[stage, k, off - 1], recv_sem.at[stage, k, off - 1], peer,
                )
            )
        return row_of

    def kernel_part(k):
        for r in range(3):
            lines = cat_ref[k : k + frames, r : r + rows].reshape(frames * places, 3 * channels)
            product = lax.dot_general(
                lines, grad_ref[...], (((0,), (0,)), ((), ())), preferred_element_type=F32
            ).reshape(per_row, 16, channels)
            low, high = product[..., :lanes], product[..., lanes:]
            at = slice(r * per_row, (r + 1) * per_row)
            own_part[k, at] = jnp.where(core == 0, low, high)
            far_part[k, at] = jnp.where(core == 0, high, low).astype(BF16)
        return send(
            far_part.at[k], core_in.at[k], send_sem.at[0, k, 0], recv_sem.at[0, k, 0], other
        )

    def first_stage(k, half):
        half.wait()

        def add_half(b, _):
            at = pl.ds(b * 4, 4)
            both = own_part[k, at] + core_in[k, at].astype(F32)
            own_part[k, at] = both
            send1[k, at] = both.astype(BF16)
            return 0

        lax.fori_loop(0, blocks // 4, add_half, 0)
        return spread_out(
            1, k, order[k][0],
            lambda there: send1.at[k, pl.ds(there * part, part)],
            lambda i: in1.at[k, i],
        )

    def second_stage(k, copies):
        for copy in copies:
            copy.wait()
        base = here[order[k][0]] * part

        def add_first(b, _):
            at = pl.ds(b * 3, 3)
            own = own_part[k, pl.ds(base + b * 3, 3)]
            for i in range(3):
                own = own + in1[k, i, at].astype(F32)
            send2[k, at] = own.astype(BF16)
            return 0

        lax.fori_loop(0, part // 3, add_first, 0)
        return spread_out(
            2, k, order[k][1],
            lambda there: send2.at[k, pl.ds(there * piece, piece)],
            lambda i: in2.at[k, i],
        )

    def third_stage(k, copies):
        for copy in copies:
            copy.wait()
        base = here[order[k][1]] * piece
        spot = here[order[k][2]]

        def add_second(b, _):
            at = pl.ds(b * 3, 3)
            own = send2[k, pl.ds(base + b * 3, 3)].astype(F32)
            for i in range(3):
                own = own + in2[k, i, at].astype(F32)
            in3[k, spot, at] = own.astype(BF16)
            return 0

        lax.fori_loop(0, piece // 3, add_second, 0)
        return spread_out(
            3, k, order[k][2], lambda there: in3.at[k, spot], lambda i: in3.at[k, spot]
        )

    def fourth_stage(k, copies):
        for copy in copies:
            copy.wait()
        base = here[order[k][0]] * part + here[order[k][1]] * piece

        def add_third(b, _):
            at = pl.ds(b * 3, 3)
            own = in3[k, 0, at].astype(F32)
            for i in range(1, 4):
                own = own + in3[k, i, at].astype(F32)
            total_ref[k, pl.ds(base + b * 3, 3), :, own_lanes] = own.astype(BF16)
            return 0

        lax.fori_loop(0, piece // 3, add_third, 0)
        spot = total_ref.at[k, pl.ds(base, piece), :, own_lanes]
        return spread_out(4, k, order[k][1], lambda there: spot, lambda i: spot)

    def fifth_stage(k, copies):
        for copy in copies:
            copy.wait()
        spot = total_ref.at[k, pl.ds(here[order[k][0]] * part, part), :, own_lanes]
        return spread_out(5, k, order[k][0], lambda there: spot, lambda i: spot)

    def sixth_stage(k, copies):
        for copy in copies:
            copy.wait()
        spot = total_ref.at[k, :, :, own_lanes]
        return send(spot, spot, send_sem.at[6, k, 0], recv_sem.at[6, k, 0], other)

    def forward_sweep(f, _):
        encoded_ref[f] = convolve(cat_ref, weight_ref, f, False).astype(BF16)
        return 0

    half0 = kernel_part(0)
    half1 = kernel_part(1)
    stage0 = first_stage(0, half0)
    half2 = kernel_part(2)
    stage1 = first_stage(1, half1)

    for copy in shares:
        copy.wait()
    total = slabs_ref[0]
    for i in range(1, slabs):
        total = total + slabs_ref[i]
    tm_total[...] = total
    core_copy = send(tm_total, core_sum, pair_send.at[7], pair_recv.at[7], other)

    lax.fori_loop(0, 2, forward_sweep, 0)
    stage2 = first_stage(2, half2)

    core_copy.wait()
    x_sums[x] = tm_total[...] + core_sum[...]
    x_copies = [
        send(x_sums.at[x], x_sums.at[x], pair_send.at[7 + off], pair_recv.at[7 + off], along(0, off)[1])
        for off in (1, 2, 3)
    ]
    lax.fori_loop(2, 5, forward_sweep, 0)
    stage0 = second_stage(0, stage0)
    lax.fori_loop(5, frames, forward_sweep, 0)
    stage1 = second_stage(1, stage1)
    encoded_copy = pltpu.make_async_copy(encoded_ref, encoded_hbm, local_sem.at[3])
    encoded_copy.start()

    for copy in x_copies:
        copy.wait()
    x_total[...] = x_sums[0] + x_sums[1] + x_sums[2] + x_sums[3]
    z_copy = send(x_total, z_sum, pair_send.at[11], pair_recv.at[11], across)

    stage0 = third_stage(0, stage0)
    stage2 = second_stage(2, stage2)
    stage1 = third_stage(1, stage1)

    shares_of = group_sum(tm_total[...] * gain, width) / count
    mean_part, along_part = shares_of[1:2], shares_of[0:1]

    def finish(f, _):
        live = mask_ref[...] * (tm * frames + f < frame_total).astype(F32)
        inner = agrad_ref[f] - mean_part - normed_ref[f] * along_part
        igrad_ref[f] = (inner * root * live).astype(BF16)
        return 0

    lax.fori_loop(0, frames, finish, 0)
    igrad_copy = pltpu.make_async_copy(igrad_ref, igrad_hbm, local_sem.at[4])
    igrad_copy.start()

    stage0 = fourth_stage(0, stage0)
    stage2 = third_stage(2, stage2)
    stage1 = fourth_stage(1, stage1)
    z_copy.wait()
    pair_ref[...] = x_total[...] + z_sum[...]
    stage0 = fifth_stage(0, stage0)
    stage2 = fourth_stage(2, stage2)
    stage1 = fifth_stage(1, stage1)
    stage2 = fifth_stage(2, stage2)
    ends = [sixth_stage(0, stage0), sixth_stage(1, stage1), sixth_stage(2, stage2)]
    for copy in ends:
        copy.wait()
    encoded_copy.wait()
    igrad_copy.wait()

    @pl.when(has_before)
    def _():
        halo.wait_send()
        bulk.wait_send()

    @pl.when(has_after)
    def _():
        tails.wait_send()


def body(loaded, lengths, resolution, weight, norm_gain, norm_bias, cotangent):
    frames, rows, cols, channels = loaded.shape[1:]
    places, width, lanes = rows * cols, channels // GROUPS, channels // 2
    slabs = lax.axis_size("tm")
    shape = jax.ShapeDtypeStruct
    slab = (frames, places, channels)
    blocks = 9 * channels // 16
    part, piece = blocks // 4, blocks // 16

    def tiles(*lead, kind=BF16):
        return pltpu.VMEM(lead + (16, lanes), kind)

    small = pltpu.VMEM((8, channels), F32)
    plane = pltpu.VMEM((places, channels), F32)
    cat = pltpu.VMEM((frames + 2, rows + 2, cols, 3 * channels), BF16)
    dma = pltpu.SemaphoreType.DMA
    encoded, igrad, total, pair = pl.pallas_call(
        functools.partial(section_kernel, rows, cols, width),
        out_shape=(
            shape(slab, BF16),
            shape(slab, BF16),
            shape((3, blocks, 16, channels), BF16),
            shape((8, channels), F32),
        ),
        in_specs=[SMEM, SMEM, ANY, ANY, ANY, VMEM, VMEM],
        out_specs=(ANY, ANY, VMEM, VMEM),
        scratch_shapes=[
            pltpu.VMEM(slab, BF16),
            pltpu.VMEM(slab, BF16),
            pltpu.VMEM(slab, BF16),
            pltpu.VMEM((2, places, channels), BF16),
            pltpu.VMEM((2, places, channels), BF16),
            pltpu.VMEM((2, places, channels), BF16),
            pltpu.VMEM((9, 3 * channels, channels), BF16),
            pltpu.VMEM((9, 3 * channels, channels), BF16),
            cat,
            cat,
            pltpu.VMEM((frames * places, channels), BF16),
            pltpu.VMEM(slab, F32),
            pltpu.VMEM(slab, F32),
            pltpu.VMEM(slab, BF16),
            pltpu.VMEM(slab, BF16),
            plane,
            plane,
            plane,
            small,
            pltpu.VMEM((slabs, 8, channels), F32),
            small,
            pltpu.VMEM((slabs, 8, channels), F32),
            tiles(3, blocks, kind=F32),
            tiles(3, blocks),
            tiles(3, blocks),
            tiles(3, blocks),
            tiles(3, 3, part),
            tiles(3, part),
            tiles(3, 3, piece),
            tiles(3, 4, piece),
            small,
            small,
            pltpu.VMEM((4, 8, channels), F32),
            small,
            small,
            dma((5,)),
            dma((3,)),
            dma((3,)),
            dma((7,)),
            dma((7,)),
            dma((7, 3, 3)),
            dma((7, 3, 3)),
            dma((12,)),
            dma((12,)),
        ],
        compiler_params=params(58, collective_id=1, has_side_effects=True),
    )(
        lengths,
        resolution,
        loaded.reshape(slab),
        cotangent.reshape(slab),
        weight.reshape(9, 3 * channels, channels),
        norm_gain.reshape(1, channels),
        norm_bias.reshape(1, channels),
    )
    scale = 1.0 / math.sqrt(lax.axis_size("dp") * slabs * frames * places)
    whole = (1, frames, rows, cols, channels)
    return (
        encoded.reshape(whole),
        igrad.reshape(whole),
        total.reshape(27, channels, channels).astype(F32) * scale,
        pair[0] * scale,
        pair[1] * scale,
    )


def solution(mesh):
    slab = P("dp", "tm", None, None, None)
    return jax.shard_map(
        body,
        mesh=mesh,
        in_specs=(slab, P("dp", None), P("dp", None), P(), P(), P(), slab),
        out_specs=(slab, slab, P(), P(), P()),
        check_vma=False,
    )
```

```python
import functools
import math

import jax
import jax.numpy as jnp
from jax import lax
from jax.experimental import pallas as pl
from jax.experimental.pallas import tpu as pltpu
from jax.sharding import PartitionSpec as P

GROUPS = 32
EPSILON = 1e-05
MESH = pl.DeviceIdType.MESH
F32 = jnp.float32
BF16 = jnp.bfloat16

VMEM = pl.BlockSpec(memory_space=pltpu.VMEM)
ANY = pl.BlockSpec(memory_space=pl.ANY)
SMEM = pl.BlockSpec(memory_space=pltpu.SMEM)


def params(limit, **others):
    return pltpu.CompilerParams(vmem_limit_bytes=limit << 20, **others)


def start_of(len_ref, slabs, index):
    total = jnp.int32(0)
    for i in range(slabs):
        total = total + jnp.where(i < index, len_ref[0, i], 0)
    return total


def length_of(len_ref, slabs, index):
    total = jnp.int32(0)
    for i in range(slabs):
        total = total + jnp.where(i == index, len_ref[0, i], 0)
    return total


def group_sum(rows, width):
    lanes = rows.shape[1]
    lane = lax.broadcasted_iota(jnp.int32, rows.shape, 1)
    step = 1
    while step < width:
        up = pltpu.roll(rows, lanes - step, 1)
        down = pltpu.roll(rows, step, 1)
        rows = rows + jnp.where((lane & step) == 0, up, down)
        step *= 2
    return rows


def cells(res_ref, cols, shape):
    place = lax.broadcasted_iota(jnp.int32, shape, 0)
    return ((place // cols) < res_ref[0, 0]) & ((place % cols) < res_ref[0, 1])


def lay_out(cat_ref, frame, value, rows, cols, first_col, last_col):
    places, channels = value.shape
    left = pltpu.roll(value, 1, 0) * first_col
    right = pltpu.roll(value, places - 1, 0) * last_col
    for k, part in enumerate((left, value, right)):
        cat_ref[frame, 1 : rows + 1, :, k * channels : (k + 1) * channels] = (
            part.astype(BF16).reshape(rows, cols, channels)
        )


def col_masks(cols, shape):
    place = lax.broadcasted_iota(jnp.int32, shape, 0) % cols
    return (place != 0).astype(F32), (place != cols - 1).astype(F32)


def section_kernel(
    rows, cols, width,
    len_ref, res_ref, loaded_hbm, cot_hbm, weight_hbm, gain_ref, bias_ref,
    encoded_hbm, igrad_hbm, total_hbm, pair_ref,
    loaded_ref, leaving_ref, arrived_ref, cot_ref, next_ref, tail_out, tail_ref, weight_ref, turned_ref,
    back_cat, cat_ref, grad_ref, agrad_ref, normed_ref, encoded_ref, igrad_ref,
    mask_ref, first_ref, last_ref, stats_out, stats_ref, sums_ref, slabs_ref,
    total_ref, own_part, far_sum, far_part, core_in, send1, in1, send2, in2, in3,
    tm_total, core_sum, x_sums, x_total, z_sum,
    local_sem, move_send, move_recv, stat_send, stat_recv,
    send_sem, recv_sem, pair_send, pair_recv,
):
    frames, places, channels = loaded_ref.shape
    blocks = own_part.shape[1]
    part, piece, lanes = blocks // 4, blocks // 16, channels // 2
    per_row = blocks // 3
    early = frames - 2
    slabs = 8

    dp, tm = lax.axis_index("dp"), lax.axis_index("tm")
    core, x, y = dp % 2, dp // 4, tm % 4
    z = (dp // 2) % 2 * 2 + tm // 4
    here = (x, y, z)

    def device(place, its_core):
        return ((place[0] * 2 + place[2] // 2) * 2 + its_core, (place[2] % 2) * 4 + place[1])

    def along(axis, off):
        place = list(here)
        place[axis] = (here[axis] + off) % 4
        return place[axis], device(place, core)

    other = device(here, 1 - core)
    across = device((x, y, (z + 2) % 4), core)
    tm_peers = [(dp, (tm + off) % slabs) for off in range(1, slabs)]
    axis_peers = [along(axis, off)[1] for axis in (0, 1, 2) for off in (1, 2, 3)]
    before, after = (dp, (tm + slabs - 1) % slabs), (dp, (tm + 1) % slabs)
    has_before, has_after = tm > 0, tm < slabs - 1

    barrier = pltpu.get_barrier_semaphore()
    greeted = [other] + axis_peers + tm_peers
    for peer in greeted:
        pl.semaphore_signal(barrier, inc=1, device_id=peer, device_id_type=MESH)

    loads = [
        pltpu.make_async_copy(src, dst, local_sem.at[i])
        for i, (src, dst) in enumerate(
            ((loaded_hbm, loaded_ref), (cot_hbm, cot_ref), (weight_hbm, weight_ref))
        )
    ]
    for load in loads:
        load.start()

    def remote(src, dst, send_at, recv_at, peer):
        return pltpu.make_async_remote_copy(
            src_ref=src, dst_ref=dst, send_sem=send_at, recv_sem=recv_at,
            device_id=peer, device_id_type=MESH,
        )

    def send(*arguments):
        copy = remote(*arguments)
        copy.start()
        return copy

    halo = remote(
        cot_hbm.at[pl.ds(0, 2)], next_ref, move_send.at[frames], move_recv.at[frames], before
    )
    tails = remote(
        tail_out, tail_ref, move_send.at[frames + 1], move_recv.at[frames + 1], after
    )

    def moved(f):
        return remote(
            leaving_ref.at[f], arrived_ref.at[f], move_send.at[f], move_recv.at[f], before
        )

    @pl.when(tm == slabs - 1)
    def _():
        next_ref[...] = jnp.zeros_like(next_ref)
        arrived_ref[...] = jnp.zeros_like(arrived_ref)

    @pl.when(tm == 0)
    def _():
        tail_ref[...] = jnp.zeros_like(tail_ref)

    own_start, own_length = start_of(len_ref, slabs, tm), length_of(len_ref, slabs, tm)
    frame_total = start_of(len_ref, slabs, slabs)
    area = res_ref[0, 0] * res_ref[0, 1] * width
    count = (frame_total * area).astype(F32)
    mask_ref[...] = cells(res_ref, cols, (places, channels)).astype(F32)
    first, last = col_masks(cols, (places, channels))
    first_ref[...] = first
    last_ref[...] = last
    zero = jnp.zeros((8, channels), F32)
    row = lax.broadcasted_iota(jnp.int32, (8, channels), 0)

    loads[0].wait()

    def fold(value):
        return jnp.sum(value.reshape(places // 8, 8, channels), axis=0)

    def over_groups(total):
        line = jnp.sum(total, axis=0, keepdims=True)
        return group_sum(jnp.broadcast_to(line, (8, channels)), width)

    def add_up(f, total):
        held = (f < own_length).astype(F32)
        return total + fold(loaded_ref[f].astype(F32) * (mask_ref[...] * held))

    own_mean = over_groups(lax.fori_loop(0, frames, add_up, zero)) / (own_length * area).astype(F32)
    mean_row = own_mean[0:1]

    def spread(f, total):
        held = (f < own_length).astype(F32)
        apart = (loaded_ref[f].astype(F32) - mean_row) * (mask_ref[...] * held)
        return total + fold(apart * apart)

    squares = over_groups(lax.fori_loop(0, frames, spread, zero))
    stats_out[...] = jnp.where(row == 0, own_mean, squares)
    stats_ref[tm] = stats_out[...]
    for k in range(2):
        offset = tm * frames + frames - 2 + k - own_start
        usable = (offset >= 0) & (offset < own_length)
        picked = loaded_ref[jnp.clip(offset, 0, frames - 1)]
        tail_out[k] = jnp.where(usable, picked, jnp.zeros_like(picked))


    def pack(f, _):
        offset = (tm - 1) * frames + f - own_start
        usable = (offset >= 0) & (offset < own_length)
        picked = loaded_ref[jnp.clip(offset, 0, frames - 1)]
        leaving_ref[f] = jnp.where(usable, picked, jnp.zeros_like(picked))
        return 0

    lax.fori_loop(0, frames, pack, 0)

    pl.semaphore_wait(barrier, len(greeted))
    stats_shares = [
        send(stats_out, stats_ref.at[tm], stat_send.at[i], stat_recv.at[i], peer)
        for i, peer in enumerate(tm_peers)
    ]

    @pl.when(has_after)
    def _():
        tails.start()

    @pl.when(has_before)
    def _():
        for f in range(frames):
            moved(f).start()
        halo.start()

    loads[2].wait()

    def turn(block, _):
        for k in range(3):
            turned_ref[block, k * channels : (k + 1) * channels, :] = weight_ref[
                block, (2 - k) * channels : (3 - k) * channels, :
            ].T
        return 0

    lax.fori_loop(0, 9, turn, 0)
    blank = jnp.zeros((cols, 3 * channels), BF16)

    def place(frame, value):
        alive = (tm * frames + frame < frame_total).astype(F32)
        value = value.astype(F32) * (mask_ref[...] * alive)
        back_cat[frame, 0] = blank
        back_cat[frame, rows + 1] = blank
        lay_out(back_cat, frame, value, rows, cols, first_ref[...], last_ref[...])
        return value

    loads[1].wait()

    def own_grad(f, _):
        value = place(f, cot_ref[f])
        grad_ref[pl.ds(pl.multiple_of(f * places, places), places)] = value.astype(BF16)
        return 0

    lax.fori_loop(0, frames, own_grad, 0)

    def convolve(source, factor, f, back):
        total = jnp.zeros((places, channels), F32)
        for d in range(3):
            for r in range(3):
                at = (f + 2 - d, 2 - r) if back else (f + d, r)
                lines = source[at[0], at[1] : at[1] + rows].reshape(places, 3 * channels)
                total = total + jnp.dot(lines, factor[3 * d + r], preferred_element_type=F32)
        return total * (mask_ref[...] * (tm * frames + f < frame_total).astype(F32))

    def back_sweep(f, _):
        agrad_ref[f] = convolve(back_cat, turned_ref, f, True)
        return 0

    lax.fori_loop(0, frames - 2, back_sweep, 0)

    for copy in stats_shares:
        copy.wait()
    counts = [(len_ref[0, i] * area).astype(F32) for i in range(slabs)]
    mean = jnp.zeros((1, channels), F32)
    for i in range(slabs):
        mean = mean + counts[i] * stats_ref[i, 0:1]
    mean = mean / count
    squares = jnp.zeros((1, channels), F32)
    for i in range(slabs):
        apart = stats_ref[i, 0:1] - mean
        squares = squares + stats_ref[i, 1:2] + counts[i] * (apart * apart)
    root = lax.rsqrt(squares / count + EPSILON)
    gain, bias = gain_ref[...], bias_ref[...]

    def activate(slot, frame_id, value):
        alive = ((frame_id >= 0) & (frame_id < frame_total)).astype(F32)
        live = mask_ref[...] * alive
        normed = (value.astype(F32) * live - mean) * live * root
        pre = normed * gain + bias
        gate = 1.0 / (1.0 + jnp.exp(-pre))
        act = (pre * gate * live).astype(BF16).astype(F32)
        cat_ref[slot, 0] = blank
        cat_ref[slot, rows + 1] = blank
        lay_out(cat_ref, slot, act, rows, cols, first_ref[...], last_ref[...])
        return normed

    @pl.when(has_before)
    def _():
        tails.wait_recv()

    for k in range(2):
        frame_id = tm * frames + k - 2
        offset = frame_id - own_start
        usable = (offset >= 0) & (offset < own_length)
        picked = jnp.where(usable, loaded_ref[jnp.clip(offset, 0, frames - 1)], tail_ref[k])
        activate(k, frame_id, picked)

    def own_frame(f, _):
        @pl.when(has_after)
        def _():
            moved(f).wait_recv()

        frame_id = tm * frames + f
        offset = frame_id - own_start
        picked = jnp.where(
            offset < own_length,
            loaded_ref[jnp.clip(offset, 0, frames - 1)],
            arrived_ref[f],
        )
        normed_ref[f] = activate(f + 2, frame_id, picked)
        return 0

    def through(f, sums):
        normed = normed_ref[f]
        pre = normed * gain + bias
        gate = 1.0 / (1.0 + jnp.exp(-pre))
        pre_grad = agrad_ref[f] * gate * (1.0 + pre * (1.0 - gate))
        agrad_ref[f] = pre_grad * gain
        return sums[0] + fold(pre_grad * normed), sums[1] + fold(pre_grad)

    order = [(k % 3, (k + 1) % 3, (k + 2) % 3) for k in range(3)]
    own_lanes = pl.ds(pl.multiple_of(core * lanes, lanes), lanes)

    def spread_out(stage, k, axis, source, target):
        row_of = []
        for off in (1, 2, 3):
            there, peer = along(axis, off)
            row_of.append(
                send(
                    source(there), target(off - 1),
                    send_sem.at[stage, k, off - 1], recv_sem.at[stage, k, off - 1], peer,
                )
            )
        return row_of

    def product(k, r, begin, end):
        lines = cat_ref[k + begin : k + end, r : r + rows].reshape(-1, 3 * channels)
        both = lax.dot_general(
            lines,
            grad_ref[begin * places : end * places],
            (((0,), (0,)), ((), ())),
            preferred_element_type=F32,
        ).reshape(per_row, 16, channels)
        low, high = both[..., :lanes], both[..., lanes:]
        return jnp.where(core == 0, low, high), jnp.where(core == 0, high, low)

    def early_part(k):
        for r in range(3):
            at = slice(r * per_row, (r + 1) * per_row)
            own_part[k, at], far_sum[k, at] = product(k, r, 0, early)

    def kernel_part(k):
        for r in range(3):
            at = slice(r * per_row, (r + 1) * per_row)
            own, far = product(k, r, early, frames)
            own_part[k, at] = own_part[k, at] + own
            far_part[k, at] = (far_sum[k, at] + far).astype(BF16)
        return send(
            far_part.at[k], core_in.at[k], send_sem.at[0, k, 0], recv_sem.at[0, k, 0], other
        )

    def first_stage(k, half):
        half.wait()

        def add_half(b, _):
            at = pl.ds(b * 4, 4)
            both = own_part[k, at] + core_in[k, at].astype(F32)
            own_part[k, at] = both
            send1[k, at] = both.astype(BF16)
            return 0

        lax.fori_loop(0, blocks // 4, add_half, 0)
        return spread_out(
            1, k, order[k][0],
            lambda there: send1.at[k, pl.ds(there * part, part)],
            lambda i: in1.at[k, i],
        )

    def second_stage(k, copies):
        for copy in copies:
            copy.wait()
        base = here[order[k][0]] * part

        def add_first(b, _):
            at = pl.ds(b * 3, 3)
            own = own_part[k, pl.ds(base + b * 3, 3)]
            for i in range(3):
                own = own + in1[k, i, at].astype(F32)
            send2[k, at] = own.astype(BF16)
            return 0

        lax.fori_loop(0, part // 3, add_first, 0)
        return spread_out(
            2, k, order[k][1],
            lambda there: send2.at[k, pl.ds(there * piece, piece)],
            lambda i: in2.at[k, i],
        )

    def third_stage(k, copies):
        for copy in copies:
            copy.wait()
        base = here[order[k][1]] * piece
        spot = here[order[k][2]]

        def add_second(b, _):
            at = pl.ds(b * 3, 3)
            own = send2[k, pl.ds(base + b * 3, 3)].astype(F32)
            for i in range(3):
                own = own + in2[k, i, at].astype(F32)
            in3[k, spot, at] = own.astype(BF16)
            return 0

        lax.fori_loop(0, piece // 3, add_second, 0)
        return spread_out(
            3, k, order[k][2], lambda there: in3.at[k, spot], lambda i: in3.at[k, spot]
        )

    def fourth_stage(k, copies):
        for copy in copies:
            copy.wait()
        base = here[order[k][0]] * part + here[order[k][1]] * piece

        def add_third(b, _):
            at = pl.ds(b * 3, 3)
            own = in3[k, 0, at].astype(F32)
            for i in range(1, 4):
                own = own + in3[k, i, at].astype(F32)
            total_ref[k, pl.ds(base + b * 3, 3), :, own_lanes] = own.astype(BF16)
            return 0

        lax.fori_loop(0, piece // 3, add_third, 0)
        spot = total_ref.at[k, pl.ds(base, piece), :, own_lanes]
        return spread_out(4, k, order[k][1], lambda there: spot, lambda i: spot)

    def region(k, there):
        return total_ref.at[k, pl.ds(there * part, part), :, own_lanes]

    def to_core(k, there, i):
        spot = region(k, there)
        return send(spot, spot, send_sem.at[6, k, i], recv_sem.at[6, k, i], other)

    def fifth_stage(k, copies):
        for copy in copies:
            copy.wait()
        mine = here[order[k][0]]
        row_of = spread_out(
            5, k, order[k][0], lambda there: region(k, mine), lambda i: region(k, mine)
        )
        return row_of, [to_core(k, mine, 0)]

    def sixth_stage(k, off, copies):
        copies[0][off - 1].wait()
        copies[1].append(to_core(k, (here[order[k][0]] + 4 - off) % 4, off))

    def forward_sweep(f, _):
        encoded_ref[f] = convolve(cat_ref, weight_ref, f, False).astype(BF16)
        return 0

    def take_in(f, _):
        own_frame(f, 0)
        forward_sweep(f, 0)
        return 0

    lax.fori_loop(0, early, take_in, 0)
    for k in range(3):
        early_part(k)
    lax.fori_loop(early, frames, own_frame, 0)

    half0 = kernel_part(0)
    half1 = kernel_part(1)
    stage0 = first_stage(0, half0)
    half2 = kernel_part(2)
    stage1 = first_stage(1, half1)
    lax.fori_loop(early, frames, forward_sweep, 0)
    encoded_copy = pltpu.make_async_copy(encoded_ref, encoded_hbm, local_sem.at[3])
    encoded_copy.start()
    stage2 = first_stage(2, half2)

    @pl.when(has_after)
    def _():
        halo.wait_recv()

    for k in range(2):
        place(frames + k, next_ref[k])
    lax.fori_loop(frames - 2, frames, back_sweep, 0)
    gain_sum, bias_sum = lax.fori_loop(0, frames, through, (zero, zero))
    sums_ref[...] = jnp.where(
        row == 0,
        jnp.sum(gain_sum, axis=0, keepdims=True),
        jnp.where(row == 1, jnp.sum(bias_sum, axis=0, keepdims=True), 0.0),
    )
    slabs_ref[tm] = sums_ref[...]
    shares = [
        send(sums_ref, slabs_ref.at[tm], pair_send.at[i], pair_recv.at[i], peer)
        for i, peer in enumerate(tm_peers)
    ]

    stage0 = second_stage(0, stage0)
    stage1 = second_stage(1, stage1)
    for copy in shares:
        copy.wait()
    total = slabs_ref[0]
    for i in range(1, slabs):
        total = total + slabs_ref[i]
    tm_total[...] = total
    core_copy = send(tm_total, core_sum, pair_send.at[7], pair_recv.at[7], other)
    stage0 = third_stage(0, stage0)
    stage2 = second_stage(2, stage2)
    stage1 = third_stage(1, stage1)

    core_copy.wait()
    x_sums[x] = tm_total[...] + core_sum[...]
    x_copies = [
        send(x_sums.at[x], x_sums.at[x], pair_send.at[7 + off], pair_recv.at[7 + off], along(0, off)[1])
        for off in (1, 2, 3)
    ]
    shares_of = group_sum(tm_total[...] * gain, width) / count
    mean_part, along_part = shares_of[1:2], shares_of[0:1]

    def finish(f, _):
        live = mask_ref[...] * (tm * frames + f < frame_total).astype(F32)
        inner = agrad_ref[f] - mean_part - normed_ref[f] * along_part
        igrad_ref[f] = (inner * root * live).astype(BF16)
        return 0

    lax.fori_loop(0, frames // 2, finish, 0)
    stage0 = fourth_stage(0, stage0)
    stage2 = third_stage(2, stage2)
    lax.fori_loop(frames // 2, frames, finish, 0)
    igrad_copy = pltpu.make_async_copy(igrad_ref, igrad_hbm, local_sem.at[4])
    igrad_copy.start()

    stage1 = fourth_stage(1, stage1)
    for copy in x_copies:
        copy.wait()
    x_total[...] = x_sums[0] + x_sums[1] + x_sums[2] + x_sums[3]
    z_copy = send(x_total, z_sum, pair_send.at[11], pair_recv.at[11], across)
    stage0 = fifth_stage(0, stage0)
    stage2 = fourth_stage(2, stage2)
    stage1 = fifth_stage(1, stage1)
    z_copy.wait()
    pair_ref[...] = x_total[...] + z_sum[...]
    stage2 = fifth_stage(2, stage2)
    ends = (stage0, stage1, stage2)
    for off in (1, 3, 2):
        for k in range(3):
            sixth_stage(k, off, ends[k])
    outs = []
    for k in range(3):
        for copy in ends[k][1]:
            copy.wait()
        out = pltpu.make_async_copy(total_ref.at[k], total_hbm.at[k], local_sem.at[5 + k])
        out.start()
        outs.append(out)
    encoded_copy.wait()
    igrad_copy.wait()

    @pl.when(has_before)
    def _():
        for f in range(frames):
            moved(f).wait_send()
        halo.wait_send()

    @pl.when(has_after)
    def _():
        tails.wait_send()

    for out in outs:
        out.wait()


def last_kernel(
    scale, encoded_in, igrad_in, total_ref, pair_in,
    encoded_out, igrad_out, kernel_ref, gain_ref, bias_ref, sem,
):
    step, steps = pl.program_id(0), pl.num_programs(0)
    copies = [
        pltpu.make_async_copy(encoded_in, encoded_out, sem.at[0]),
        pltpu.make_async_copy(igrad_in, igrad_out, sem.at[1]),
    ]

    @pl.when(step == 0)
    def _():
        for copy in copies:
            copy.start()
        gain_ref[...] = pair_in[0:1] * scale
        bias_ref[...] = pair_in[1:2] * scale

    kernel_ref[...] = total_ref[...].astype(F32) * scale

    @pl.when(step == steps - 1)
    def _():
        for copy in copies:
            copy.wait()


def body(loaded, lengths, resolution, weight, norm_gain, norm_bias, cotangent):
    frames, rows, cols, channels = loaded.shape[1:]
    places, width, lanes = rows * cols, channels // GROUPS, channels // 2
    slabs = lax.axis_size("tm")
    shape = jax.ShapeDtypeStruct
    slab = (frames, places, channels)
    blocks = 9 * channels // 16
    part, piece = blocks // 4, blocks // 16

    def tiles(*lead, kind=BF16):
        return pltpu.VMEM(lead + (16, lanes), kind)

    small = pltpu.VMEM((8, channels), F32)
    plane = pltpu.VMEM((places, channels), F32)
    cat = pltpu.VMEM((frames + 2, rows + 2, cols, 3 * channels), BF16)
    dma = pltpu.SemaphoreType.DMA
    encoded, igrad, total, pair = pl.pallas_call(
        functools.partial(section_kernel, rows, cols, width),
        out_shape=(
            shape(slab, BF16),
            shape(slab, BF16),
            shape((3, blocks, 16, channels), BF16),
            shape((8, channels), F32),
        ),
        in_specs=[SMEM, SMEM, ANY, ANY, ANY, VMEM, VMEM],
        out_specs=(ANY, ANY, ANY, VMEM),
        scratch_shapes=[
            pltpu.VMEM(slab, BF16),
            pltpu.VMEM(slab, BF16),
            pltpu.VMEM(slab, BF16),
            pltpu.VMEM(slab, BF16),
            pltpu.VMEM((2, places, channels), BF16),
            pltpu.VMEM((2, places, channels), BF16),
            pltpu.VMEM((2, places, channels), BF16),
            pltpu.VMEM((9, 3 * channels, channels), BF16),
            pltpu.VMEM((9, 3 * channels, channels), BF16),
            cat,
            cat,
            pltpu.VMEM((frames * places, channels), BF16),
            pltpu.VMEM(slab, F32),
            pltpu.VMEM(slab, F32),
            pltpu.VMEM(slab, BF16),
            pltpu.VMEM(slab, BF16),
            plane,
            plane,
            plane,
            small,
            pltpu.VMEM((slabs, 8, channels), F32),
            small,
            pltpu.VMEM((slabs, 8, channels), F32),
            pltpu.VMEM((3, blocks, 16, channels), BF16),
            tiles(3, blocks, kind=F32),
            tiles(3, blocks, kind=F32),
            tiles(3, blocks),
            tiles(3, blocks),
            tiles(3, blocks),
            tiles(3, 3, part),
            tiles(3, part),
            tiles(3, 3, piece),
            tiles(3, 4, piece),
            small,
            small,
            pltpu.VMEM((4, 8, channels), F32),
            small,
            small,
            dma((8,)),
            dma((frames + 2,)),
            dma((frames + 2,)),
            dma((7,)),
            dma((7,)),
            dma((7, 3, 4)),
            dma((7, 3, 4)),
            dma((12,)),
            dma((12,)),
        ],
        compiler_params=params(58, collective_id=1, has_side_effects=True),
    )(
        lengths,
        resolution,
        loaded.reshape(slab),
        cotangent.reshape(slab),
        weight.reshape(9, 3 * channels, channels),
        norm_gain.reshape(1, channels),
        norm_bias.reshape(1, channels),
    )
    scale = 1.0 / math.sqrt(lax.axis_size("dp") * slabs * frames * places)
    taps = pl.BlockSpec((3, channels, channels), lambda i: (i, 0, 0))
    line = pl.BlockSpec((1, channels), lambda i: (0, 0))
    encoded, igrad, kernel, gain, bias = pl.pallas_call(
        functools.partial(last_kernel, scale),
        out_shape=(
            shape(slab, BF16),
            shape(slab, BF16),
            shape((27, channels, channels), F32),
            shape((1, channels), F32),
            shape((1, channels), F32),
        ),
        grid=(9,),
        in_specs=[ANY, ANY, taps, pl.BlockSpec((8, channels), lambda i: (0, 0))],
        out_specs=(ANY, ANY, taps, line, line),
        scratch_shapes=[dma((2,))],
        compiler_params=params(58),
    )(encoded, igrad, total.reshape(27, channels, channels), pair)
    whole = (1, frames, rows, cols, channels)
    return (
        encoded.reshape(whole),
        igrad.reshape(whole),
        kernel,
        gain.reshape(channels),
        bias.reshape(channels),
    )


def solution(mesh):
    slab = P("dp", "tm", None, None, None)
    return jax.shard_map(
        body,
        mesh=mesh,
        in_specs=(slab, P("dp", None), P("dp", None), P(), P(), P(), slab),
        out_specs=(slab, slab, P(), P(), P()),
        check_vma=False,
    )
```

```python
import functools
import math

import jax
import jax.numpy as jnp
from jax import lax
from jax.experimental import pallas as pl
from jax.experimental.pallas import tpu as pltpu
from jax.sharding import PartitionSpec as P

GROUPS = 32
EPSILON = 1e-05
LIMIT = 45
MESH = pl.DeviceIdType.MESH
F32 = jnp.float32
BF16 = jnp.bfloat16

VMEM = pl.BlockSpec(memory_space=pltpu.VMEM)
HBM = pl.BlockSpec(memory_space=pltpu.HBM)
SMEM = pl.BlockSpec(memory_space=pltpu.SMEM)


def params(limit, **others):
    return pltpu.CompilerParams(vmem_limit_bytes=limit << 20, **others)


def start_of(len_ref, slabs, index):
    total = jnp.int32(0)
    for i in range(slabs):
        total = total + jnp.where(i < index, len_ref[0, i], 0)
    return total


def length_of(len_ref, slabs, index):
    total = jnp.int32(0)
    for i in range(slabs):
        total = total + jnp.where(i == index, len_ref[0, i], 0)
    return total


def group_sum(rows, width):
    lanes = rows.shape[1]
    lane = lax.broadcasted_iota(jnp.int32, rows.shape, 1)
    step = 1
    while step < width:
        up = pltpu.roll(rows, lanes - step, 1)
        down = pltpu.roll(rows, step, 1)
        rows = rows + jnp.where((lane & step) == 0, up, down)
        step *= 2
    return rows


def cells(res_ref, cols, shape):
    place = lax.broadcasted_iota(jnp.int32, shape, 0)
    return ((place // cols) < res_ref[0, 0]) & ((place % cols) < res_ref[0, 1])


def lay_out(cat_ref, frame, value, rows, cols, first_col, last_col):
    places, channels = value.shape
    left = pltpu.roll(value, 1, 0) * first_col
    right = pltpu.roll(value, places - 1, 0) * last_col
    for k, part in enumerate((left, value, right)):
        cat_ref[frame, 1 : rows + 1, :, k * channels : (k + 1) * channels] = (
            part.astype(BF16).reshape(rows, cols, channels)
        )


def col_masks(cols, shape):
    place = lax.broadcasted_iota(jnp.int32, shape, 0) % cols
    return (place != 0).astype(F32), (place != cols - 1).astype(F32)


def section_kernel(
    rows, cols, width,
    len_ref, res_ref, loaded_ref, cot_ref, weight_hbm, gain_ref, bias_ref,
    encoded_ref, igrad_ref, total_ref, pair_ref,
    arrived_ref, next_ref, tail_out, tail_ref, weight_ref, turned_ref,
    back_cat, cat_ref, grad_ref, agrad_ref, normed_ref,
    mask_ref, first_ref, last_ref, stats_out, stats_ref, sums_ref, slabs_ref,
    own_part, far_sum, far_part, core_in, send1, in1, send2, in2, in3,
    tm_total, core_sum, x_sums, x_total, z_sum,
    local_sem, move_send, move_recv, stat_send, stat_recv,
    send_sem, recv_sem, pair_send, pair_recv,
):
    frames, places, channels = loaded_ref.shape
    blocks = own_part.shape[1]
    part, piece, lanes = blocks // 4, blocks // 16, channels // 2
    per_row = blocks // 3
    early = frames - 2
    slabs = 8

    dp, tm = lax.axis_index("dp"), lax.axis_index("tm")
    core, x, y = dp % 2, dp // 4, tm % 4
    z = (dp // 2) % 2 * 2 + tm // 4
    here = (x, y, z)

    def device(place, its_core):
        return ((place[0] * 2 + place[2] // 2) * 2 + its_core, (place[2] % 2) * 4 + place[1])

    def along(axis, off):
        place = list(here)
        place[axis] = (here[axis] + off) % 4
        return place[axis], device(place, core)

    other = device(here, 1 - core)
    across = device((x, y, (z + 2) % 4), core)
    tm_peers = [(dp, (tm + off) % slabs) for off in range(1, slabs)]
    axis_peers = [along(axis, off)[1] for axis in (0, 1, 2) for off in (1, 2, 3)]
    before, after = (dp, (tm + slabs - 1) % slabs), (dp, (tm + 1) % slabs)
    has_before, has_after = tm > 0, tm < slabs - 1

    barrier = pltpu.get_barrier_semaphore()
    greeted = [other] + axis_peers + tm_peers
    for peer in greeted:
        pl.semaphore_signal(barrier, inc=1, device_id=peer, device_id_type=MESH)

    load = pltpu.make_async_copy(weight_hbm, weight_ref, local_sem)
    load.start()

    def remote(src, dst, send_at, recv_at, peer):
        return pltpu.make_async_remote_copy(
            src_ref=src, dst_ref=dst, send_sem=send_at, recv_sem=recv_at,
            device_id=peer, device_id_type=MESH,
        )

    def send(*arguments):
        copy = remote(*arguments)
        copy.start()
        return copy

    halo = remote(
        cot_ref.at[pl.ds(0, 2)], next_ref, move_send.at[frames], move_recv.at[frames], before
    )
    tails = remote(
        tail_out, tail_ref, move_send.at[frames + 1], move_recv.at[frames + 1], after
    )

    def moved(f):
        return remote(
            igrad_ref.at[f], arrived_ref.at[f], move_send.at[f], move_recv.at[f], before
        )

    @pl.when(tm == slabs - 1)
    def _():
        next_ref[...] = jnp.zeros_like(next_ref)
        arrived_ref[...] = jnp.zeros_like(arrived_ref)

    @pl.when(tm == 0)
    def _():
        tail_ref[...] = jnp.zeros_like(tail_ref)

    own_start, own_length = start_of(len_ref, slabs, tm), length_of(len_ref, slabs, tm)
    frame_total = start_of(len_ref, slabs, slabs)
    area = res_ref[0, 0] * res_ref[0, 1] * width
    count = (frame_total * area).astype(F32)
    mask_ref[...] = cells(res_ref, cols, (places, channels)).astype(F32)
    first, last = col_masks(cols, (places, channels))
    first_ref[...] = first
    last_ref[...] = last
    zero = jnp.zeros((8, channels), F32)
    row = lax.broadcasted_iota(jnp.int32, (8, channels), 0)


    def fold(value):
        return jnp.sum(value.reshape(places // 8, 8, channels), axis=0)

    def over_groups(total):
        line = jnp.sum(total, axis=0, keepdims=True)
        return group_sum(jnp.broadcast_to(line, (8, channels)), width)

    def add_up(f, total):
        held = (f < own_length).astype(F32)
        return total + fold(loaded_ref[f].astype(F32) * (mask_ref[...] * held))

    own_mean = over_groups(lax.fori_loop(0, frames, add_up, zero)) / (own_length * area).astype(F32)
    mean_row = own_mean[0:1]

    def spread(f, total):
        held = (f < own_length).astype(F32)
        apart = (loaded_ref[f].astype(F32) - mean_row) * (mask_ref[...] * held)
        return total + fold(apart * apart)

    squares = over_groups(lax.fori_loop(0, frames, spread, zero))
    stats_out[...] = jnp.where(row == 0, own_mean, squares)
    stats_ref[tm] = stats_out[...]
    for k in range(2):
        offset = tm * frames + frames - 2 + k - own_start
        usable = (offset >= 0) & (offset < own_length)
        picked = loaded_ref[jnp.clip(offset, 0, frames - 1)]
        tail_out[k] = jnp.where(usable, picked, jnp.zeros_like(picked))


    def pack(f, _):
        offset = (tm - 1) * frames + f - own_start
        usable = (offset >= 0) & (offset < own_length)
        picked = loaded_ref[jnp.clip(offset, 0, frames - 1)]
        igrad_ref[f] = jnp.where(usable, picked, jnp.zeros_like(picked))
        return 0

    lax.fori_loop(0, frames, pack, 0)

    pl.semaphore_wait(barrier, len(greeted))
    stats_shares = [
        send(stats_out, stats_ref.at[tm], stat_send.at[i], stat_recv.at[i], peer)
        for i, peer in enumerate(tm_peers)
    ]

    @pl.when(has_after)
    def _():
        tails.start()

    @pl.when(has_before)
    def _():
        moved(0).start()

    load.wait()

    def turn(block, _):
        for k in range(3):
            turned_ref[block, k * channels : (k + 1) * channels, :] = weight_ref[
                block, (2 - k) * channels : (3 - k) * channels, :
            ].T
        return 0

    lax.fori_loop(0, 9, turn, 0)
    blank = jnp.zeros((cols, 3 * channels), BF16)

    def place(frame, value):
        alive = (tm * frames + frame < frame_total).astype(F32)
        value = value.astype(F32) * (mask_ref[...] * alive)
        back_cat[frame, 0] = blank
        back_cat[frame, rows + 1] = blank
        lay_out(back_cat, frame, value, rows, cols, first_ref[...], last_ref[...])
        return value


    def own_grad(f, _):
        value = place(f, cot_ref[f])
        grad_ref[pl.ds(pl.multiple_of(f * places, places), places)] = value.astype(BF16)
        return 0

    lax.fori_loop(0, frames, own_grad, 0)

    def convolve(source, factor, f, back):
        total = jnp.zeros((places, channels), F32)
        for d in range(3):
            for r in range(3):
                at = (f + 2 - d, 2 - r) if back else (f + d, r)
                lines = source[at[0], at[1] : at[1] + rows].reshape(places, 3 * channels)
                total = total + jnp.dot(lines, factor[3 * d + r], preferred_element_type=F32)
        return total * (mask_ref[...] * (tm * frames + f < frame_total).astype(F32))

    def back_sweep(f, _):
        agrad_ref[f] = convolve(back_cat, turned_ref, f, True)
        return 0

    for copy in stats_shares:
        copy.wait()

    @pl.when(has_before)
    def _():
        for f in range(1, frames):
            moved(f).start()
        halo.start()

    lax.fori_loop(0, frames - 2, back_sweep, 0)

    counts = [(len_ref[0, i] * area).astype(F32) for i in range(slabs)]
    mean = jnp.zeros((1, channels), F32)
    for i in range(slabs):
        mean = mean + counts[i] * stats_ref[i, 0:1]
    mean = mean / count
    squares = jnp.zeros((1, channels), F32)
    for i in range(slabs):
        apart = stats_ref[i, 0:1] - mean
        squares = squares + stats_ref[i, 1:2] + counts[i] * (apart * apart)
    root = lax.rsqrt(squares / count + EPSILON)
    gain, bias = gain_ref[...], bias_ref[...]

    def activate(slot, frame_id, value):
        alive = ((frame_id >= 0) & (frame_id < frame_total)).astype(F32)
        live = mask_ref[...] * alive
        normed = (value.astype(F32) * live - mean) * live * root
        pre = normed * gain + bias
        gate = 1.0 / (1.0 + jnp.exp(-pre))
        act = (pre * gate * live).astype(BF16).astype(F32)
        cat_ref[slot, 0] = blank
        cat_ref[slot, rows + 1] = blank
        lay_out(cat_ref, slot, act, rows, cols, first_ref[...], last_ref[...])
        return normed

    @pl.when(has_before)
    def _():
        tails.wait_recv()

    for k in range(2):
        frame_id = tm * frames + k - 2
        offset = frame_id - own_start
        usable = (offset >= 0) & (offset < own_length)
        picked = jnp.where(usable, loaded_ref[jnp.clip(offset, 0, frames - 1)], tail_ref[k])
        activate(k, frame_id, picked)

    def own_frame(f, _):
        @pl.when(has_after)
        def _():
            moved(f).wait_recv()

        frame_id = tm * frames + f
        offset = frame_id - own_start
        picked = jnp.where(
            offset < own_length,
            loaded_ref[jnp.clip(offset, 0, frames - 1)],
            arrived_ref[f],
        )
        normed_ref[f] = activate(f + 2, frame_id, picked)
        return 0

    def through(f, sums):
        normed = normed_ref[f]
        pre = normed * gain + bias
        gate = 1.0 / (1.0 + jnp.exp(-pre))
        pre_grad = agrad_ref[f] * gate * (1.0 + pre * (1.0 - gate))
        agrad_ref[f] = pre_grad * gain
        return sums[0] + fold(pre_grad * normed), sums[1] + fold(pre_grad)

    order = [(k % 3, (k + 1) % 3, (k + 2) % 3) for k in range(3)]
    own_lanes = pl.ds(pl.multiple_of(core * lanes, lanes), lanes)

    def spread_out(stage, k, axis, source, target):
        row_of = []
        for off in (1, 2, 3):
            there, peer = along(axis, off)
            row_of.append(
                send(
                    source(there), target(off - 1),
                    send_sem.at[stage, k, off - 1], recv_sem.at[stage, k, off - 1], peer,
                )
            )
        return row_of

    def product(k, r, begin, end):
        lines = cat_ref[k + begin : k + end, r : r + rows].reshape(-1, 3 * channels)
        both = lax.dot_general(
            lines,
            grad_ref[begin * places : end * places],
            (((0,), (0,)), ((), ())),
            preferred_element_type=F32,
        ).reshape(per_row, 16, channels)
        low, high = both[..., :lanes], both[..., lanes:]
        return jnp.where(core == 0, low, high), jnp.where(core == 0, high, low)

    def early_part(k):
        for r in range(3):
            at = slice(r * per_row, (r + 1) * per_row)
            own_part[k, at], far_sum[k, at] = product(k, r, 0, early)

    def kernel_part(k):
        for r in range(3):
            at = slice(r * per_row, (r + 1) * per_row)
            own, far = product(k, r, early, frames)
            own_part[k, at] = own_part[k, at] + own
            far_part[k, at] = (far_sum[k, at] + far).astype(BF16)
        return send(
            far_part.at[k], core_in.at[k], send_sem.at[0, k, 0], recv_sem.at[0, k, 0], other
        )

    def first_stage(k, half):
        half.wait()

        def add_half(b, _):
            at = pl.ds(b * 4, 4)
            both = own_part[k, at] + core_in[k, at].astype(F32)
            own_part[k, at] = both
            send1[k, at] = both.astype(BF16)
            return 0

        lax.fori_loop(0, blocks // 4, add_half, 0)
        return spread_out(
            1, k, order[k][0],
            lambda there: send1.at[k, pl.ds(there * part, part)],
            lambda i: in1.at[k, i],
        )

    def second_stage(k, copies):
        for copy in copies:
            copy.wait()
        base = here[order[k][0]] * part

        def add_first(b, _):
            at = pl.ds(b * 3, 3)
            own = own_part[k, pl.ds(base + b * 3, 3)]
            for i in range(3):
                own = own + in1[k, i, at].astype(F32)
            send2[k, at] = own.astype(BF16)
            return 0

        lax.fori_loop(0, part // 3, add_first, 0)
        return spread_out(
            2, k, order[k][1],
            lambda there: send2.at[k, pl.ds(there * piece, piece)],
            lambda i: in2.at[k, i],
        )

    def third_stage(k, copies):
        for copy in copies:
            copy.wait()
        base = here[order[k][1]] * piece
        spot = here[order[k][2]]

        def add_second(b, _):
            at = pl.ds(b * 3, 3)
            own = send2[k, pl.ds(base + b * 3, 3)].astype(F32)
            for i in range(3):
                own = own + in2[k, i, at].astype(F32)
            in3[k, spot, at] = own.astype(BF16)
            return 0

        lax.fori_loop(0, piece // 3, add_second, 0)
        return spread_out(
            3, k, order[k][2], lambda there: in3.at[k, spot], lambda i: in3.at[k, spot]
        )

    def fourth_stage(k, copies):
        for copy in copies:
            copy.wait()
        base = here[order[k][0]] * part + here[order[k][1]] * piece

        def add_third(b, _):
            at = pl.ds(b * 3, 3)
            own = in3[k, 0, at].astype(F32)
            for i in range(1, 4):
                own = own + in3[k, i, at].astype(F32)
            total_ref[k, pl.ds(base + b * 3, 3), :, own_lanes] = own.astype(BF16)
            return 0

        lax.fori_loop(0, piece // 3, add_third, 0)
        spot = total_ref.at[k, pl.ds(base, piece), :, own_lanes]
        return spread_out(4, k, order[k][1], lambda there: spot, lambda i: spot)

    def region(k, there):
        return total_ref.at[k, pl.ds(there * part, part), :, own_lanes]

    def to_core(k, there, i):
        spot = region(k, there)
        return send(spot, spot, send_sem.at[6, k, i], recv_sem.at[6, k, i], other)

    def fifth_stage(k, copies):
        for copy in copies:
            copy.wait()
        mine = here[order[k][0]]
        row_of = spread_out(
            5, k, order[k][0], lambda there: region(k, mine), lambda i: region(k, mine)
        )
        return row_of, [to_core(k, mine, 0)]

    def sixth_stage(k, off, copies):
        copies[0][off - 1].wait()
        copies[1].append(to_core(k, (here[order[k][0]] + 4 - off) % 4, off))

    def forward_sweep(f, _):
        encoded_ref[f] = convolve(cat_ref, weight_ref, f, False).astype(BF16)
        return 0

    def take_in(f, _):
        own_frame(f, 0)
        forward_sweep(f, 0)
        return 0

    lax.fori_loop(0, early, take_in, 0)
    for k in range(3):
        early_part(k)
    lax.fori_loop(early, frames, own_frame, 0)

    half0 = kernel_part(0)
    half1 = kernel_part(1)
    stage0 = first_stage(0, half0)
    half2 = kernel_part(2)
    stage1 = first_stage(1, half1)
    lax.fori_loop(early, frames, forward_sweep, 0)
    stage2 = first_stage(2, half2)

    @pl.when(has_after)
    def _():
        halo.wait_recv()

    for k in range(2):
        place(frames + k, next_ref[k])
    lax.fori_loop(frames - 2, frames, back_sweep, 0)
    gain_sum, bias_sum = lax.fori_loop(0, frames, through, (zero, zero))
    sums_ref[...] = jnp.where(
        row == 0,
        jnp.sum(gain_sum, axis=0, keepdims=True),
        jnp.where(row == 1, jnp.sum(bias_sum, axis=0, keepdims=True), 0.0),
    )
    slabs_ref[tm] = sums_ref[...]
    shares = [
        send(sums_ref, slabs_ref.at[tm], pair_send.at[i], pair_recv.at[i], peer)
        for i, peer in enumerate(tm_peers)
    ]

    stage0 = second_stage(0, stage0)
    stage1 = second_stage(1, stage1)
    for copy in shares:
        copy.wait()
    total = slabs_ref[0]
    for i in range(1, slabs):
        total = total + slabs_ref[i]
    tm_total[...] = total
    core_copy = send(tm_total, core_sum, pair_send.at[7], pair_recv.at[7], other)
    stage0 = third_stage(0, stage0)
    stage2 = second_stage(2, stage2)
    stage1 = third_stage(1, stage1)

    core_copy.wait()
    x_sums[x] = tm_total[...] + core_sum[...]
    x_copies = [
        send(x_sums.at[x], x_sums.at[x], pair_send.at[7 + off], pair_recv.at[7 + off], along(0, off)[1])
        for off in (1, 2, 3)
    ]
    shares_of = group_sum(tm_total[...] * gain, width) / count
    mean_part, along_part = shares_of[1:2], shares_of[0:1]

    @pl.when(has_before)
    def _():
        for f in range(frames):
            moved(f).wait_send()

    def finish(f, _):
        live = mask_ref[...] * (tm * frames + f < frame_total).astype(F32)
        inner = agrad_ref[f] - mean_part - normed_ref[f] * along_part
        igrad_ref[f] = (inner * root * live).astype(BF16)
        return 0

    lax.fori_loop(0, frames // 2, finish, 0)
    stage0 = fourth_stage(0, stage0)
    stage2 = third_stage(2, stage2)
    lax.fori_loop(frames // 2, frames, finish, 0)

    stage1 = fourth_stage(1, stage1)
    for copy in x_copies:
        copy.wait()
    x_total[...] = x_sums[0] + x_sums[1] + x_sums[2] + x_sums[3]
    z_copy = send(x_total, z_sum, pair_send.at[11], pair_recv.at[11], across)
    stage0 = fifth_stage(0, stage0)
    stage2 = fourth_stage(2, stage2)
    stage1 = fifth_stage(1, stage1)
    z_copy.wait()
    pair_ref[...] = x_total[...] + z_sum[...]
    stage2 = fifth_stage(2, stage2)
    ends = (stage0, stage1, stage2)
    for off in (1, 3, 2):
        for k in range(3):
            sixth_stage(k, off, ends[k])
    for k in range(3):
        for copy in ends[k][1]:
            copy.wait()

    @pl.when(has_before)
    def _():
        halo.wait_send()

    @pl.when(has_after)
    def _():
        tails.wait_send()


def body(loaded, lengths, resolution, weight, norm_gain, norm_bias, cotangent):
    frames, rows, cols, channels = loaded.shape[1:]
    places, width, lanes = rows * cols, channels // GROUPS, channels // 2
    slabs = lax.axis_size("tm")
    shape = jax.ShapeDtypeStruct
    slab = (frames, places, channels)
    blocks = 9 * channels // 16
    part, piece = blocks // 4, blocks // 16

    def tiles(*lead, kind=BF16):
        return pltpu.VMEM(lead + (16, lanes), kind)

    small = pltpu.VMEM((8, channels), F32)
    plane = pltpu.VMEM((places, channels), F32)
    cat = pltpu.VMEM((frames + 2, rows + 2, cols, 3 * channels), BF16)
    dma = pltpu.SemaphoreType.DMA
    encoded, igrad, total, pair = pl.pallas_call(
        functools.partial(section_kernel, rows, cols, width),
        out_shape=(
            shape(slab, BF16),
            shape(slab, BF16),
            shape((3, blocks, 16, channels), BF16),
            shape((8, channels), F32),
        ),
        in_specs=[SMEM, SMEM, VMEM, VMEM, HBM, VMEM, VMEM],
        out_specs=(VMEM,) * 4,
        scratch_shapes=[
            pltpu.VMEM(slab, BF16),
            pltpu.VMEM((2, places, channels), BF16),
            pltpu.VMEM((2, places, channels), BF16),
            pltpu.VMEM((2, places, channels), BF16),
            pltpu.VMEM((9, 3 * channels, channels), BF16),
            pltpu.VMEM((9, 3 * channels, channels), BF16),
            cat,
            cat,
            pltpu.VMEM((frames * places, channels), BF16),
            pltpu.VMEM(slab, F32),
            pltpu.VMEM(slab, F32),
            plane,
            plane,
            plane,
            small,
            pltpu.VMEM((slabs, 8, channels), F32),
            small,
            pltpu.VMEM((slabs, 8, channels), F32),
            tiles(3, blocks, kind=F32),
            tiles(3, blocks, kind=F32),
            tiles(3, blocks),
            tiles(3, blocks),
            tiles(3, blocks),
            tiles(3, 3, part),
            tiles(3, part),
            tiles(3, 3, piece),
            tiles(3, 4, piece),
            small,
            small,
            pltpu.VMEM((4, 8, channels), F32),
            small,
            small,
            dma,
            dma((frames + 2,)),
            dma((frames + 2,)),
            dma((7,)),
            dma((7,)),
            dma((7, 3, 4)),
            dma((7, 3, 4)),
            dma((12,)),
            dma((12,)),
        ],
        compiler_params=params(LIMIT, collective_id=1, has_side_effects=True),
    )(
        lengths,
        resolution,
        loaded.reshape(slab),
        cotangent.reshape(slab),
        weight.reshape(9, 3 * channels, channels),
        norm_gain.reshape(1, channels),
        norm_bias.reshape(1, channels),
    )
    scale = 1.0 / math.sqrt(lax.axis_size("dp") * slabs * frames * places)
    whole = (1, frames, rows, cols, channels)
    return (
        encoded.reshape(whole),
        igrad.reshape(whole),
        total.reshape(27, channels, channels).astype(F32) * scale,
        pair[0] * scale,
        pair[1] * scale,
    )


def solution(mesh):
    slab = P("dp", "tm", None, None, None)
    return jax.shard_map(
        body,
        mesh=mesh,
        in_specs=(slab, P("dp", None), P("dp", None), P(), P(), P(), slab),
        out_specs=(slab, slab, P(), P(), P()),
        check_vma=False,
    )
```

```python
import functools
import math

import jax
import jax.numpy as jnp
from jax import lax
from jax.experimental import pallas as pl
from jax.experimental.pallas import tpu as pltpu
from jax.sharding import PartitionSpec as P

GROUPS = 32
EPSILON = 1e-05
LIMIT = 45
MESH = pl.DeviceIdType.MESH
F32 = jnp.float32
BF16 = jnp.bfloat16

VMEM = pl.BlockSpec(memory_space=pltpu.VMEM)
HBM = pl.BlockSpec(memory_space=pltpu.HBM)
SMEM = pl.BlockSpec(memory_space=pltpu.SMEM)


def params(limit, **others):
    return pltpu.CompilerParams(vmem_limit_bytes=limit << 20, **others)


def start_of(len_ref, slabs, index):
    total = jnp.int32(0)
    for i in range(slabs):
        total = total + jnp.where(i < index, len_ref[0, i], 0)
    return total


def length_of(len_ref, slabs, index):
    total = jnp.int32(0)
    for i in range(slabs):
        total = total + jnp.where(i == index, len_ref[0, i], 0)
    return total


def group_sum(rows, width):
    lanes = rows.shape[1]
    lane = lax.broadcasted_iota(jnp.int32, rows.shape, 1)
    step = 1
    while step < width:
        up = pltpu.roll(rows, lanes - step, 1)
        down = pltpu.roll(rows, step, 1)
        rows = rows + jnp.where((lane & step) == 0, up, down)
        step *= 2
    return rows


def cells(res_ref, cols, shape):
    place = lax.broadcasted_iota(jnp.int32, shape, 0)
    return ((place // cols) < res_ref[0, 0]) & ((place % cols) < res_ref[0, 1])


def lay_out(cat_ref, frame, value, rows, cols, first_col, last_col):
    places, channels = value.shape
    left = pltpu.roll(value, 1, 0) * first_col
    right = pltpu.roll(value, places - 1, 0) * last_col
    for k, part in enumerate((left, value, right)):
        cat_ref[frame, 1 : rows + 1, :, k * channels : (k + 1) * channels] = (
            part.astype(BF16).reshape(rows, cols, channels)
        )


def col_masks(cols, shape):
    place = lax.broadcasted_iota(jnp.int32, shape, 0) % cols
    return (place != 0).astype(F32), (place != cols - 1).astype(F32)


def section_kernel(
    rows, cols, width,
    len_ref, res_ref, loaded_ref, cot_ref, weight_hbm, gain_ref, bias_ref,
    encoded_ref, igrad_ref, total_ref, pair_ref,
    arrived_ref, next_ref, tail_out, tail_ref, weight_ref, turned_ref,
    back_cat, cat_ref, grad_ref, agrad_ref, normed_ref,
    mask_ref, first_ref, last_ref, stats_out, stats_ref, sums_ref, slabs_ref,
    own_part, far_sum, far_part, core_in, send1, in1, send2, in2, in3,
    tm_total, core_sum, x_sums, x_total, z_sum,
    local_sem, move_send, move_recv, stat_send, stat_recv,
    send_sem, recv_sem, pair_send, pair_recv,
):
    frames, places, channels = loaded_ref.shape
    blocks = own_part.shape[1]
    part, piece, lanes = blocks // 4, blocks // 16, channels // 2
    per_row = blocks // 3
    early = frames - 2
    slabs = 8

    dp, tm = lax.axis_index("dp"), lax.axis_index("tm")
    core, x, y = dp % 2, dp // 4, tm % 4
    z = (dp // 2) % 2 * 2 + tm // 4
    here = (x, y, z)

    def device(place, its_core):
        return ((place[0] * 2 + place[2] // 2) * 2 + its_core, (place[2] % 2) * 4 + place[1])

    def along(axis, off):
        place = list(here)
        place[axis] = (here[axis] + off) % 4
        return place[axis], device(place, core)

    other = device(here, 1 - core)
    across = device((x, y, (z + 2) % 4), core)
    tm_peers = [(dp, (tm + off) % slabs) for off in range(1, slabs)]
    axis_peers = [along(axis, off)[1] for axis in (0, 1, 2) for off in (1, 2, 3)]
    before, after = (dp, (tm + slabs - 1) % slabs), (dp, (tm + 1) % slabs)
    has_before, has_after = tm > 0, tm < slabs - 1

    barrier = pltpu.get_barrier_semaphore()
    greeted = [other] + axis_peers + tm_peers
    for peer in greeted:
        pl.semaphore_signal(barrier, inc=1, device_id=peer, device_id_type=MESH)

    load = pltpu.make_async_copy(weight_hbm, weight_ref, local_sem)
    load.start()

    def remote(src, dst, send_at, recv_at, peer):
        return pltpu.make_async_remote_copy(
            src_ref=src, dst_ref=dst, send_sem=send_at, recv_sem=recv_at,
            device_id=peer, device_id_type=MESH,
        )

    def send(*arguments):
        copy = remote(*arguments)
        copy.start()
        return copy

    halo = remote(
        cot_ref.at[pl.ds(0, 2)], next_ref, move_send.at[frames], move_recv.at[frames], before
    )
    tails = remote(
        tail_out, tail_ref, move_send.at[frames + 1], move_recv.at[frames + 1], after
    )

    def moved(f):
        return remote(
            igrad_ref.at[f], arrived_ref.at[f], move_send.at[f], move_recv.at[f], before
        )

    @pl.when(tm == slabs - 1)
    def _():
        next_ref[...] = jnp.zeros_like(next_ref)
        arrived_ref[...] = jnp.zeros_like(arrived_ref)

    @pl.when(tm == 0)
    def _():
        tail_ref[...] = jnp.zeros_like(tail_ref)

    own_start, own_length = start_of(len_ref, slabs, tm), length_of(len_ref, slabs, tm)
    frame_total = start_of(len_ref, slabs, slabs)
    area = res_ref[0, 0] * res_ref[0, 1] * width
    count = (frame_total * area).astype(F32)
    mask_ref[...] = cells(res_ref, cols, (places, channels)).astype(F32)
    first, last = col_masks(cols, (places, channels))
    first_ref[...] = first
    last_ref[...] = last
    zero = jnp.zeros((8, channels), F32)
    row = lax.broadcasted_iota(jnp.int32, (8, channels), 0)


    def fold(value):
        return jnp.sum(value.reshape(places // 8, 8, channels), axis=0)

    def over_groups(total):
        line = jnp.sum(total, axis=0, keepdims=True)
        return group_sum(jnp.broadcast_to(line, (8, channels)), width)

    def add_up(f, total):
        held = (f < own_length).astype(F32)
        return total + fold(loaded_ref[f].astype(F32) * (mask_ref[...] * held))

    own_mean = over_groups(lax.fori_loop(0, frames, add_up, zero)) / (own_length * area).astype(F32)
    mean_row = own_mean[0:1]

    def spread(f, total):
        held = (f < own_length).astype(F32)
        apart = (loaded_ref[f].astype(F32) - mean_row) * (mask_ref[...] * held)
        return total + fold(apart * apart)

    squares = over_groups(lax.fori_loop(0, frames, spread, zero))
    stats_out[...] = jnp.where(row == 0, own_mean, squares)
    stats_ref[tm] = stats_out[...]
    for k in range(2):
        offset = tm * frames + frames - 2 + k - own_start
        usable = (offset >= 0) & (offset < own_length)
        picked = loaded_ref[jnp.clip(offset, 0, frames - 1)]
        tail_out[k] = jnp.where(usable, picked, jnp.zeros_like(picked))


    def pack(f, _):
        offset = (tm - 1) * frames + f - own_start
        usable = (offset >= 0) & (offset < own_length)
        picked = loaded_ref[jnp.clip(offset, 0, frames - 1)]
        igrad_ref[f] = jnp.where(usable, picked, jnp.zeros_like(picked))
        return 0

    lax.fori_loop(0, frames, pack, 0)

    pl.semaphore_wait(barrier, len(greeted))
    stats_shares = [
        send(stats_out, stats_ref.at[tm], stat_send.at[i], stat_recv.at[i], peer)
        for i, peer in enumerate(tm_peers)
    ]

    @pl.when(has_after)
    def _():
        tails.start()

    @pl.when(has_before)
    def _():
        moved(0).start()

    load.wait()

    def turn(block, _):
        for k in range(3):
            turned_ref[block, k * channels : (k + 1) * channels, :] = weight_ref[
                block, (2 - k) * channels : (3 - k) * channels, :
            ].T
        return 0

    lax.fori_loop(0, 9, turn, 0)
    blank = jnp.zeros((cols, 3 * channels), BF16)

    def place(frame, value):
        alive = (tm * frames + frame < frame_total).astype(F32)
        value = value.astype(F32) * (mask_ref[...] * alive)
        back_cat[frame, 0] = blank
        back_cat[frame, rows + 1] = blank
        lay_out(back_cat, frame, value, rows, cols, first_ref[...], last_ref[...])
        return value


    def own_grad(f, _):
        value = place(f, cot_ref[f])
        grad_ref[pl.ds(pl.multiple_of(f * places, places), places)] = value.astype(BF16)
        return 0

    lax.fori_loop(0, frames, own_grad, 0)

    def convolve(source, factor, f, back):
        total = jnp.zeros((places, channels), F32)
        for d in range(3):
            for r in range(3):
                at = (f + 2 - d, 2 - r) if back else (f + d, r)
                lines = source[at[0], at[1] : at[1] + rows].reshape(places, 3 * channels)
                total = total + jnp.dot(lines, factor[3 * d + r], preferred_element_type=F32)
        return total * (mask_ref[...] * (tm * frames + f < frame_total).astype(F32))

    def back_sweep(f, _):
        agrad_ref[f] = convolve(back_cat, turned_ref, f, True)
        return 0

    for copy in stats_shares:
        copy.wait()

    @pl.when(has_before)
    def _():
        for f in range(1, frames):
            moved(f).start()
        halo.start()

    lax.fori_loop(0, frames - 2, back_sweep, 0)

    counts = [(len_ref[0, i] * area).astype(F32) for i in range(slabs)]
    mean = jnp.zeros((1, channels), F32)
    for i in range(slabs):
        mean = mean + counts[i] * stats_ref[i, 0:1]
    mean = mean / count
    squares = jnp.zeros((1, channels), F32)
    for i in range(slabs):
        apart = stats_ref[i, 0:1] - mean
        squares = squares + stats_ref[i, 1:2] + counts[i] * (apart * apart)
    root = lax.rsqrt(squares / count + EPSILON)
    gain, bias = gain_ref[...], bias_ref[...]

    def activate(slot, frame_id, value):
        alive = ((frame_id >= 0) & (frame_id < frame_total)).astype(F32)
        live = mask_ref[...] * alive
        normed = (value.astype(F32) * live - mean) * live * root
        pre = normed * gain + bias
        gate = 1.0 / (1.0 + jnp.exp(-pre))
        act = (pre * gate * live).astype(BF16).astype(F32)
        cat_ref[slot, 0] = blank
        cat_ref[slot, rows + 1] = blank
        lay_out(cat_ref, slot, act, rows, cols, first_ref[...], last_ref[...])
        return normed

    @pl.when(has_before)
    def _():
        tails.wait_recv()

    for k in range(2):
        frame_id = tm * frames + k - 2
        offset = frame_id - own_start
        usable = (offset >= 0) & (offset < own_length)
        picked = jnp.where(usable, loaded_ref[jnp.clip(offset, 0, frames - 1)], tail_ref[k])
        activate(k, frame_id, picked)

    def own_frame(f, _):
        @pl.when(has_after)
        def _():
            moved(f).wait_recv()

        frame_id = tm * frames + f
        offset = frame_id - own_start
        picked = jnp.where(
            offset < own_length,
            loaded_ref[jnp.clip(offset, 0, frames - 1)],
            arrived_ref[f],
        )
        normed_ref[f] = activate(f + 2, frame_id, picked)
        return 0

    def through(f, sums):
        normed = normed_ref[f]
        pre = normed * gain + bias
        gate = 1.0 / (1.0 + jnp.exp(-pre))
        pre_grad = agrad_ref[f] * gate * (1.0 + pre * (1.0 - gate))
        agrad_ref[f] = pre_grad * gain
        return sums[0] + fold(pre_grad * normed), sums[1] + fold(pre_grad)

    order = [(k % 3, (k + 1) % 3, (k + 2) % 3) for k in range(3)]
    own_lanes = pl.ds(pl.multiple_of(core * lanes, lanes), lanes)

    def spread_out(stage, k, axis, source, target):
        row_of = []
        for off in (1, 2, 3):
            there, peer = along(axis, off)
            row_of.append(
                send(
                    source(there), target(off - 1),
                    send_sem.at[stage, k, off - 1], recv_sem.at[stage, k, off - 1], peer,
                )
            )
        return row_of

    def product(k, r, begin, end):
        lines = cat_ref[k + begin : k + end, r : r + rows].reshape(-1, 3 * channels)
        both = lax.dot_general(
            lines,
            grad_ref[begin * places : end * places],
            (((0,), (0,)), ((), ())),
            preferred_element_type=F32,
        ).reshape(per_row, 16, channels)
        low, high = both[..., :lanes], both[..., lanes:]
        return jnp.where(core == 0, low, high), jnp.where(core == 0, high, low)

    def early_part(k):
        for r in range(3):
            at = slice(r * per_row, (r + 1) * per_row)
            own_part[k, at], far_sum[k, at] = product(k, r, 0, early)

    def kernel_part(k):
        for r in range(3):
            at = slice(r * per_row, (r + 1) * per_row)
            own, far = product(k, r, early, frames)
            own_part[k, at] = own_part[k, at] + own
            far_part[k, at] = (far_sum[k, at] + far).astype(BF16)
        return send(
            far_part.at[k], core_in.at[k], send_sem.at[0, k, 0], recv_sem.at[0, k, 0], other
        )

    def first_stage(k, half):
        half.wait()

        def add_half(b, _):
            at = pl.ds(b * 4, 4)
            both = own_part[k, at] + core_in[k, at].astype(F32)
            own_part[k, at] = both
            send1[k, at] = both.astype(BF16)
            return 0

        lax.fori_loop(0, blocks // 4, add_half, 0)
        return spread_out(
            1, k, order[k][0],
            lambda there: send1.at[k, pl.ds(there * part, part)],
            lambda i: in1.at[k, i],
        )

    def second_stage(k, copies):
        for copy in copies:
            copy.wait()
        base = here[order[k][0]] * part

        def add_first(b, _):
            at = pl.ds(b * 3, 3)
            own = own_part[k, pl.ds(base + b * 3, 3)]
            for i in range(3):
                own = own + in1[k, i, at].astype(F32)
            send2[k, at] = own.astype(BF16)
            return 0

        lax.fori_loop(0, part // 3, add_first, 0)
        return spread_out(
            2, k, order[k][1],
            lambda there: send2.at[k, pl.ds(there * piece, piece)],
            lambda i: in2.at[k, i],
        )

    def third_stage(k, copies):
        for copy in copies:
            copy.wait()
        base = here[order[k][1]] * piece
        spot = here[order[k][2]]

        def add_second(b, _):
            at = pl.ds(b * 3, 3)
            own = send2[k, pl.ds(base + b * 3, 3)].astype(F32)
            for i in range(3):
                own = own + in2[k, i, at].astype(F32)
            in3[k, spot, at] = own.astype(BF16)
            return 0

        lax.fori_loop(0, piece // 3, add_second, 0)
        return spread_out(
            3, k, order[k][2], lambda there: in3.at[k, spot], lambda i: in3.at[k, spot]
        )

    def fourth_stage(k, copies):
        for copy in copies:
            copy.wait()
        base = here[order[k][0]] * part + here[order[k][1]] * piece

        def add_third(b, _):
            at = pl.ds(b * 3, 3)
            own = in3[k, 0, at].astype(F32)
            for i in range(1, 4):
                own = own + in3[k, i, at].astype(F32)
            total_ref[k, pl.ds(base + b * 3, 3), :, own_lanes] = own.astype(BF16)
            return 0

        lax.fori_loop(0, piece // 3, add_third, 0)
        row_of = spread_out(
            4, k, order[k][1],
            lambda there: fragment(k, here[order[k][1]]),
            lambda i: fragment(k, here[order[k][1]]),
        )
        return row_of, [hand_on(k, 0)]

    def fragment(k, there):
        base = here[order[k][0]] * part + there * piece
        return total_ref.at[k, pl.ds(base, piece), :, own_lanes]

    def hand_on(k, back):
        spot = fragment(k, (here[order[k][1]] + 4 - back) % 4)
        row_of = []
        for off in (1, 2, 3):
            at = 3 * back + off - 1
            row_of.append(
                send(
                    spot, spot, send_sem.at[5, k, at], recv_sem.at[5, k, at],
                    along(order[k][0], off)[1],
                )
            )
        return row_of

    def region(k, there):
        return total_ref.at[k, pl.ds(there * part, part), :, own_lanes]

    def to_core(k, there, i):
        spot = region(k, there)
        return send(spot, spot, send_sem.at[6, k, i], recv_sem.at[6, k, i], other)

    def fifth_stage(k, copies):
        arriving, pieces = copies
        for back in (1, 3, 2):
            arriving[back - 1].wait()
            pieces.append(hand_on(k, back))
        return pieces, [to_core(k, here[order[k][0]], 0)]

    def sixth_stage(k, off, copies):
        for row_of in copies[0]:
            row_of[off - 1].wait()
        copies[1].append(to_core(k, (here[order[k][0]] + 4 - off) % 4, off))

    def forward_sweep(f, _):
        encoded_ref[f] = convolve(cat_ref, weight_ref, f, False).astype(BF16)
        return 0

    def take_in(f, _):
        own_frame(f, 0)
        forward_sweep(f, 0)
        return 0

    lax.fori_loop(0, early, take_in, 0)
    for k in range(3):
        early_part(k)
    lax.fori_loop(early, frames, own_frame, 0)

    half0 = kernel_part(0)
    half1 = kernel_part(1)
    stage0 = first_stage(0, half0)
    half2 = kernel_part(2)
    stage1 = first_stage(1, half1)
    stage2 = first_stage(2, half2)
    lax.fori_loop(early, frames, forward_sweep, 0)

    @pl.when(has_after)
    def _():
        halo.wait_recv()

    for k in range(2):
        place(frames + k, next_ref[k])
    lax.fori_loop(frames - 2, frames, back_sweep, 0)
    gain_sum, bias_sum = lax.fori_loop(0, frames, through, (zero, zero))
    sums_ref[...] = jnp.where(
        row == 0,
        jnp.sum(gain_sum, axis=0, keepdims=True),
        jnp.where(row == 1, jnp.sum(bias_sum, axis=0, keepdims=True), 0.0),
    )
    slabs_ref[tm] = sums_ref[...]
    shares = [
        send(sums_ref, slabs_ref.at[tm], pair_send.at[i], pair_recv.at[i], peer)
        for i, peer in enumerate(tm_peers)
    ]

    stage0 = second_stage(0, stage0)
    stage1 = second_stage(1, stage1)
    for copy in shares:
        copy.wait()
    total = slabs_ref[0]
    for i in range(1, slabs):
        total = total + slabs_ref[i]
    tm_total[...] = total
    core_copy = send(tm_total, core_sum, pair_send.at[7], pair_recv.at[7], other)
    stage0 = third_stage(0, stage0)
    stage2 = second_stage(2, stage2)
    stage1 = third_stage(1, stage1)

    core_copy.wait()
    x_sums[x] = tm_total[...] + core_sum[...]
    x_copies = [
        send(x_sums.at[x], x_sums.at[x], pair_send.at[7 + off], pair_recv.at[7 + off], along(0, off)[1])
        for off in (1, 2, 3)
    ]
    shares_of = group_sum(tm_total[...] * gain, width) / count
    mean_part, along_part = shares_of[1:2], shares_of[0:1]

    @pl.when(has_before)
    def _():
        for f in range(frames):
            moved(f).wait_send()

    def finish(f, _):
        live = mask_ref[...] * (tm * frames + f < frame_total).astype(F32)
        inner = agrad_ref[f] - mean_part - normed_ref[f] * along_part
        igrad_ref[f] = (inner * root * live).astype(BF16)
        return 0

    lax.fori_loop(0, frames // 2, finish, 0)
    stage0 = fourth_stage(0, stage0)
    stage2 = third_stage(2, stage2)
    lax.fori_loop(frames // 2, frames, finish, 0)

    stage1 = fourth_stage(1, stage1)
    for copy in x_copies:
        copy.wait()
    x_total[...] = x_sums[0] + x_sums[1] + x_sums[2] + x_sums[3]
    z_copy = send(x_total, z_sum, pair_send.at[11], pair_recv.at[11], across)
    stage0 = fifth_stage(0, stage0)
    stage2 = fourth_stage(2, stage2)
    stage1 = fifth_stage(1, stage1)
    z_copy.wait()
    pair_ref[...] = x_total[...] + z_sum[...]
    stage2 = fifth_stage(2, stage2)
    ends = (stage0, stage1, stage2)
    for off in (1, 3, 2):
        for k in range(3):
            sixth_stage(k, off, ends[k])
    for k in range(3):
        for copy in ends[k][1]:
            copy.wait()

    @pl.when(has_before)
    def _():
        halo.wait_send()

    @pl.when(has_after)
    def _():
        tails.wait_send()


def pinned(value):
    return pltpu.with_memory_space_constraint(value, pltpu.HBM)


def body(loaded, lengths, resolution, weight, norm_gain, norm_bias, cotangent):
    frames, rows, cols, channels = loaded.shape[1:]
    places, width, lanes = rows * cols, channels // GROUPS, channels // 2
    slabs = lax.axis_size("tm")
    shape = jax.ShapeDtypeStruct
    slab = (frames, places, channels)
    blocks = 9 * channels // 16
    part, piece = blocks // 4, blocks // 16

    def tiles(*lead, kind=BF16):
        return pltpu.VMEM(lead + (16, lanes), kind)

    small = pltpu.VMEM((8, channels), F32)
    plane = pltpu.VMEM((places, channels), F32)
    cat = pltpu.VMEM((frames + 2, rows + 2, cols, 3 * channels), BF16)
    dma = pltpu.SemaphoreType.DMA
    encoded, igrad, total, pair = pl.pallas_call(
        functools.partial(section_kernel, rows, cols, width),
        out_shape=(
            shape(slab, BF16),
            shape(slab, BF16),
            shape((3, blocks, 16, channels), BF16),
            shape((8, channels), F32),
        ),
        in_specs=[SMEM, SMEM, VMEM, VMEM, HBM, VMEM, VMEM],
        out_specs=(VMEM,) * 4,
        scratch_shapes=[
            pltpu.VMEM(slab, BF16),
            pltpu.VMEM((2, places, channels), BF16),
            pltpu.VMEM((2, places, channels), BF16),
            pltpu.VMEM((2, places, channels), BF16),
            pltpu.VMEM((9, 3 * channels, channels), BF16),
            pltpu.VMEM((9, 3 * channels, channels), BF16),
            cat,
            cat,
            pltpu.VMEM((frames * places, channels), BF16),
            pltpu.VMEM(slab, F32),
            pltpu.VMEM(slab, F32),
            plane,
            plane,
            plane,
            small,
            pltpu.VMEM((slabs, 8, channels), F32),
            small,
            pltpu.VMEM((slabs, 8, channels), F32),
            tiles(3, blocks, kind=F32),
            tiles(3, blocks, kind=F32),
            tiles(3, blocks),
            tiles(3, blocks),
            tiles(3, blocks),
            tiles(3, 3, part),
            tiles(3, part),
            tiles(3, 3, piece),
            tiles(3, 4, piece),
            small,
            small,
            pltpu.VMEM((4, 8, channels), F32),
            small,
            small,
            dma,
            dma((frames + 2,)),
            dma((frames + 2,)),
            dma((7,)),
            dma((7,)),
            dma((7, 3, 12)),
            dma((7, 3, 12)),
            dma((12,)),
            dma((12,)),
        ],
        compiler_params=params(LIMIT, collective_id=1, has_side_effects=True),
    )(
        *map(
            pinned,
            (
                lengths,
                resolution,
                loaded.reshape(slab),
                cotangent.reshape(slab),
                weight.reshape(9, 3 * channels, channels),
                norm_gain.reshape(1, channels),
                norm_bias.reshape(1, channels),
            ),
        )
    )
    scale = 1.0 / math.sqrt(lax.axis_size("dp") * slabs * frames * places)
    whole = (1, frames, rows, cols, channels)
    return (
        encoded.reshape(whole),
        igrad.reshape(whole),
        total.reshape(27, channels, channels).astype(F32) * scale,
        pair[0] * scale,
        pair[1] * scale,
    )


def solution(mesh):
    slab = P("dp", "tm", None, None, None)
    return jax.shard_map(
        body,
        mesh=mesh,
        in_specs=(slab, P("dp", None), P("dp", None), P(), P(), P(), slab),
        out_specs=(slab, slab, P(), P(), P()),
        check_vma=False,
    )
```

```python
import functools
import math

import jax
import jax.numpy as jnp
from jax import lax
from jax.experimental import pallas as pl
from jax.experimental.pallas import tpu as pltpu
from jax.sharding import PartitionSpec as P

GROUPS = 32
EPSILON = 1e-05
LIMIT = 45
MESH = pl.DeviceIdType.MESH
F32 = jnp.float32
BF16 = jnp.bfloat16

VMEM = pl.BlockSpec(memory_space=pltpu.VMEM)
HBM = pl.BlockSpec(memory_space=pltpu.HBM)
SMEM = pl.BlockSpec(memory_space=pltpu.SMEM)


def params(limit, **others):
    return pltpu.CompilerParams(vmem_limit_bytes=limit << 20, **others)


def start_of(len_ref, slabs, index):
    total = jnp.int32(0)
    for i in range(slabs):
        total = total + jnp.where(i < index, len_ref[0, i], 0)
    return total


def length_of(len_ref, slabs, index):
    total = jnp.int32(0)
    for i in range(slabs):
        total = total + jnp.where(i == index, len_ref[0, i], 0)
    return total


def group_sum(rows, width):
    lanes = rows.shape[1]
    lane = lax.broadcasted_iota(jnp.int32, rows.shape, 1)
    step = 1
    while step < width:
        up = pltpu.roll(rows, lanes - step, 1)
        down = pltpu.roll(rows, step, 1)
        rows = rows + jnp.where((lane & step) == 0, up, down)
        step *= 2
    return rows


def cells(res_ref, cols, shape):
    place = lax.broadcasted_iota(jnp.int32, shape, 0)
    return ((place // cols) < res_ref[0, 0]) & ((place % cols) < res_ref[0, 1])


def lay_out(cat_ref, frame, value, rows, cols, first_col, last_col):
    places, channels = value.shape
    left = pltpu.roll(value, 1, 0) * first_col
    right = pltpu.roll(value, places - 1, 0) * last_col
    for k, part in enumerate((left, value, right)):
        cat_ref[frame, 1 : rows + 1, :, k * channels : (k + 1) * channels] = (
            part.astype(BF16).reshape(rows, cols, channels)
        )


def col_masks(cols, shape):
    place = lax.broadcasted_iota(jnp.int32, shape, 0) % cols
    return (place != 0).astype(F32), (place != cols - 1).astype(F32)


def section_kernel(
    rows, cols, width,
    len_ref, res_ref, loaded_ref, cot_ref, weight_hbm, gain_ref, bias_ref,
    encoded_ref, igrad_ref, total_ref, pair_ref,
    arrived_ref, next_ref, tail_out, tail_ref, weight_ref, turned_ref,
    back_cat, cat_ref, grad_ref, agrad_ref, normed_ref,
    mask_ref, first_ref, last_ref, stats_out, stats_ref, sums_ref, slabs_ref,
    own_part, far_sum, far_part, core_in, send1, in1, send2, in2, in3,
    tm_total, core_sum, x_sums, x_total, z_sum,
    local_sem, move_send, move_recv, stat_send, stat_recv,
    send_sem, recv_sem, pair_send, pair_recv,
):
    frames, places, channels = loaded_ref.shape
    blocks = own_part.shape[1]
    part, piece, lanes = blocks // 4, blocks // 16, channels // 2
    per_row = blocks // 3
    early = frames - 2
    slabs = 8

    dp, tm = lax.axis_index("dp"), lax.axis_index("tm")
    core, x, y = dp % 2, dp // 4, tm % 4
    z = (dp // 2) % 2 * 2 + tm // 4
    here = (x, y, z)

    def device(place, its_core):
        return ((place[0] * 2 + place[2] // 2) * 2 + its_core, (place[2] % 2) * 4 + place[1])

    def along(axis, off):
        place = list(here)
        place[axis] = (here[axis] + off) % 4
        return place[axis], device(place, core)

    other = device(here, 1 - core)
    across = device((x, y, (z + 2) % 4), core)
    tm_peers = [(dp, (tm + off) % slabs) for off in range(1, slabs)]
    axis_peers = [along(axis, off)[1] for axis in (0, 1, 2) for off in (1, 2, 3)]
    before, after = (dp, (tm + slabs - 1) % slabs), (dp, (tm + 1) % slabs)
    has_before, has_after = tm > 0, tm < slabs - 1

    barrier = pltpu.get_barrier_semaphore()
    greeted = [other] + axis_peers + tm_peers
    for peer in greeted:
        pl.semaphore_signal(barrier, inc=1, device_id=peer, device_id_type=MESH)

    load = pltpu.make_async_copy(weight_hbm, weight_ref, local_sem)
    load.start()

    def remote(src, dst, send_at, recv_at, peer):
        return pltpu.make_async_remote_copy(
            src_ref=src, dst_ref=dst, send_sem=send_at, recv_sem=recv_at,
            device_id=peer, device_id_type=MESH,
        )

    def send(*arguments):
        copy = remote(*arguments)
        copy.start()
        return copy

    halo = remote(
        cot_ref.at[pl.ds(0, 2)], next_ref, move_send.at[frames], move_recv.at[frames], before
    )
    tails = remote(
        tail_out, tail_ref, move_send.at[frames + 1], move_recv.at[frames + 1], after
    )

    def moved(f):
        return remote(
            igrad_ref.at[f], arrived_ref.at[f], move_send.at[f], move_recv.at[f], before
        )

    @pl.when(tm == slabs - 1)
    def _():
        next_ref[...] = jnp.zeros_like(next_ref)
        arrived_ref[...] = jnp.zeros_like(arrived_ref)

    @pl.when(tm == 0)
    def _():
        tail_ref[...] = jnp.zeros_like(tail_ref)

    own_start, own_length = start_of(len_ref, slabs, tm), length_of(len_ref, slabs, tm)
    frame_total = start_of(len_ref, slabs, slabs)
    area = res_ref[0, 0] * res_ref[0, 1] * width
    count = (frame_total * area).astype(F32)
    mask_ref[...] = cells(res_ref, cols, (places, channels)).astype(F32)
    first, last = col_masks(cols, (places, channels))
    first_ref[...] = first
    last_ref[...] = last
    zero = jnp.zeros((8, channels), F32)
    row = lax.broadcasted_iota(jnp.int32, (8, channels), 0)


    def fold(value):
        return jnp.sum(value.reshape(places // 8, 8, channels), axis=0)

    def over_groups(total):
        line = jnp.sum(total, axis=0, keepdims=True)
        return group_sum(jnp.broadcast_to(line, (8, channels)), width)

    def add_up(f, total):
        held = (f < own_length).astype(F32)
        return total + fold(loaded_ref[f].astype(F32) * (mask_ref[...] * held))

    own_mean = over_groups(lax.fori_loop(0, frames, add_up, zero)) / (own_length * area).astype(F32)
    mean_row = own_mean[0:1]

    def spread(f, total):
        held = (f < own_length).astype(F32)
        apart = (loaded_ref[f].astype(F32) - mean_row) * (mask_ref[...] * held)
        return total + fold(apart * apart)

    squares = over_groups(lax.fori_loop(0, frames, spread, zero))
    stats_out[...] = jnp.where(row == 0, own_mean, squares)
    stats_ref[tm] = stats_out[...]
    for k in range(2):
        offset = tm * frames + frames - 2 + k - own_start
        usable = (offset >= 0) & (offset < own_length)
        picked = loaded_ref[jnp.clip(offset, 0, frames - 1)]
        tail_out[k] = jnp.where(usable, picked, jnp.zeros_like(picked))


    def pack(f, _):
        offset = (tm - 1) * frames + f - own_start
        usable = (offset >= 0) & (offset < own_length)
        picked = loaded_ref[jnp.clip(offset, 0, frames - 1)]
        igrad_ref[f] = jnp.where(usable, picked, jnp.zeros_like(picked))
        return 0

    lax.fori_loop(0, frames, pack, 0)

    pl.semaphore_wait(barrier, len(greeted))
    stats_shares = [
        send(stats_out, stats_ref.at[tm], stat_send.at[i], stat_recv.at[i], peer)
        for i, peer in enumerate(tm_peers)
    ]

    @pl.when(has_after)
    def _():
        tails.start()

    @pl.when(has_before)
    def _():
        moved(0).start()
        moved(1).start()

    load.wait()

    def turn(block, _):
        for k in range(3):
            turned_ref[block, k * channels : (k + 1) * channels, :] = weight_ref[
                block, (2 - k) * channels : (3 - k) * channels, :
            ].T
        return 0

    lax.fori_loop(0, 9, turn, 0)
    blank = jnp.zeros((cols, 3 * channels), BF16)

    def place(frame, value):
        alive = (tm * frames + frame < frame_total).astype(F32)
        value = value.astype(F32) * (mask_ref[...] * alive)
        back_cat[frame, 0] = blank
        back_cat[frame, rows + 1] = blank
        lay_out(back_cat, frame, value, rows, cols, first_ref[...], last_ref[...])
        return value


    def own_grad(f, _):
        value = place(f, cot_ref[f])
        grad_ref[pl.ds(pl.multiple_of(f * places, places), places)] = value.astype(BF16)
        return 0

    lax.fori_loop(0, frames, own_grad, 0)

    def convolve(source, factor, f, back):
        total = jnp.zeros((places, channels), F32)
        for d in range(3):
            for r in range(3):
                at = (f + 2 - d, 2 - r) if back else (f + d, r)
                lines = source[at[0], at[1] : at[1] + rows].reshape(places, 3 * channels)
                total = total + jnp.dot(lines, factor[3 * d + r], preferred_element_type=F32)
        return total * (mask_ref[...] * (tm * frames + f < frame_total).astype(F32))

    def back_sweep(f, _):
        agrad_ref[f] = convolve(back_cat, turned_ref, f, True)
        return 0

    for copy in stats_shares:
        copy.wait()

    @pl.when(has_before)
    def _():
        for f in range(2, frames):
            moved(f).start()
        halo.start()

    lax.fori_loop(0, frames - 2, back_sweep, 0)

    counts = [(len_ref[0, i] * area).astype(F32) for i in range(slabs)]
    mean = jnp.zeros((1, channels), F32)
    for i in range(slabs):
        mean = mean + counts[i] * stats_ref[i, 0:1]
    mean = mean / count
    squares = jnp.zeros((1, channels), F32)
    for i in range(slabs):
        apart = stats_ref[i, 0:1] - mean
        squares = squares + stats_ref[i, 1:2] + counts[i] * (apart * apart)
    root = lax.rsqrt(squares / count + EPSILON)
    gain, bias = gain_ref[...], bias_ref[...]

    def activate(slot, frame_id, value):
        alive = ((frame_id >= 0) & (frame_id < frame_total)).astype(F32)
        live = mask_ref[...] * alive
        normed = (value.astype(F32) * live - mean) * live * root
        pre = normed * gain + bias
        gate = 1.0 / (1.0 + jnp.exp(-pre))
        act = (pre * gate * live).astype(BF16).astype(F32)
        cat_ref[slot, 0] = blank
        cat_ref[slot, rows + 1] = blank
        lay_out(cat_ref, slot, act, rows, cols, first_ref[...], last_ref[...])
        return normed

    @pl.when(has_before)
    def _():
        tails.wait_recv()

    for k in range(2):
        frame_id = tm * frames + k - 2
        offset = frame_id - own_start
        usable = (offset >= 0) & (offset < own_length)
        picked = jnp.where(usable, loaded_ref[jnp.clip(offset, 0, frames - 1)], tail_ref[k])
        activate(k, frame_id, picked)

    def own_frame(f, _):
        @pl.when(has_after)
        def _():
            moved(f).wait_recv()

        frame_id = tm * frames + f
        offset = frame_id - own_start
        picked = jnp.where(
            offset < own_length,
            loaded_ref[jnp.clip(offset, 0, frames - 1)],
            arrived_ref[f],
        )
        normed_ref[f] = activate(f + 2, frame_id, picked)
        return 0

    def through(f, sums):
        normed = normed_ref[f]
        pre = normed * gain + bias
        gate = 1.0 / (1.0 + jnp.exp(-pre))
        pre_grad = agrad_ref[f] * gate * (1.0 + pre * (1.0 - gate))
        agrad_ref[f] = pre_grad * gain
        return sums[0] + fold(pre_grad * normed), sums[1] + fold(pre_grad)

    order = [(k % 3, (k + 1) % 3, (k + 2) % 3) for k in range(3)]
    own_lanes = pl.ds(pl.multiple_of(core * lanes, lanes), lanes)

    def spread_out(stage, k, axis, source, target):
        row_of = []
        for off in (1, 2, 3):
            there, peer = along(axis, off)
            row_of.append(
                send(
                    source(there), target(off - 1),
                    send_sem.at[stage, k, off - 1], recv_sem.at[stage, k, off - 1], peer,
                )
            )
        return row_of

    def product(k, r, begin, end):
        lines = cat_ref[k + begin : k + end, r : r + rows].reshape(-1, 3 * channels)
        both = lax.dot_general(
            lines,
            grad_ref[begin * places : end * places],
            (((0,), (0,)), ((), ())),
            preferred_element_type=F32,
        ).reshape(per_row, 16, channels)
        low, high = both[..., :lanes], both[..., lanes:]
        return jnp.where(core == 0, low, high), jnp.where(core == 0, high, low)

    def early_part(k):
        for r in range(3):
            at = slice(r * per_row, (r + 1) * per_row)
            own_part[k, at], far_sum[k, at] = product(k, r, 0, early)

    def kernel_part(k):
        for r in range(3):
            at = slice(r * per_row, (r + 1) * per_row)
            own, far = product(k, r, early, frames)
            own_part[k, at] = own_part[k, at] + own
            far_part[k, at] = (far_sum[k, at] + far).astype(BF16)
        return send(
            far_part.at[k], core_in.at[k], send_sem.at[0, k, 0], recv_sem.at[0, k, 0], other
        )

    def first_stage(k, half):
        half.wait()

        def add_half(b, _):
            at = pl.ds(b * 4, 4)
            both = own_part[k, at] + core_in[k, at].astype(F32)
            own_part[k, at] = both
            send1[k, at] = both.astype(BF16)
            return 0

        lax.fori_loop(0, blocks // 4, add_half, 0)
        return spread_out(
            1, k, order[k][0],
            lambda there: send1.at[k, pl.ds(there * part, part)],
            lambda i: in1.at[k, i],
        )

    def second_stage(k, copies):
        for copy in copies:
            copy.wait()
        base = here[order[k][0]] * part

        def add_first(b, _):
            at = pl.ds(b * 3, 3)
            own = own_part[k, pl.ds(base + b * 3, 3)]
            for i in range(3):
                own = own + in1[k, i, at].astype(F32)
            send2[k, at] = own.astype(BF16)
            return 0

        lax.fori_loop(0, part // 3, add_first, 0)
        return spread_out(
            2, k, order[k][1],
            lambda there: send2.at[k, pl.ds(there * piece, piece)],
            lambda i: in2.at[k, i],
        )

    def third_stage(k, copies):
        for copy in copies:
            copy.wait()
        base = here[order[k][1]] * piece
        spot = here[order[k][2]]

        def add_second(b, _):
            at = pl.ds(b * 3, 3)
            own = send2[k, pl.ds(base + b * 3, 3)].astype(F32)
            for i in range(3):
                own = own + in2[k, i, at].astype(F32)
            in3[k, spot, at] = own.astype(BF16)
            return 0

        lax.fori_loop(0, piece // 3, add_second, 0)
        return spread_out(
            3, k, order[k][2], lambda there: in3.at[k, spot], lambda i: in3.at[k, spot]
        )

    def fourth_stage(k, copies):
        for copy in copies:
            copy.wait()
        base = here[order[k][0]] * part + here[order[k][1]] * piece

        def add_third(b, _):
            at = pl.ds(b * 3, 3)
            own = in3[k, 0, at].astype(F32)
            for i in range(1, 4):
                own = own + in3[k, i, at].astype(F32)
            total_ref[k, pl.ds(base + b * 3, 3), :, own_lanes] = own.astype(BF16)
            return 0

        lax.fori_loop(0, piece // 3, add_third, 0)
        row_of = spread_out(
            4, k, order[k][1],
            lambda there: fragment(k, here[order[k][1]]),
            lambda i: fragment(k, here[order[k][1]]),
        )
        return row_of, [hand_on(k, 0)]

    def fragment(k, there):
        base = here[order[k][0]] * part + there * piece
        return total_ref.at[k, pl.ds(base, piece), :, own_lanes]

    def hand_on(k, back):
        spot = fragment(k, (here[order[k][1]] + 4 - back) % 4)
        row_of = []
        for off in (1, 2, 3):
            at = 3 * back + off - 1
            row_of.append(
                send(
                    spot, spot, send_sem.at[5, k, at], recv_sem.at[5, k, at],
                    along(order[k][0], off)[1],
                )
            )
        return row_of

    def region(k, there):
        return total_ref.at[k, pl.ds(there * part, part), :, own_lanes]

    def to_core(k, there, i):
        spot = region(k, there)
        return send(spot, spot, send_sem.at[6, k, i], recv_sem.at[6, k, i], other)

    def fifth_stage(k, copies):
        arriving, pieces = copies
        for back in (1, 3, 2):
            arriving[back - 1].wait()
            pieces.append(hand_on(k, back))
        return pieces, [to_core(k, here[order[k][0]], 0)]

    def sixth_stage(k, off, copies):
        for row_of in copies[0]:
            row_of[off - 1].wait()
        copies[1].append(to_core(k, (here[order[k][0]] + 4 - off) % 4, off))

    def forward_sweep(f, _):
        encoded_ref[f] = convolve(cat_ref, weight_ref, f, False).astype(BF16)
        return 0

    def take_in(f, _):
        own_frame(f, 0)
        forward_sweep(f, 0)
        return 0

    lax.fori_loop(0, early, take_in, 0)
    for k in range(3):
        early_part(k)
    lax.fori_loop(early, frames, own_frame, 0)

    half0 = kernel_part(0)
    half1 = kernel_part(1)
    stage0 = first_stage(0, half0)
    half2 = kernel_part(2)
    stage1 = first_stage(1, half1)
    stage2 = first_stage(2, half2)
    lax.fori_loop(early, frames, forward_sweep, 0)

    @pl.when(has_after)
    def _():
        halo.wait_recv()

    for k in range(2):
        place(frames + k, next_ref[k])
    lax.fori_loop(frames - 2, frames, back_sweep, 0)
    gain_sum, bias_sum = lax.fori_loop(0, frames, through, (zero, zero))
    sums_ref[...] = jnp.where(
        row == 0,
        jnp.sum(gain_sum, axis=0, keepdims=True),
        jnp.where(row == 1, jnp.sum(bias_sum, axis=0, keepdims=True), 0.0),
    )
    slabs_ref[tm] = sums_ref[...]
    shares = [
        send(sums_ref, slabs_ref.at[tm], pair_send.at[i], pair_recv.at[i], peer)
        for i, peer in enumerate(tm_peers)
    ]

    stage0 = second_stage(0, stage0)
    stage1 = second_stage(1, stage1)
    for copy in shares:
        copy.wait()
    total = slabs_ref[0]
    for i in range(1, slabs):
        total = total + slabs_ref[i]
    tm_total[...] = total
    core_copy = send(tm_total, core_sum, pair_send.at[7], pair_recv.at[7], other)
    stage0 = third_stage(0, stage0)
    stage2 = second_stage(2, stage2)
    stage1 = third_stage(1, stage1)

    core_copy.wait()
    x_sums[x] = tm_total[...] + core_sum[...]
    x_copies = [
        send(x_sums.at[x], x_sums.at[x], pair_send.at[7 + off], pair_recv.at[7 + off], along(0, off)[1])
        for off in (1, 2, 3)
    ]
    shares_of = group_sum(tm_total[...] * gain, width) / count
    mean_part, along_part = shares_of[1:2], shares_of[0:1]

    @pl.when(has_before)
    def _():
        for f in range(frames):
            moved(f).wait_send()

    def finish(f, _):
        live = mask_ref[...] * (tm * frames + f < frame_total).astype(F32)
        inner = agrad_ref[f] - mean_part - normed_ref[f] * along_part
        igrad_ref[f] = (inner * root * live).astype(BF16)
        return 0

    lax.fori_loop(0, frames // 2, finish, 0)
    stage0 = fourth_stage(0, stage0)
    stage2 = third_stage(2, stage2)
    lax.fori_loop(frames // 2, frames, finish, 0)

    stage1 = fourth_stage(1, stage1)
    for copy in x_copies:
        copy.wait()
    x_total[...] = x_sums[0] + x_sums[1] + x_sums[2] + x_sums[3]
    z_copy = send(x_total, z_sum, pair_send.at[11], pair_recv.at[11], across)
    stage0 = fifth_stage(0, stage0)
    stage2 = fourth_stage(2, stage2)
    stage1 = fifth_stage(1, stage1)
    z_copy.wait()
    pair_ref[...] = x_total[...] + z_sum[...]
    stage2 = fifth_stage(2, stage2)
    ends = (stage0, stage1, stage2)
    for off in (1, 3, 2):
        for k in range(3):
            sixth_stage(k, off, ends[k])
    for k in range(3):
        for copy in ends[k][1]:
            copy.wait()

    @pl.when(has_before)
    def _():
        halo.wait_send()

    @pl.when(has_after)
    def _():
        tails.wait_send()


def pinned(value):
    return pltpu.with_memory_space_constraint(value, pltpu.HBM)


def body(loaded, lengths, resolution, weight, norm_gain, norm_bias, cotangent):
    frames, rows, cols, channels = loaded.shape[1:]
    places, width, lanes = rows * cols, channels // GROUPS, channels // 2
    slabs = lax.axis_size("tm")
    shape = jax.ShapeDtypeStruct
    slab = (frames, places, channels)
    blocks = 9 * channels // 16
    part, piece = blocks // 4, blocks // 16

    def tiles(*lead, kind=BF16):
        return pltpu.VMEM(lead + (16, lanes), kind)

    small = pltpu.VMEM((8, channels), F32)
    plane = pltpu.VMEM((places, channels), F32)
    cat = pltpu.VMEM((frames + 2, rows + 2, cols, 3 * channels), BF16)
    dma = pltpu.SemaphoreType.DMA
    encoded, igrad, total, pair = pl.pallas_call(
        functools.partial(section_kernel, rows, cols, width),
        out_shape=(
            shape(slab, BF16),
            shape(slab, BF16),
            shape((3, blocks, 16, channels), BF16),
            shape((8, channels), F32),
        ),
        in_specs=[SMEM, SMEM, VMEM, VMEM, HBM, VMEM, VMEM],
        out_specs=(VMEM,) * 4,
        scratch_shapes=[
            pltpu.VMEM(slab, BF16),
            pltpu.VMEM((2, places, channels), BF16),
            pltpu.VMEM((2, places, channels), BF16),
            pltpu.VMEM((2, places, channels), BF16),
            pltpu.VMEM((9, 3 * channels, channels), BF16),
            pltpu.VMEM((9, 3 * channels, channels), BF16),
            cat,
            cat,
            pltpu.VMEM((frames * places, channels), BF16),
            pltpu.VMEM(slab, F32),
            pltpu.VMEM(slab, F32),
            plane,
            plane,
            plane,
            small,
            pltpu.VMEM((slabs, 8, channels), F32),
            small,
            pltpu.VMEM((slabs, 8, channels), F32),
            tiles(3, blocks, kind=F32),
            tiles(3, blocks, kind=F32),
            tiles(3, blocks),
            tiles(3, blocks),
            tiles(3, blocks),
            tiles(3, 3, part),
            tiles(3, part),
            tiles(3, 3, piece),
            tiles(3, 4, piece),
            small,
            small,
            pltpu.VMEM((4, 8, channels), F32),
            small,
            small,
            dma,
            dma((frames + 2,)),
            dma((frames + 2,)),
            dma((7,)),
            dma((7,)),
            dma((7, 3, 12)),
            dma((7, 3, 12)),
            dma((12,)),
            dma((12,)),
        ],
        compiler_params=params(LIMIT, collective_id=1, has_side_effects=True),
    )(
        *map(
            pinned,
            (
                lengths,
                resolution,
                loaded.reshape(slab),
                cotangent.reshape(slab),
                weight.reshape(9, 3 * channels, channels),
                norm_gain.reshape(1, channels),
                norm_bias.reshape(1, channels),
            ),
        )
    )
    scale = 1.0 / math.sqrt(lax.axis_size("dp") * slabs * frames * places)
    whole = (1, frames, rows, cols, channels)
    return (
        encoded.reshape(whole),
        igrad.reshape(whole),
        total.reshape(27, channels, channels).astype(F32) * scale,
        pair[0] * scale,
        pair[1] * scale,
    )


def solution(mesh):
    slab = P("dp", "tm", None, None, None)
    return jax.shard_map(
        body,
        mesh=mesh,
        in_specs=(slab, P("dp", None), P("dp", None), P(), P(), P(), slab),
        out_specs=(slab, slab, P(), P(), P()),
        check_vma=False,
    )
```

```python
import functools
import math

import jax
import jax.numpy as jnp
from jax import lax
from jax.experimental import pallas as pl
from jax.experimental.pallas import tpu as pltpu
from jax.sharding import PartitionSpec as P

GROUPS = 32
EPSILON = 1e-05
LIMIT = 45
MESH = pl.DeviceIdType.MESH
F32 = jnp.float32
BF16 = jnp.bfloat16

VMEM = pl.BlockSpec(memory_space=pltpu.VMEM)
HBM = pl.BlockSpec(memory_space=pltpu.HBM)
SMEM = pl.BlockSpec(memory_space=pltpu.SMEM)


def params(limit, **others):
    return pltpu.CompilerParams(vmem_limit_bytes=limit << 20, **others)


def start_of(len_ref, slabs, index):
    total = jnp.int32(0)
    for i in range(slabs):
        total = total + jnp.where(i < index, len_ref[0, i], 0)
    return total


def length_of(len_ref, slabs, index):
    total = jnp.int32(0)
    for i in range(slabs):
        total = total + jnp.where(i == index, len_ref[0, i], 0)
    return total


def group_sum(rows, width):
    lanes = rows.shape[1]
    lane = lax.broadcasted_iota(jnp.int32, rows.shape, 1)
    step = 1
    while step < width:
        up = pltpu.roll(rows, lanes - step, 1)
        down = pltpu.roll(rows, step, 1)
        rows = rows + jnp.where((lane & step) == 0, up, down)
        step *= 2
    return rows


def cells(res_ref, cols, shape):
    place = lax.broadcasted_iota(jnp.int32, shape, 0)
    return ((place // cols) < res_ref[0, 0]) & ((place % cols) < res_ref[0, 1])


def lay_out(cat_ref, frame, value, rows, cols, first_col, last_col):
    places, channels = value.shape
    left = pltpu.roll(value, 1, 0) * first_col
    right = pltpu.roll(value, places - 1, 0) * last_col
    for k, part in enumerate((left, value, right)):
        cat_ref[frame, 1 : rows + 1, :, k * channels : (k + 1) * channels] = (
            part.astype(BF16).reshape(rows, cols, channels)
        )


def col_masks(cols, shape):
    place = lax.broadcasted_iota(jnp.int32, shape, 0) % cols
    return (place != 0).astype(F32), (place != cols - 1).astype(F32)


def section_kernel(
    rows, cols, width,
    len_ref, res_ref, loaded_ref, cot_ref, weight_hbm, gain_ref, bias_ref,
    encoded_ref, igrad_ref, total_ref, pair_ref,
    arrived_ref, next_ref, tail_out, tail_ref, weight_ref, turned_ref,
    back_cat, cat_ref, grad_ref, agrad_ref, normed_ref,
    mask_ref, first_ref, last_ref, stats_out, stats_ref, sums_ref, slabs_ref,
    own_part, far_sum, far_part, core_in, send1, in1, send2, in2, in3,
    tm_total, core_sum, x_sums, x_total, z_sum,
    local_sem, move_send, move_recv, stat_send, stat_recv,
    send_sem, recv_sem, pair_send, pair_recv,
):
    frames, places, channels = loaded_ref.shape
    blocks = own_part.shape[1]
    part, piece, lanes = blocks // 4, blocks // 16, channels // 2
    per_row = blocks // 3
    early = frames - 2
    slabs = 8

    dp, tm = lax.axis_index("dp"), lax.axis_index("tm")
    core, x, y = dp % 2, dp // 4, tm % 4
    z = (dp // 2) % 2 * 2 + tm // 4
    here = (x, y, z)

    def device(place, its_core):
        return ((place[0] * 2 + place[2] // 2) * 2 + its_core, (place[2] % 2) * 4 + place[1])

    def along(axis, off):
        place = list(here)
        place[axis] = (here[axis] + off) % 4
        return place[axis], device(place, core)

    other = device(here, 1 - core)
    across = device((x, y, (z + 2) % 4), core)
    tm_peers = [(dp, (tm + off) % slabs) for off in range(1, slabs)]
    axis_peers = [along(axis, off)[1] for axis in (0, 1, 2) for off in (1, 2, 3)]
    before, after = (dp, (tm + slabs - 1) % slabs), (dp, (tm + 1) % slabs)
    has_before, has_after = tm > 0, tm < slabs - 1

    barrier = pltpu.get_barrier_semaphore()
    greeted = [other] + axis_peers + tm_peers
    for peer in greeted:
        pl.semaphore_signal(barrier, inc=1, device_id=peer, device_id_type=MESH)

    load = pltpu.make_async_copy(weight_hbm, weight_ref, local_sem)
    load.start()

    def remote(src, dst, send_at, recv_at, peer):
        return pltpu.make_async_remote_copy(
            src_ref=src, dst_ref=dst, send_sem=send_at, recv_sem=recv_at,
            device_id=peer, device_id_type=MESH,
        )

    def send(*arguments):
        copy = remote(*arguments)
        copy.start()
        return copy

    halo = remote(
        cot_ref.at[pl.ds(0, 2)], next_ref, move_send.at[frames], move_recv.at[frames], before
    )
    tails = remote(
        tail_out, tail_ref, move_send.at[frames + 1], move_recv.at[frames + 1], after
    )

    def moved(f):
        return remote(
            igrad_ref.at[f], arrived_ref.at[f], move_send.at[f], move_recv.at[f], before
        )

    @pl.when(tm == slabs - 1)
    def _():
        next_ref[...] = jnp.zeros_like(next_ref)
        arrived_ref[...] = jnp.zeros_like(arrived_ref)

    @pl.when(tm == 0)
    def _():
        tail_ref[...] = jnp.zeros_like(tail_ref)

    own_start, own_length = start_of(len_ref, slabs, tm), length_of(len_ref, slabs, tm)
    frame_total = start_of(len_ref, slabs, slabs)
    area = res_ref[0, 0] * res_ref[0, 1] * width
    count = (frame_total * area).astype(F32)
    mask_ref[...] = cells(res_ref, cols, (places, channels)).astype(F32)
    first, last = col_masks(cols, (places, channels))
    first_ref[...] = first
    last_ref[...] = last
    zero = jnp.zeros((8, channels), F32)
    row = lax.broadcasted_iota(jnp.int32, (8, channels), 0)


    def fold(value):
        return jnp.sum(value.reshape(places // 8, 8, channels), axis=0)

    def over_groups(total):
        line = jnp.sum(total, axis=0, keepdims=True)
        return group_sum(jnp.broadcast_to(line, (8, channels)), width)

    def add_up(f, total):
        held = (f < own_length).astype(F32)
        return total + fold(loaded_ref[f].astype(F32) * (mask_ref[...] * held))

    own_mean = over_groups(lax.fori_loop(0, frames, add_up, zero)) / (own_length * area).astype(F32)
    mean_row = own_mean[0:1]

    def spread(f, total):
        held = (f < own_length).astype(F32)
        apart = (loaded_ref[f].astype(F32) - mean_row) * (mask_ref[...] * held)
        return total + fold(apart * apart)

    squares = over_groups(lax.fori_loop(0, frames, spread, zero))
    stats_out[...] = jnp.where(row == 0, own_mean, squares)
    stats_ref[tm] = stats_out[...]
    for k in range(2):
        offset = tm * frames + frames - 2 + k - own_start
        usable = (offset >= 0) & (offset < own_length)
        picked = loaded_ref[jnp.clip(offset, 0, frames - 1)]
        tail_out[k] = jnp.where(usable, picked, jnp.zeros_like(picked))


    def pack(f, _):
        offset = (tm - 1) * frames + f - own_start
        usable = (offset >= 0) & (offset < own_length)
        picked = loaded_ref[jnp.clip(offset, 0, frames - 1)]
        igrad_ref[f] = jnp.where(usable, picked, jnp.zeros_like(picked))
        return 0

    lax.fori_loop(0, frames, pack, 0)

    pl.semaphore_wait(barrier, len(greeted))
    stats_shares = [
        send(stats_out, stats_ref.at[tm], stat_send.at[i], stat_recv.at[i], peer)
        for i, peer in enumerate(tm_peers)
    ]

    @pl.when(has_after)
    def _():
        tails.start()

    @pl.when(has_before)
    def _():
        moved(0).start()
        moved(1).start()

    load.wait()

    def turn(block, _):
        for k in range(3):
            turned_ref[block, k * channels : (k + 1) * channels, :] = weight_ref[
                block, (2 - k) * channels : (3 - k) * channels, :
            ].T
        return 0

    lax.fori_loop(0, 9, turn, 0)
    blank = jnp.zeros((cols, 3 * channels), BF16)

    def place(frame, value):
        alive = (tm * frames + frame < frame_total).astype(F32)
        value = value.astype(F32) * (mask_ref[...] * alive)
        back_cat[frame, 0] = blank
        back_cat[frame, rows + 1] = blank
        lay_out(back_cat, frame, value, rows, cols, first_ref[...], last_ref[...])
        return value


    def own_grad(f, _):
        value = place(f, cot_ref[f])
        grad_ref[pl.ds(pl.multiple_of(f * places, places), places)] = value.astype(BF16)
        return 0

    lax.fori_loop(0, frames, own_grad, 0)

    def convolve(source, factor, f, back):
        total = jnp.zeros((places, channels), F32)
        for d in range(3):
            for r in range(3):
                at = (f + 2 - d, 2 - r) if back else (f + d, r)
                lines = source[at[0], at[1] : at[1] + rows].reshape(places, 3 * channels)
                total = total + jnp.dot(lines, factor[3 * d + r], preferred_element_type=F32)
        return total * (mask_ref[...] * (tm * frames + f < frame_total).astype(F32))

    def back_sweep(f, _):
        agrad_ref[f] = convolve(back_cat, turned_ref, f, True)
        return 0

    for copy in stats_shares:
        copy.wait()

    @pl.when(has_before)
    def _():
        for f in range(2, frames):
            moved(f).start()
        halo.start()

    lax.fori_loop(0, frames - 2, back_sweep, 0)

    counts = [(len_ref[0, i] * area).astype(F32) for i in range(slabs)]
    mean = jnp.zeros((1, channels), F32)
    for i in range(slabs):
        mean = mean + counts[i] * stats_ref[i, 0:1]
    mean = mean / count
    squares = jnp.zeros((1, channels), F32)
    for i in range(slabs):
        apart = stats_ref[i, 0:1] - mean
        squares = squares + stats_ref[i, 1:2] + counts[i] * (apart * apart)
    root = lax.rsqrt(squares / count + EPSILON)
    gain, bias = gain_ref[...], bias_ref[...]

    def activate(slot, frame_id, value):
        alive = ((frame_id >= 0) & (frame_id < frame_total)).astype(F32)
        live = mask_ref[...] * alive
        normed = (value.astype(F32) * live - mean) * live * root
        pre = normed * gain + bias
        gate = 1.0 / (1.0 + jnp.exp(-pre))
        act = (pre * gate * live).astype(BF16).astype(F32)
        cat_ref[slot, 0] = blank
        cat_ref[slot, rows + 1] = blank
        lay_out(cat_ref, slot, act, rows, cols, first_ref[...], last_ref[...])
        return normed

    @pl.when(has_before)
    def _():
        tails.wait_recv()

    for k in range(2):
        frame_id = tm * frames + k - 2
        offset = frame_id - own_start
        usable = (offset >= 0) & (offset < own_length)
        picked = jnp.where(usable, loaded_ref[jnp.clip(offset, 0, frames - 1)], tail_ref[k])
        activate(k, frame_id, picked)

    def own_frame(f, _):
        @pl.when(has_after)
        def _():
            moved(f).wait_recv()

        frame_id = tm * frames + f
        offset = frame_id - own_start
        picked = jnp.where(
            offset < own_length,
            loaded_ref[jnp.clip(offset, 0, frames - 1)],
            arrived_ref[f],
        )
        normed_ref[f] = activate(f + 2, frame_id, picked)
        return 0

    def through(f, sums):
        normed = normed_ref[f]
        pre = normed * gain + bias
        gate = 1.0 / (1.0 + jnp.exp(-pre))
        pre_grad = agrad_ref[f] * gate * (1.0 + pre * (1.0 - gate))
        agrad_ref[f] = pre_grad * gain
        return sums[0] + fold(pre_grad * normed), sums[1] + fold(pre_grad)

    order = [(k % 3, (k + 1) % 3, (k + 2) % 3) for k in range(3)]
    own_lanes = pl.ds(pl.multiple_of(core * lanes, lanes), lanes)

    def spread_out(stage, k, axis, source, target):
        row_of = []
        for off in (1, 2, 3):
            there, peer = along(axis, off)
            row_of.append(
                send(
                    source(there), target(off - 1),
                    send_sem.at[stage, k, off - 1], recv_sem.at[stage, k, off - 1], peer,
                )
            )
        return row_of

    def product(k, r, begin, end):
        lines = cat_ref[k + begin : k + end, r : r + rows].reshape(-1, 3 * channels)
        both = lax.dot_general(
            lines,
            grad_ref[begin * places : end * places],
            (((0,), (0,)), ((), ())),
            preferred_element_type=F32,
        ).reshape(per_row, 16, channels)
        low, high = both[..., :lanes], both[..., lanes:]
        return jnp.where(core == 0, low, high), jnp.where(core == 0, high, low)

    def early_part(k):
        for r in range(3):
            at = slice(r * per_row, (r + 1) * per_row)
            own_part[k, at], far_sum[k, at] = product(k, r, 0, early)

    def kernel_part(k):
        for r in range(3):
            at = slice(r * per_row, (r + 1) * per_row)
            own, far = product(k, r, early, frames)
            own_part[k, at] = own_part[k, at] + own
            far_part[k, at] = (far_sum[k, at] + far).astype(BF16)
        return send(
            far_part.at[k], core_in.at[k], send_sem.at[0, k, 0], recv_sem.at[0, k, 0], other
        )

    def first_stage(k, half):
        half.wait()

        def add_half(b, _):
            at = pl.ds(b * 4, 4)
            both = own_part[k, at] + core_in[k, at].astype(F32)
            own_part[k, at] = both
            send1[k, at] = both.astype(BF16)
            return 0

        lax.fori_loop(0, blocks // 4, add_half, 0)
        return spread_out(
            1, k, order[k][0],
            lambda there: send1.at[k, pl.ds(there * part, part)],
            lambda i: in1.at[k, i],
        )

    def second_stage(k, copies):
        for copy in copies:
            copy.wait()
        base = here[order[k][0]] * part

        def add_first(b, _):
            at = pl.ds(b * 3, 3)
            own = own_part[k, pl.ds(base + b * 3, 3)]
            for i in range(3):
                own = own + in1[k, i, at].astype(F32)
            send2[k, at] = own.astype(BF16)
            return 0

        lax.fori_loop(0, part // 3, add_first, 0)
        return spread_out(
            2, k, order[k][1],
            lambda there: send2.at[k, pl.ds(there * piece, piece)],
            lambda i: in2.at[k, i],
        )

    def third_stage(k, copies):
        for copy in copies:
            copy.wait()
        base = here[order[k][1]] * piece
        spot = here[order[k][2]]

        def add_second(b, _):
            at = pl.ds(b * 3, 3)
            own = send2[k, pl.ds(base + b * 3, 3)].astype(F32)
            for i in range(3):
                own = own + in2[k, i, at].astype(F32)
            in3[k, spot, at] = own.astype(BF16)
            return 0

        lax.fori_loop(0, piece // 3, add_second, 0)
        return spread_out(
            3, k, order[k][2], lambda there: in3.at[k, spot], lambda i: in3.at[k, spot]
        )

    def fourth_stage(k, copies):
        for copy in copies:
            copy.wait()
        base = here[order[k][0]] * part + here[order[k][1]] * piece

        def add_third(b, _):
            at = pl.ds(b * 3, 3)
            own = in3[k, 0, at].astype(F32)
            for i in range(1, 4):
                own = own + in3[k, i, at].astype(F32)
            total_ref[k, pl.ds(base + b * 3, 3), :, own_lanes] = own.astype(BF16)
            return 0

        lax.fori_loop(0, piece // 3, add_third, 0)
        row_of = spread_out(
            4, k, order[k][1],
            lambda there: fragment(k, here[order[k][1]]),
            lambda i: fragment(k, here[order[k][1]]),
        )
        return row_of, [hand_on(k, 0)]

    def fragment(k, there):
        base = here[order[k][0]] * part + there * piece
        return total_ref.at[k, pl.ds(base, piece), :, own_lanes]

    def hand_on(k, back):
        spot = fragment(k, (here[order[k][1]] + 4 - back) % 4)
        row_of = []
        for off in (1, 2, 3):
            at = 3 * back + off - 1
            row_of.append(
                send(
                    spot, spot, send_sem.at[5, k, at], recv_sem.at[5, k, at],
                    along(order[k][0], off)[1],
                )
            )
        return row_of

    def region(k, there):
        return total_ref.at[k, pl.ds(there * part, part), :, own_lanes]

    def to_core(k, there, i):
        spot = region(k, there)
        return send(spot, spot, send_sem.at[6, k, i], recv_sem.at[6, k, i], other)

    def fifth_stage(k, copies):
        arriving, pieces = copies
        for back in (1, 3, 2):
            arriving[back - 1].wait()
            pieces.append(hand_on(k, back))
        return pieces, [to_core(k, here[order[k][0]], 0)]

    def sixth_stage(k, off, copies):
        for row_of in copies[0]:
            row_of[off - 1].wait()
        copies[1].append(to_core(k, (here[order[k][0]] + 4 - off) % 4, off))

    def forward_sweep(f, _):
        encoded_ref[f] = convolve(cat_ref, weight_ref, f, False).astype(BF16)
        return 0

    def take_in(f, _):
        own_frame(f, 0)
        forward_sweep(f, 0)
        return 0

    lax.fori_loop(0, early - 1, take_in, 0)
    lax.fori_loop(early - 1, early, own_frame, 0)
    for k in range(3):
        early_part(k)
    lax.fori_loop(early, frames, own_frame, 0)

    half0 = kernel_part(0)
    half1 = kernel_part(1)
    stage0 = first_stage(0, half0)
    half2 = kernel_part(2)
    stage1 = first_stage(1, half1)
    stage2 = first_stage(2, half2)
    lax.fori_loop(early - 1, frames, forward_sweep, 0)

    @pl.when(has_after)
    def _():
        halo.wait_recv()

    for k in range(2):
        place(frames + k, next_ref[k])
    lax.fori_loop(frames - 2, frames, back_sweep, 0)
    gain_sum, bias_sum = lax.fori_loop(0, frames, through, (zero, zero))
    sums_ref[...] = jnp.where(
        row == 0,
        jnp.sum(gain_sum, axis=0, keepdims=True),
        jnp.where(row == 1, jnp.sum(bias_sum, axis=0, keepdims=True), 0.0),
    )
    slabs_ref[tm] = sums_ref[...]
    shares = [
        send(sums_ref, slabs_ref.at[tm], pair_send.at[i], pair_recv.at[i], peer)
        for i, peer in enumerate(tm_peers)
    ]

    stage0 = second_stage(0, stage0)
    stage1 = second_stage(1, stage1)
    for copy in shares:
        copy.wait()
    total = slabs_ref[0]
    for i in range(1, slabs):
        total = total + slabs_ref[i]
    tm_total[...] = total
    core_copy = send(tm_total, core_sum, pair_send.at[7], pair_recv.at[7], other)
    stage0 = third_stage(0, stage0)
    stage2 = second_stage(2, stage2)
    stage1 = third_stage(1, stage1)

    core_copy.wait()
    x_sums[x] = tm_total[...] + core_sum[...]
    x_copies = [
        send(x_sums.at[x], x_sums.at[x], pair_send.at[7 + off], pair_recv.at[7 + off], along(0, off)[1])
        for off in (1, 2, 3)
    ]
    shares_of = group_sum(tm_total[...] * gain, width) / count
    mean_part, along_part = shares_of[1:2], shares_of[0:1]

    @pl.when(has_before)
    def _():
        for f in range(frames):
            moved(f).wait_send()

    def finish(f, _):
        live = mask_ref[...] * (tm * frames + f < frame_total).astype(F32)
        inner = agrad_ref[f] - mean_part - normed_ref[f] * along_part
        igrad_ref[f] = (inner * root * live).astype(BF16)
        return 0

    lax.fori_loop(0, frames // 2, finish, 0)
    stage0 = fourth_stage(0, stage0)
    stage2 = third_stage(2, stage2)
    lax.fori_loop(frames // 2, frames, finish, 0)

    stage1 = fourth_stage(1, stage1)
    for copy in x_copies:
        copy.wait()
    x_total[...] = x_sums[0] + x_sums[1] + x_sums[2] + x_sums[3]
    z_copy = send(x_total, z_sum, pair_send.at[11], pair_recv.at[11], across)
    stage0 = fifth_stage(0, stage0)
    stage2 = fourth_stage(2, stage2)
    stage1 = fifth_stage(1, stage1)
    z_copy.wait()
    pair_ref[...] = x_total[...] + z_sum[...]
    stage2 = fifth_stage(2, stage2)
    ends = (stage0, stage1, stage2)
    for off in (1, 3, 2):
        for k in range(3):
            sixth_stage(k, off, ends[k])
    for k in range(3):
        for copy in ends[k][1]:
            copy.wait()

    @pl.when(has_before)
    def _():
        halo.wait_send()

    @pl.when(has_after)
    def _():
        tails.wait_send()


def pinned(value):
    return pltpu.with_memory_space_constraint(value, pltpu.HBM)


def body(loaded, lengths, resolution, weight, norm_gain, norm_bias, cotangent):
    frames, rows, cols, channels = loaded.shape[1:]
    places, width, lanes = rows * cols, channels // GROUPS, channels // 2
    slabs = lax.axis_size("tm")
    shape = jax.ShapeDtypeStruct
    slab = (frames, places, channels)
    blocks = 9 * channels // 16
    part, piece = blocks // 4, blocks // 16

    def tiles(*lead, kind=BF16):
        return pltpu.VMEM(lead + (16, lanes), kind)

    small = pltpu.VMEM((8, channels), F32)
    plane = pltpu.VMEM((places, channels), F32)
    cat = pltpu.VMEM((frames + 2, rows + 2, cols, 3 * channels), BF16)
    dma = pltpu.SemaphoreType.DMA
    encoded, igrad, total, pair = pl.pallas_call(
        functools.partial(section_kernel, rows, cols, width),
        out_shape=(
            shape(slab, BF16),
            shape(slab, BF16),
            shape((3, blocks, 16, channels), BF16),
            shape((8, channels), F32),
        ),
        in_specs=[SMEM, SMEM, VMEM, VMEM, HBM, VMEM, VMEM],
        out_specs=(VMEM,) * 4,
        scratch_shapes=[
            pltpu.VMEM(slab, BF16),
            pltpu.VMEM((2, places, channels), BF16),
            pltpu.VMEM((2, places, channels), BF16),
            pltpu.VMEM((2, places, channels), BF16),
            pltpu.VMEM((9, 3 * channels, channels), BF16),
            pltpu.VMEM((9, 3 * channels, channels), BF16),
            cat,
            cat,
            pltpu.VMEM((frames * places, channels), BF16),
            pltpu.VMEM(slab, F32),
            pltpu.VMEM(slab, F32),
            plane,
            plane,
            plane,
            small,
            pltpu.VMEM((slabs, 8, channels), F32),
            small,
            pltpu.VMEM((slabs, 8, channels), F32),
            tiles(3, blocks, kind=F32),
            tiles(3, blocks, kind=F32),
            tiles(3, blocks),
            tiles(3, blocks),
            tiles(3, blocks),
            tiles(3, 3, part),
            tiles(3, part),
            tiles(3, 3, piece),
            tiles(3, 4, piece),
            small,
            small,
            pltpu.VMEM((4, 8, channels), F32),
            small,
            small,
            dma,
            dma((frames + 2,)),
            dma((frames + 2,)),
            dma((7,)),
            dma((7,)),
            dma((7, 3, 12)),
            dma((7, 3, 12)),
            dma((12,)),
            dma((12,)),
        ],
        compiler_params=params(LIMIT, collective_id=1, has_side_effects=True),
    )(
        *map(
            pinned,
            (
                lengths,
                resolution,
                loaded.reshape(slab),
                cotangent.reshape(slab),
                weight.reshape(9, 3 * channels, channels),
                norm_gain.reshape(1, channels),
                norm_bias.reshape(1, channels),
            ),
        )
    )
    scale = 1.0 / math.sqrt(lax.axis_size("dp") * slabs * frames * places)
    whole = (1, frames, rows, cols, channels)
    return (
        encoded.reshape(whole),
        igrad.reshape(whole),
        total.reshape(27, channels, channels).astype(F32) * scale,
        pair[0] * scale,
        pair[1] * scale,
    )


def solution(mesh):
    slab = P("dp", "tm", None, None, None)
    return jax.shard_map(
        body,
        mesh=mesh,
        in_specs=(slab, P("dp", None), P("dp", None), P(), P(), P(), slab),
        out_specs=(slab, slab, P(), P(), P()),
        check_vma=False,
    )
```
